32 devices in a mesh: section: 4 (over y, x), vertex: 4 (over z), feat: 2 (over core).
Axes of the slice: x: 2, y: 2, z: 4, core: 2. Of those that a mesh axis runs over, the one named last changes fastest.
Arguments:
- features: bfloat16 [8192, 1024], P('vertex', 'feat'), may hold values from -6 to 6
- history: bfloat16 [4, 8192, 1024], P('section', 'vertex', 'feat'), may hold values from -6 to 6
- weights: bfloat16 [4, 1024, 1024], P('section', None, 'feat'), may hold values from -0.1875 to 0.1875
- tile_values: bfloat16 [3, 64, 128, 128], P(None, 'vertex'), may hold values from -0.25 to 0.25
- tile_rows: int32 [3, 64], P(None, 'vertex'), may hold values from 0 to 3, as said below
- tile_cols: int32 [3, 64], P(None, 'vertex'), may hold values from 0 to 15
- tile_counts: int32 [3, 4], P(None, 'vertex'), may hold values from 1 to 16, as said below
- span_ids: int32 [3, 512], P(None, 'vertex'), may hold values from 0 to 2047, as said below
Outputs:
- layer_out: bfloat16 [4, 3, 512, 1024], P('section', None, 'vertex', 'feat')
- new_history: bfloat16 [4, 8192, 1024], P('section', 'vertex', 'feat')
The draws below stay inside these ranges and needn't reach their ends.
Inputs may be any that keep to these rules, and one draw needn't show every extreme that they name: `tile_rows`: within one owner's list for one block the (row block, column block) pairs are distinct. `tile_counts`: in every block some owner has exactly 16 live tiles. `span_ids`: the 384 entries of one owner over all blocks are distinct.
All inputs are finite; a program needn't handle non-finite values.
Results may differ from the reference program's by a relative error of at most 0.018.
Values may be sent and summed in bfloat16 or wider, within the bound.
A program may use at most 128 MiB of HBM per device.

```python
import math
import jax
import jax.numpy as jnp
from jax import lax

F = 1024
BLOCK = 128
SPANS = 3
ROWS_DEV = 128
VD = 2048
LAYERS = 4
V = 8192
TILES = 16
N_SECTION = 4
N_VERTEX = 4


def tile_pairs(key):
    row_blocks = ROWS_DEV * N_VERTEX // BLOCK
    col_blocks = VD // BLOCK
    keys = jax.random.split(jax.random.fold_in(key, 11), SPANS * N_VERTEX)
    picks = jax.vmap(lambda single: jax.random.permutation(single, row_blocks * col_blocks)[:TILES])(keys)
    return (picks.reshape(SPANS, N_VERTEX * TILES).astype(jnp.int32), col_blocks)


def draw_tile_rows(key, part):
    picks, col_blocks = tile_pairs(key)
    return (picks // col_blocks).astype(jnp.int32)


def draw_tile_cols(key, part):
    picks, col_blocks = tile_pairs(key)
    return (picks % col_blocks).astype(jnp.int32)


def draw_tile_counts(key, part):
    lowest = max(1, TILES // 8)
    base = jax.random.randint(jax.random.fold_in(key, 5), (SPANS, N_VERTEX), lowest, TILES // 2 + 1)
    busiest = jax.random.randint(jax.random.fold_in(key, 6), (SPANS, 1), 0, N_VERTEX)
    owner_index = jnp.arange(N_VERTEX)[None, :]
    return jnp.where(owner_index == busiest, TILES, base).astype(jnp.int32)


def draw_span_ids(key, part):
    keys = jax.random.split(jax.random.fold_in(key, 17), N_VERTEX)
    picks = jax.vmap(lambda single: jax.random.permutation(single, VD)[:SPANS * ROWS_DEV])(keys)
    picks = picks.reshape(N_VERTEX, SPANS, ROWS_DEV).transpose(1, 0, 2)
    return picks.reshape(SPANS, N_VERTEX * ROWS_DEV).astype(jnp.int32)


def levels(key, shape, shards, least, top_value):
    factor_of, own = 1.0, jax.random.fold_in(key, 6)
    for position, blocks in shards:
        draws = jnp.exp(jax.random.uniform(jax.random.fold_in(own, position), (blocks,), jnp.float32, least / len(shards), top_value / len(shards)))
        factor_of = factor_of * jnp.repeat(draws, shape[position] // blocks).reshape([-1 if axis == position else 1 for axis in range(len(shape))])
    return factor_of


def bell_draw(rng, shape, width, limit, cuts=(), dtype=jnp.bfloat16):
    values = width * jax.random.normal(rng, shape, jnp.float32)
    if cuts:
        values = values * levels(rng, shape, cuts, -0.22, 0.18)
    return jnp.clip(values, -limit, limit).astype(dtype)


def setup_inputs(seed: int = 0) -> dict:
    splits = jax.random.split(jax.random.key(seed), 9)
    features = bell_draw(splits[0], (V, F), 1.0, 6.0, ((0, 4), (1, 2)))
    history = bell_draw(splits[1], (LAYERS, V, F), 1.0, 6.0, ((0, 4), (1, 4), (2, 2)))
    weights = bell_draw(splits[2], (LAYERS, F, F), F ** -0.5, 0.1875, ((0, 4), (2, 2)))
    tile_values = bell_draw(splits[3], (SPANS, N_VERTEX * TILES, BLOCK, BLOCK), (N_VERTEX * VD // 16) ** -0.5, 0.25, ((1, 4),))
    tile_rows = draw_tile_rows(jax.random.fold_in(splits[8], 71), 0)
    tile_cols = draw_tile_cols(jax.random.fold_in(splits[8], 71), 0)
    tile_counts = draw_tile_counts(jax.random.fold_in(splits[8], 71), 0)
    span_ids = draw_span_ids(jax.random.fold_in(splits[8], 71), 0)
    return {"features": features, "history": history, "weights": weights, "tile_values": tile_values, "tile_rows": tile_rows, "tile_cols": tile_cols, "tile_counts": tile_counts, "span_ids": span_ids}


RESIDUAL_SHARE = 0.2
BETA_SCALE = 0.5


def reference(features, history, weights, tile_values, tile_rows, tile_cols, tile_counts, span_ids):
    row_blocks = ROWS_DEV * N_VERTEX // BLOCK
    col_blocks = VD // BLOCK
    owners = (jnp.arange(ROWS_DEV * N_VERTEX) // ROWS_DEV).astype(jnp.int32) * VD
    outputs = []
    tables = []
    previous = None
    for layer in range(N_SECTION):
        table = history[layer]
        beta_rate = math.log(BETA_SCALE / (layer + 1) + 1.0)
        results = []
        for span_index in range(SPANS):
            vertex_ids = span_ids[span_index].astype(jnp.int32) + owners
            initial = features[vertex_ids]
            fresh_rows = initial if layer == 0 else previous[span_index]
            table = table.at[vertex_ids].set(fresh_rows)
            blocks = table.reshape(N_VERTEX * col_blocks, BLOCK, F)
            values_here = tile_values[span_index]
            rows_here = tile_rows[span_index]
            cols_here = tile_cols[span_index]
            counts_here = tile_counts[span_index]

            def device_term(device, running):
                first = (device * TILES).astype(jnp.int32)
                tile_block = lax.dynamic_slice_in_dim(values_here, first, TILES, 0).astype(jnp.float32)
                row_ids = lax.dynamic_slice_in_dim(rows_here, first, TILES, 0)
                col_ids = lax.dynamic_slice_in_dim(cols_here, first, TILES, 0) + (device * col_blocks).astype(jnp.int32)
                alive = (jnp.arange(TILES) < counts_here[device]).astype(jnp.float32)
                picked = blocks[col_ids].astype(jnp.float32)
                products = jnp.einsum("tij,tjc->tic", tile_block, picked, precision=lax.Precision.HIGHEST)
                products = products * alive[:, None, None]
                summed = jax.ops.segment_sum(products, row_ids, num_segments=row_blocks)
                rounded = lax.optimization_barrier(summed.astype(jnp.bfloat16))
                return running + rounded.astype(jnp.float32)

            aggregate = lax.fori_loop(0, N_VERTEX, device_term, jnp.zeros((row_blocks, BLOCK, F), jnp.float32))
            aggregate = aggregate.reshape(ROWS_DEV * N_VERTEX, F)
            support = ((1.0 - RESIDUAL_SHARE) * aggregate + RESIDUAL_SHARE * initial.astype(jnp.float32)).astype(jnp.bfloat16)
            projected = jnp.dot(support, weights[layer], preferred_element_type=jnp.float32)
            layer_rows = jax.nn.relu((1.0 - beta_rate) * support.astype(jnp.float32) + beta_rate * projected).astype(jnp.bfloat16)
            results.append(layer_rows)
        previous = results
        outputs.append(jnp.stack(results))
        tables.append(table)
    return jnp.stack(outputs), jnp.stack(tables)
```

```python
import functools

import jax
import jax.numpy as jnp
from jax import lax
from jax.experimental import pallas as pl
from jax.experimental.pallas import tpu as pltpu
from jax.sharding import PartitionSpec as P

RESIDUAL_SHARE = 0.2
BETA_SCALE = 0.5
MESH = pl.DeviceIdType.MESH
VMEM_BYTES = 60_000 * 1024


def chosen(ids_row, rows, first=0):
    shape = (rows, ids_row.shape[1])
    return (lax.broadcasted_iota(jnp.int32, shape, 0) + first == ids_row).astype(jnp.float32)


def prepare(rows_ref, cols_ref, counts_ref, tiles_ref, dense_hbm, dense, dense_sem):
    spans, _, side, _ = tiles_ref.shape
    copies = []
    for span in range(spans):
        dense[span] = jnp.zeros(dense.shape[1:], dense.dtype)

        def place(t, _, span=span):
            row = pl.multiple_of(rows_ref[span, t] * side, side)
            col = pl.multiple_of(cols_ref[span, t] * side, side)
            dense[span, pl.ds(row, side), pl.ds(col, side)] = tiles_ref[span, t]
            return 0

        lax.fori_loop(0, counts_ref[0, span], place, 0)
        copies.append(pltpu.make_async_copy(dense.at[span], dense_hbm.at[span], dense_sem.at[span]))
        copies[-1].start()
    for copy in copies:
        copy.wait()


def relay(
    sections, vertices, feats,
    dense_hbm, ids_ref, weight_hbm, kept_hbm, features_hbm, out_ref, table_hbm,
    dense, base_ref, picks_ref, weight_ref, kept_ref, features_ref, select_ref, initial_ref, fresh_ref,
    arrived, partial, parts, passing, support, other, result,
    load_sem, table_sem, x_send, x_recv, p_send, p_recv, h_send, h_recv, s_send, s_recv,
):
    section = lax.axis_index("section")
    vertex = lax.axis_index("vertex")
    feat = lax.axis_index("feat")
    spans, span_rows, width = arrived.shape
    last = vertices - 1
    partner = lax.rem(feat + 1, feats)
    beta = jnp.log(BETA_SCALE / (section + 1).astype(jnp.float32) + 1.0)
    halves = 2
    piece = span_rows // halves
    relayed = vertices > 3

    rows_whole = dense.shape[1]
    owned = kept_ref.shape[0]
    group = min(512, rows_whole)
    chunk = min(256, owned)

    def load_dense(span):
        return pltpu.make_async_copy(dense_hbm.at[span], dense.at[span % 2], load_sem.at[span])

    load_weight = pltpu.make_async_copy(weight_hbm, weight_ref, load_sem.at[spans])
    load_kept = pltpu.make_async_copy(kept_hbm, kept_ref, load_sem.at[spans + 1])
    load_features = pltpu.make_async_copy(features_hbm, features_ref, load_sem.at[spans + 2])
    load_kept.start()
    load_features.start()
    for span in range(min(2, spans)):
        load_dense(span).start()
    load_weight.start()

    barrier = pltpu.get_barrier_semaphore()
    for step in range(1, vertices):
        peer = lax.rem(vertex + step, vertices)
        pl.semaphore_signal(barrier, inc=1, device_id=(section, peer, feat), device_id_type=MESH)
    pl.semaphore_signal(barrier, inc=1, device_id=(section, vertex, partner), device_id_type=MESH)
    for step in (1, sections - 1):
        peer = lax.rem(section + step, sections)
        pl.semaphore_signal(barrier, inc=1, device_id=(peer, vertex, feat), device_id_type=MESH)
    if relayed:
        @pl.when(vertex == 0)
        def _():
            parts[:, 0] = jnp.zeros((spans, span_rows, width), jnp.bfloat16)

        @pl.when(vertex == last)
        def _():
            parts[:, last - 1] = jnp.zeros((spans, span_rows, width), jnp.bfloat16)

    pl.semaphore_wait(barrier, vertices - 1 + 1 + 2)

    def half_of(half):
        return slice(half * piece, (half + 1) * piece)

    def row_copy(span, half):
        rows = pl.ds(half * piece, piece)
        return pltpu.make_async_remote_copy(
            src_ref=result.at[span, rows], dst_ref=arrived.at[span, rows],
            send_sem=x_send.at[span, half], recv_sem=x_recv.at[span, half],
            device_id=(lax.rem(section + 1, sections), vertex, feat), device_id_type=MESH,
        )

    def chunk_rows(peer, half):
        return pl.ds(pl.multiple_of(peer * span_rows + half * piece, piece), piece)

    def part_copy(span, step, half):
        peer = lax.rem(vertex + step, vertices)
        return pltpu.make_async_remote_copy(
            src_ref=partial.at[span, chunk_rows(peer, half)],
            dst_ref=parts.at[span, step - 1, pl.ds(half * piece, piece)],
            send_sem=p_send.at[span, step - 1, half], recv_sem=p_recv.at[span, step - 1, half],
            device_id=(section, peer, feat), device_id_type=MESH,
        )

    def pass_copy(span, half):
        far = jnp.where(vertex == 0, last, 0)
        near = jnp.where(vertex == 0, 1, last - 1)
        return pltpu.make_async_remote_copy(
            src_ref=partial.at[span, chunk_rows(far, half)],
            dst_ref=passing.at[span, pl.ds(half * piece, piece)],
            send_sem=h_send.at[span, half], recv_sem=h_recv.at[span, half],
            device_id=(section, near, feat), device_id_type=MESH,
        )

    def support_copy(span, half):
        rows = pl.ds(half * piece, piece)
        return pltpu.make_async_remote_copy(
            src_ref=support.at[span, rows], dst_ref=other.at[span, rows],
            send_sem=s_send.at[span, half], recv_sem=s_recv.at[span, half],
            device_id=(section, vertex, partner), device_id_type=MESH,
        )

    at_end = (vertex == 0) | (vertex == last)

    def is_direct(step):
        if not relayed:
            return vertex >= 0
        peer = lax.rem(vertex + step, vertices)
        ends = ((vertex == 0) & (peer == last)) | ((vertex == last) & (peer == 0))
        inner = ((vertex == 1) & (peer == last)) | ((vertex == last - 1) & (peer == 0))
        return jnp.logical_not(ends | inner)

    def is_sent(step):
        if not relayed:
            return vertex >= 0
        peer = lax.rem(vertex + step, vertices)
        return jnp.logical_not(((vertex == 0) & (peer == last)) | ((vertex == last) & (peer == 0)))

    def is_received(step):
        if not relayed:
            return vertex >= 0
        source = lax.rem(vertex + vertices - step, vertices)
        return jnp.logical_not(((vertex == 0) & (source == last)) | ((vertex == last) & (source == 0)))

    def local(span, leading):
        mine = slice(span * span_rows, (span + 1) * span_rows)
        used = (span + 1) * span_rows

        def clear(i, _):
            first = pl.multiple_of(i * chunk, chunk)
            here = pl.ds(first, chunk)
            hot = chosen(ids_ref[span : span + 1, :], chunk, first)
            select_ref[here, mine] = hot.astype(jnp.bfloat16)
            taken = jnp.max(hot, axis=1, keepdims=True) > 0.5
            filler = features_ref[here, :].astype(jnp.float32) if leading else 0.0
            kept_ref[here, :] = jnp.where(taken, filler, kept_ref[here, :].astype(jnp.float32)).astype(jnp.bfloat16)
            return 0

        lax.fori_loop(0, owned // chunk, clear, 0)
        load_dense(span).wait()

        def multiply(i, _):
            here = pl.ds(pl.multiple_of(i * group, group), group)
            block = dense[span % 2, here, :]
            product = jnp.dot(block, kept_ref[...], preferred_element_type=jnp.float32)
            if leading:
                partial[span, here, :] = product.astype(jnp.bfloat16)
            else:
                base_ref[span, here, :] = product
                picks_ref[span, here, :used] = jnp.dot(
                    block, select_ref[:, :used], preferred_element_type=jnp.float32
                ).astype(jnp.bfloat16)
            return 0

        lax.fori_loop(0, rows_whole // group, multiply, 0)
        if span + 2 < spans:
            load_dense(span + 2).start()

    def gather():
        initial_ref[...] = lax.dot_general(
            select_ref[...], features_ref[...], (((0,), (0,)), ((), ())), preferred_element_type=jnp.float32
        ).astype(jnp.bfloat16)

    def earlier(span):
        used = span * span_rows

        def add(i, _):
            here = pl.ds(pl.multiple_of(i * group, group), group)
            base_ref[span, here, :] += jnp.dot(
                picks_ref[span, here, :used], fresh_ref[:used, :], preferred_element_type=jnp.float32
            )
            return 0

        lax.fori_loop(0, rows_whole // group, add, 0)

    def scatter(span):
        mine = slice(span * span_rows, (span + 1) * span_rows)
        @pl.when(section > 0)
        def _():
            for half in range(halves):
                row_copy(span, half).wait_recv()
            fresh_ref[mine, :] = arrived[span]


        def compute(peer):
            here = pl.ds(pl.multiple_of(peer * span_rows, span_rows), span_rows)
            total = base_ref[span, here, :] + jnp.dot(
                picks_ref[span, here, mine], fresh_ref[mine, :], preferred_element_type=jnp.float32
            )
            partial[span, here, :] = total.astype(jnp.bfloat16)

        if relayed:
            @pl.when(at_end & (section > 0))
            def _():
                compute(jnp.where(vertex == 0, last, 0))

            @pl.when(at_end)
            def _():
                for half in range(halves):
                    pass_copy(span, half).start()

        for step in range(1, vertices):
            @pl.when(is_sent(step) & (section > 0))
            def _(step=step):
                compute(lax.rem(vertex + step, vertices))

            @pl.when(is_direct(step))
            def _(step=step):
                part_copy(span, step, 0).start()

        for half in range(1, halves):
            for step in range(1, vertices):
                @pl.when(is_direct(step))
                def _(step=step, half=half):
                    part_copy(span, step, half).start()

        @pl.when(section > 0)
        def _():
            compute(vertex)

    def pass_on(span):
        if relayed:
            for who, step in ((1, last - 1), (last - 1, 2)):
                @pl.when(vertex == who)
                def _(who=who, step=step):
                    far = last if who == 1 else 0
                    for half in range(halves):
                        pass_copy(span, half).wait_recv()
                        here = pl.ds(far * span_rows + half * piece, piece)
                        partial[span, here, :] = (
                            partial[span, here, :].astype(jnp.float32)
                            + passing[span, half_of(half), :].astype(jnp.float32)
                        ).astype(jnp.bfloat16)
                        part_copy(span, step, half).start()

    def finish(span, half):
        total = partial[span, chunk_rows(vertex, half), :].astype(jnp.float32)
        for step in range(1, vertices):
            @pl.when(is_received(step))
            def _(step=step):
                part_copy(span, step, half).wait_recv()

        for step in range(1, vertices):
            total += parts[span, step - 1, half_of(half), :].astype(jnp.float32)
        mixed = (
            (1.0 - RESIDUAL_SHARE) * total
            + RESIDUAL_SHARE * initial_ref[pl.ds(span * span_rows + half * piece, piece), :].astype(jnp.float32)
        ).astype(jnp.bfloat16)
        support[span, half_of(half), :] = mixed
        support_copy(span, half).start()
        mine = pl.ds(pl.multiple_of(feat * width, width), width)
        theirs = pl.ds(pl.multiple_of(partner * width, width), width)
        projected = jnp.dot(mixed, weight_ref[mine, :], preferred_element_type=jnp.float32)
        support_copy(span, half).wait_recv()
        projected += jnp.dot(other[span, half_of(half), :], weight_ref[theirs, :], preferred_element_type=jnp.float32)
        rows = jnp.maximum((1.0 - beta) * mixed.astype(jnp.float32) + beta * projected, 0.0).astype(jnp.bfloat16)
        result[span, half_of(half), :] = rows
        out_ref[span, half_of(half), :] = rows

        @pl.when(section < sections - 1)
        def _():
            row_copy(span, half).start()

    def finish_all(span):
        for half in range(halves):
            finish(span, half)

    load_kept.wait()
    load_features.wait()

    @pl.when(section == 0)
    def _():
        for span in range(spans):
            local(span, True)
            scatter(span)
            if span:
                pass_on(span - 1)
        gather()
        load_weight.wait()
        for span in range(spans - 1):
            finish_all(span)
            if span == 0:
                pass_on(spans - 1)

    @pl.when(section > 0)
    def _():
        for span in range(spans):
            local(span, False)
        gather()
        load_weight.wait()
        for span in range(spans):
            scatter(span)
            pass_on(span)
            if span:
                finish_all(span - 1)
            if span + 1 < spans:
                earlier(span + 1)

    def merge(i, _):
        here = pl.ds(pl.multiple_of(i * chunk, chunk), chunk)
        moved = jnp.dot(select_ref[here, :], fresh_ref[...], preferred_element_type=jnp.float32)
        kept_ref[here, :] = (kept_ref[here, :].astype(jnp.float32) + moved).astype(jnp.bfloat16)
        return 0

    @pl.when(section > 0)
    def _():
        lax.fori_loop(0, owned // chunk, merge, 0)

    store = pltpu.make_async_copy(kept_ref, table_hbm, table_sem)
    store.start()
    finish_all(spans - 1)

    for span in range(spans):
        for half in range(halves):
            support_copy(span, half).wait_send()
            for step in range(1, vertices):
                @pl.when(is_sent(step))
                def _(span=span, step=step, half=half):
                    part_copy(span, step, half).wait_send()

            if relayed:
                @pl.when(at_end)
                def _(span=span, half=half):
                    pass_copy(span, half).wait_send()

            @pl.when(section < sections - 1)
            def _(span=span, half=half):
                row_copy(span, half).wait_send()

    store.wait()

LINE = 4


def stream(
    sections, vertices, feats,
    rows_ref, cols_ref, counts_ref, ids_ref, tiles_hbm, weight_hbm, kept_hbm, features_hbm, out_ref, table_hbm,
    tiles, left, right, right_select, base_ref, picks_ref, weight_ref, kept_ref, features_ref, select_ref, initial_ref,
    fresh_ref, partial, parts, passing, support, other, result,
    load_sem, table_sem, x_send, x_recv, p_send, p_recv, h_send, h_recv, s_send, s_recv,
):
    section = lax.axis_index("section")
    vertex = lax.axis_index("vertex")
    feat = lax.axis_index("feat")
    spans, pieces, span_rows, part = result.shape
    slots, side = tiles.shape[1:3]
    row_blocks = left.shape[0] // side
    width = pieces * part
    rows_all = spans * span_rows
    last = vertices - 1
    partner = lax.rem(feat + 1, feats)
    beta = jnp.log(BETA_SCALE / (section + 1).astype(jnp.float32) + 1.0)
    col_blocks = kept_ref.shape[0]

    def load_tiles(span):
        return pltpu.make_async_copy(tiles_hbm.at[span], tiles.at[span], load_sem.at[span])

    load_weight = pltpu.make_async_copy(weight_hbm, weight_ref, load_sem.at[spans])
    load_kept = pltpu.make_async_copy(kept_hbm, kept_ref, load_sem.at[spans + 1])
    load_features = pltpu.make_async_copy(features_hbm, features_ref, load_sem.at[spans + 2])
    load_kept.start()
    load_features.start()
    for span in range(spans):
        load_tiles(span).start()
    load_weight.start()

    barrier = pltpu.get_barrier_semaphore()
    for step in range(1, vertices):
        peer = lax.rem(vertex + step, vertices)
        pl.semaphore_signal(barrier, inc=1, device_id=(section, peer, feat), device_id_type=MESH)
    pl.semaphore_signal(barrier, inc=1, device_id=(section, vertex, partner), device_id_type=MESH)
    for step in (1, sections - 1):
        peer = lax.rem(section + step, sections)
        pl.semaphore_signal(barrier, inc=1, device_id=(peer, vertex, feat), device_id_type=MESH)

    def meet():
        pl.semaphore_wait(barrier, vertices - 1 + 1 + 2)

    at_end = (vertex == 0) | (vertex == last)

    @pl.when(vertex == 0)
    def _():
        parts[:, 0] = jnp.zeros(parts.shape[:1] + parts.shape[2:], jnp.bfloat16)

    @pl.when(vertex == last)
    def _():
        parts[:, last - 1] = jnp.zeros(parts.shape[:1] + parts.shape[2:], jnp.bfloat16)

    def columns(j):
        return slice(j * part, (j + 1) * part)

    def span_of(span):
        return slice(span * span_rows, (span + 1) * span_rows)

    def row_copy(span, j):
        return pltpu.make_async_remote_copy(
            src_ref=result.at[span, j], dst_ref=fresh_ref.at[j, pl.ds(span * span_rows, span_rows)],
            send_sem=x_send.at[span, j], recv_sem=x_recv.at[span, j],
            device_id=(lax.rem(section + 1, sections), vertex, feat), device_id_type=MESH,
        )

    def rows_of(peer):
        return pl.ds(pl.multiple_of(peer * span_rows, span_rows), span_rows)

    def part_copy(span, step, j):
        peer = lax.rem(vertex + step, vertices)
        return pltpu.make_async_remote_copy(
            src_ref=partial.at[span, j, rows_of(peer)], dst_ref=parts.at[span, step - 1, j],
            send_sem=p_send.at[span, step - 1, j], recv_sem=p_recv.at[span, step - 1, j],
            device_id=(section, peer, feat), device_id_type=MESH,
        )

    def pass_copy(span, j):
        far = jnp.where(vertex == 0, last, 0)
        near = jnp.where(vertex == 0, 1, last - 1)
        return pltpu.make_async_remote_copy(
            src_ref=partial.at[span, j, rows_of(far)], dst_ref=passing.at[span, j],
            send_sem=h_send.at[span, j], recv_sem=h_recv.at[span, j],
            device_id=(section, near, feat), device_id_type=MESH,
        )

    def support_copy(span, j):
        return pltpu.make_async_remote_copy(
            src_ref=support.at[span, j], dst_ref=other.at[span, j],
            send_sem=s_send.at[span, j], recv_sem=s_recv.at[span, j],
            device_id=(section, vertex, partner), device_id_type=MESH,
        )

    def ends_meet(here, there):
        return ((here == 0) & (there == last)) | ((here == last) & (there == 0))

    def is_relayed(step):
        peer = lax.rem(vertex + step, vertices)
        return ((vertex == 1) & (peer == last)) | ((vertex == last - 1) & (peer == 0))

    def is_sent(step):
        return jnp.logical_not(ends_meet(vertex, lax.rem(vertex + step, vertices)))

    def is_received(step):
        return jnp.logical_not(ends_meet(lax.rem(vertex + vertices - step, vertices), vertex))

    def mark(span, leading):
        def clear(i, _):
            hot = chosen(ids_ref[span : span + 1, :], side, i * side)
            select_ref[i, :, span_of(span)] = hot.astype(jnp.bfloat16)
            taken = jnp.max(hot, axis=1, keepdims=True) > 0.5
            filler = features_ref[i].astype(jnp.float32) if leading else 0.0
            kept_ref[i] = jnp.where(taken, filler, kept_ref[i].astype(jnp.float32)).astype(jnp.bfloat16)
            return 0

        lax.fori_loop(0, col_blocks, clear, 0)

    def lay(span, leading):
        used = (span + 1) * span_rows
        load_tiles(span).wait()
        lives = jnp.full((side, side), counts_ref[0, span], jnp.int32)

        def place(t, _):
            col = cols_ref[span, t]
            here = pl.ds(pl.multiple_of(t * side, side), side)
            tile = tiles[span, t].astype(jnp.float32)
            rows = jnp.where(lives > t, jnp.full(tile.shape, rows_ref[span, t], jnp.int32), row_blocks)
            for block in range(row_blocks):
                left[block * side : (block + 1) * side, here] = jnp.where(rows == block, tile, 0.0).astype(left.dtype)
            right[here, :] = kept_ref[col]
            if not leading:
                right_select[here, :] = select_ref[col]
            return 0

        lax.fori_loop(0, slots, place, 0)

    def gather():
        initial_ref[...] = lax.dot_general(
            select_ref[...].reshape(col_blocks * side, rows_all),
            features_ref[...].reshape(col_blocks * side, width),
            (((0,), (0,)), ((), ())),
            preferred_element_type=jnp.float32,
        ).astype(jnp.bfloat16)

    def product(j):
        return jnp.dot(left[...], right[:, columns(j)], preferred_element_type=jnp.float32)

    def first_sums(span, j):
        partial[span, j] = product(j).astype(jnp.bfloat16)

    def later_sums(span, j):
        row_copy(span, j).wait_recv()
        partial[span, j] = (
            base_ref[span, j]
            + jnp.dot(picks_ref[span, :, span_of(span)], fresh_ref[j, span_of(span), :], preferred_element_type=jnp.float32)
        ).astype(jnp.bfloat16)

    def scatter(span, sums):
        for j in range(pieces):
            sums(span, j)

            @pl.when(at_end)
            def _(j=j):
                pass_copy(span, j).start()

            @pl.when(jnp.logical_not(at_end))
            def _(j=j):
                for step in (1, last):
                    part_copy(span, step, j).start()

        for j in range(pieces):
            for step in (2, 1, last):
                @pl.when(at_end & is_sent(step))
                def _(step=step, j=j):
                    part_copy(span, step, j).start()

    def pass_on(span):
        for who, step in ((1, last - 1), (last - 1, 2)):
            @pl.when(vertex == who)
            def _(who=who, step=step):
                far = last if who == 1 else 0
                here = pl.ds(far * span_rows, span_rows)
                for j in range(pieces):
                    pass_copy(span, j).wait_recv()
                    partial[span, j, here] = (
                        partial[span, j, here].astype(jnp.float32) + passing[span, j].astype(jnp.float32)
                    ).astype(jnp.bfloat16)
                    part_copy(span, step, j).start()

    def keep(span):
        used = (span + 1) * span_rows
        for j in range(pieces):
            base_ref[span, j] = product(j)
        picks_ref[span, :, :used] = jnp.dot(
            left[...], right_select[:, :used], preferred_element_type=jnp.float32
        ).astype(jnp.bfloat16)

    def earlier(span):
        used = span * span_rows
        for j in range(pieces):
            base_ref[span, j] += jnp.dot(
                picks_ref[span, :, :used], fresh_ref[j, :used, :], preferred_element_type=jnp.float32
            )

    def weight_rows(which, j):
        return pl.ds(pl.multiple_of(which * width + j * part, part), part)

    def finish(span):
        for j in range(pieces):
            for step in range(1, vertices):
                @pl.when(is_received(step))
                def _(step=step, j=j):
                    part_copy(span, step, j).wait_recv()

            total = partial[span, j, rows_of(vertex)].astype(jnp.float32)
            for step in range(1, vertices):
                total += parts[span, step - 1, j].astype(jnp.float32)
            support[span, j] = (
                (1.0 - RESIDUAL_SHARE) * total
                + RESIDUAL_SHARE * initial_ref[span_of(span), columns(j)].astype(jnp.float32)
            ).astype(jnp.bfloat16)
            support_copy(span, j).start()

        projected = [
            sum(
                jnp.dot(support[span, k], weight_ref[weight_rows(feat, k), columns(j)], preferred_element_type=jnp.float32)
                for k in range(pieces)
            )
            for j in range(pieces)
        ]
        for j in range(pieces):
            support_copy(span, j).wait_recv()
        for j in range(pieces):
            for k in range(pieces):
                projected[j] += jnp.dot(
                    other[span, k], weight_ref[weight_rows(partner, k), columns(j)], preferred_element_type=jnp.float32
                )
            rows = jnp.maximum(
                (1.0 - beta) * support[span, j].astype(jnp.float32) + beta * projected[j], 0.0
            ).astype(jnp.bfloat16)
            result[span, j] = rows

            @pl.when(section < sections - 1)
            def _(j=j):
                row_copy(span, j).start()

            out_ref[span, :, columns(j)] = rows

    load_kept.wait()
    load_features.wait()

    @pl.when(section == 0)
    def _():
        for span in range(spans):
            mark(span, True)
            lay(span, True)
            if span == 0:
                meet()
            else:
                pass_on(span - 1)
            scatter(span, first_sums)
        gather()
        load_weight.wait()
        for span in range(spans - 1):
            finish(span)
            if span == spans - 2:
                pass_on(spans - 1)

    @pl.when(section > 0)
    def _():
        for span in range(spans):
            mark(span, False)
            lay(span, False)
            keep(span)
        gather()
        load_weight.wait()
        meet()
        for span in range(spans):
            scatter(span, later_sums)
            if span:
                finish(span - 1)
            pass_on(span)
            if span + 1 < spans:
                earlier(span + 1)

    def merge(i, _):
        for j in range(pieces):
            moved = jnp.dot(select_ref[i], fresh_ref[j], preferred_element_type=jnp.float32)
            kept_ref[i, :, columns(j)] = (kept_ref[i, :, columns(j)].astype(jnp.float32) + moved).astype(jnp.bfloat16)
        return 0

    @pl.when(section > 0)
    def _():
        lax.fori_loop(0, col_blocks, merge, 0)

    store = pltpu.make_async_copy(kept_ref, table_hbm, table_sem)
    store.start()
    finish(spans - 1)

    for span in range(spans):
        for j in range(pieces):
            support_copy(span, j).wait_send()
            for step in range(1, vertices):
                @pl.when(is_sent(step))
                def _(span=span, step=step, j=j):
                    part_copy(span, step, j).wait_send()

            @pl.when(at_end)
            def _(span=span, j=j):
                pass_copy(span, j).wait_send()

            @pl.when(section < sections - 1)
            def _(span=span, j=j):
                row_copy(span, j).wait_send()

    store.wait()


def deliver(rows_hbm, table_hbm, rows_out, table_out, rows_ref, table_ref, in_sem, out_sem):
    chunks = in_sem.shape[0] - 1
    size = table_ref.shape[0] // chunks
    moves = []
    for i in range(chunks):
        here = pl.ds(i * size, size)
        moves.append((
            pltpu.make_async_copy(table_hbm.at[here], table_ref.at[here], in_sem.at[i]),
            pltpu.make_async_copy(table_ref.at[here], table_out.at[here], out_sem.at[i]),
        ))
    moves.append((
        pltpu.make_async_copy(rows_hbm, rows_ref, in_sem.at[chunks]),
        pltpu.make_async_copy(rows_ref, rows_out, out_sem.at[chunks]),
    ))
    for get, _ in moves:
        get.start()
    for get, put in moves:
        get.wait()
        put.start()
    for _, put in moves:
        put.wait()


def long_line(sizes, features, history, weights, tile_values, tile_rows, tile_cols, tile_counts, span_ids):
    sections, vertices, feats = sizes
    spans, span_rows = span_ids.shape
    owned, width = features.shape
    rows_whole = span_rows * vertices
    rows_all = spans * span_rows
    vmem = pl.BlockSpec(memory_space=pltpu.VMEM)
    smem = pl.BlockSpec(memory_space=pltpu.SMEM)
    anywhere = pl.BlockSpec(memory_space=pl.ANY)

    dense = pl.pallas_call(
        prepare,
        name="prepare",
        out_shape=jax.ShapeDtypeStruct((spans, rows_whole, owned), jnp.bfloat16),
        in_specs=[smem, smem, smem, vmem],
        out_specs=anywhere,
        scratch_shapes=[
            pltpu.VMEM((spans, rows_whole, owned), jnp.bfloat16),
            pltpu.SemaphoreType.DMA((spans,)),
        ],
        compiler_params=pltpu.CompilerParams(vmem_limit_bytes=VMEM_BYTES),
    )(tile_rows, tile_cols, tile_counts.reshape(1, spans), tile_values)

    rows_type = jax.ShapeDtypeStruct((spans, span_rows, width), jnp.bfloat16)
    table_type = jax.ShapeDtypeStruct((owned, width), jnp.bfloat16)
    block = pltpu.VMEM(rows_type.shape, jnp.bfloat16)
    halves = 2
    pair = pltpu.SemaphoreType.DMA((spans, halves))
    return pl.pallas_call(
        functools.partial(relay, sections, vertices, feats),
        name="relay",
        out_shape=(rows_type, table_type),
        in_specs=[anywhere, vmem, anywhere, anywhere, anywhere],
        out_specs=(vmem, anywhere),
        scratch_shapes=[
            pltpu.VMEM((min(2, spans), rows_whole, owned), jnp.bfloat16),
            pltpu.VMEM((spans, rows_whole, width), jnp.float32),
            pltpu.VMEM((spans, rows_whole, rows_all), jnp.bfloat16),
            pltpu.VMEM(weights.shape[1:], weights.dtype),
            pltpu.VMEM((owned, width), jnp.bfloat16),
            pltpu.VMEM((owned, width), jnp.bfloat16),
            pltpu.VMEM((owned, rows_all), jnp.bfloat16),
            pltpu.VMEM((rows_all, width), jnp.bfloat16),
            pltpu.VMEM((rows_all, width), jnp.bfloat16),
            block,
            pltpu.VMEM((spans, rows_whole, width), jnp.bfloat16),
            pltpu.VMEM((spans, vertices - 1, span_rows, width), jnp.bfloat16),
            block, block, block, block,
            pltpu.SemaphoreType.DMA((spans + 3,)),
            pltpu.SemaphoreType.DMA,
            pair, pair,
            pltpu.SemaphoreType.DMA((spans, vertices - 1, halves)),
            pltpu.SemaphoreType.DMA((spans, vertices - 1, halves)),
            pair, pair, pair, pair,
        ],
        compiler_params=pltpu.CompilerParams(
            vmem_limit_bytes=VMEM_BYTES, collective_id=0, has_side_effects=True
        ),
    )(dense, span_ids, weights[0], history[0], features)


def short_line(sizes, features, history, weights, tile_values, tile_rows, tile_cols, tile_counts, span_ids):
    sections, vertices, feats = sizes
    spans, span_rows = span_ids.shape
    slots, side = tile_values.shape[1:3]
    owned, width = features.shape
    rows_whole = span_rows * vertices
    rows_all = spans * span_rows
    pieces = 2
    part = width // pieces
    vmem = pl.BlockSpec(memory_space=pltpu.VMEM)
    smem = pl.BlockSpec(memory_space=pltpu.SMEM)
    anywhere = pl.BlockSpec(memory_space=pl.ANY)
    block = pltpu.VMEM((spans, pieces, span_rows, part), jnp.bfloat16)
    pair = pltpu.SemaphoreType.DMA((spans, pieces))
    triple = pltpu.SemaphoreType.DMA((spans, vertices - 1, pieces))
    table = history[0].reshape(owned // side, side, width)
    layer_rows, table_new = pl.pallas_call(
        functools.partial(stream, sections, vertices, feats),
        name="stream",
        out_shape=(
            jax.ShapeDtypeStruct((spans, span_rows, width), jnp.bfloat16),
            jax.ShapeDtypeStruct(table.shape, jnp.bfloat16),
        ),
        in_specs=[smem, smem, smem, vmem, anywhere, anywhere, anywhere, anywhere],
        out_specs=(vmem, anywhere),
        scratch_shapes=[
            pltpu.VMEM(tile_values.shape, jnp.bfloat16),
            pltpu.VMEM((rows_whole, slots * side), jnp.bfloat16),
            pltpu.VMEM((slots * side, width), jnp.bfloat16),
            pltpu.VMEM((slots * side, rows_all), jnp.bfloat16),
            pltpu.VMEM((spans, pieces, rows_whole, part), jnp.float32),
            pltpu.VMEM((spans, rows_whole, rows_all), jnp.bfloat16),
            pltpu.VMEM(weights.shape[1:], weights.dtype),
            pltpu.VMEM(table.shape, jnp.bfloat16),
            pltpu.VMEM(table.shape, jnp.bfloat16),
            pltpu.VMEM((owned // side, side, rows_all), jnp.bfloat16),
            pltpu.VMEM((rows_all, width), jnp.bfloat16),
            pltpu.VMEM((pieces, rows_all, part), jnp.bfloat16),
            pltpu.VMEM((spans, pieces, rows_whole, part), jnp.bfloat16),
            pltpu.VMEM((spans, vertices - 1, pieces, span_rows, part), jnp.bfloat16),
            block, block, block, block,
            pltpu.SemaphoreType.DMA((spans + 3,)),
            pltpu.SemaphoreType.DMA,
            pair, pair, triple, triple, pair, pair, pair, pair,
        ],
        compiler_params=pltpu.CompilerParams(
            vmem_limit_bytes=VMEM_BYTES, collective_id=0, has_side_effects=True
        ),
    )(tile_rows, tile_cols, tile_counts.reshape(1, spans), span_ids, tile_values, weights[0], table,
      features.reshape(table.shape))
    return layer_rows, table_new.reshape(owned, width)


def shards(sizes, features, history, weights, tile_values, tile_rows, tile_cols, tile_counts, span_ids):
    spans, span_rows = span_ids.shape
    owned, width = features.shape
    rows_type = jax.ShapeDtypeStruct((spans, span_rows, width), jnp.bfloat16)
    table_type = jax.ShapeDtypeStruct((owned, width), jnp.bfloat16)
    anywhere = pl.BlockSpec(memory_space=pl.ANY)
    layers = short_line if sizes[1] == LINE else long_line
    layer_rows, table_new = layers(
        sizes, features, history, weights, tile_values, tile_rows, tile_cols, tile_counts, span_ids
    )

    chunks = 8
    layer_rows, table_new = pl.pallas_call(
        deliver,
        name="deliver",
        out_shape=(rows_type, table_type),
        in_specs=[anywhere, anywhere],
        out_specs=(anywhere, anywhere),
        scratch_shapes=[
            pltpu.VMEM(rows_type.shape, jnp.bfloat16),
            pltpu.VMEM(table_type.shape, jnp.bfloat16),
            pltpu.SemaphoreType.DMA((chunks + 1,)),
            pltpu.SemaphoreType.DMA((chunks + 1,)),
        ],
        compiler_params=pltpu.CompilerParams(vmem_limit_bytes=VMEM_BYTES),
    )(layer_rows, table_new)
    return (layer_rows[None], table_new[None])


def solution(mesh):
    placed = (
        P("vertex", "feat"),
        P("section", "vertex", "feat"),
        P("section", None, "feat"),
        P(None, "vertex", None, None),
        P(None, "vertex"),
        P(None, "vertex"),
        P(None, "vertex"),
        P(None, "vertex"),
    )
    sizes = (mesh.shape["section"], mesh.shape["vertex"], mesh.shape["feat"])
    return jax.shard_map(
        functools.partial(shards, sizes),
        mesh=mesh,
        in_specs=placed,
        out_specs=(P("section", None, "vertex", "feat"), P("section", "vertex", "feat")),
        check_vma=False,
    )
```

```python
import functools

import jax
import jax.numpy as jnp
from jax import lax
from jax.experimental import pallas as pl
from jax.experimental.pallas import tpu as pltpu
from jax.sharding import PartitionSpec as P

RESIDUAL_SHARE = 0.2
BETA_SCALE = 0.5
MESH = pl.DeviceIdType.MESH
VMEM_BYTES = 60_000 * 1024


def chosen(ids_row, rows, first=0):
    shape = (rows, ids_row.shape[1])
    return (lax.broadcasted_iota(jnp.int32, shape, 0) + first == ids_row).astype(jnp.float32)


def prepare(rows_ref, cols_ref, counts_ref, tiles_ref, dense_hbm, dense, dense_sem):
    spans, _, side, _ = tiles_ref.shape
    copies = []
    for span in range(spans):
        dense[span] = jnp.zeros(dense.shape[1:], dense.dtype)

        def place(t, _, span=span):
            row = pl.multiple_of(rows_ref[span, t] * side, side)
            col = pl.multiple_of(cols_ref[span, t] * side, side)
            dense[span, pl.ds(row, side), pl.ds(col, side)] = tiles_ref[span, t]
            return 0

        lax.fori_loop(0, counts_ref[0, span], place, 0)
        copies.append(pltpu.make_async_copy(dense.at[span], dense_hbm.at[span], dense_sem.at[span]))
        copies[-1].start()
    for copy in copies:
        copy.wait()


def relay(
    sections, vertices, feats,
    dense_hbm, ids_ref, weight_hbm, kept_hbm, features_hbm, out_ref, table_hbm,
    dense, base_ref, picks_ref, weight_ref, kept_ref, features_ref, select_ref, initial_ref, fresh_ref,
    arrived, partial, parts, passing, support, other, result,
    load_sem, table_sem, x_send, x_recv, p_send, p_recv, h_send, h_recv, s_send, s_recv,
):
    section = lax.axis_index("section")
    vertex = lax.axis_index("vertex")
    feat = lax.axis_index("feat")
    spans, span_rows, width = arrived.shape
    last = vertices - 1
    partner = lax.rem(feat + 1, feats)
    beta = jnp.log(BETA_SCALE / (section + 1).astype(jnp.float32) + 1.0)
    halves = 2
    piece = span_rows // halves
    relayed = vertices > 3

    rows_whole = dense.shape[1]
    owned = kept_ref.shape[0]
    group = min(512, rows_whole)
    chunk = min(256, owned)

    def load_dense(span):
        return pltpu.make_async_copy(dense_hbm.at[span], dense.at[span % 2], load_sem.at[span])

    load_weight = pltpu.make_async_copy(weight_hbm, weight_ref, load_sem.at[spans])
    load_kept = pltpu.make_async_copy(kept_hbm, kept_ref, load_sem.at[spans + 1])
    load_features = pltpu.make_async_copy(features_hbm, features_ref, load_sem.at[spans + 2])
    load_kept.start()
    load_features.start()
    for span in range(min(2, spans)):
        load_dense(span).start()
    load_weight.start()

    barrier = pltpu.get_barrier_semaphore()
    for step in range(1, vertices):
        peer = lax.rem(vertex + step, vertices)
        pl.semaphore_signal(barrier, inc=1, device_id=(section, peer, feat), device_id_type=MESH)
    pl.semaphore_signal(barrier, inc=1, device_id=(section, vertex, partner), device_id_type=MESH)
    for step in (1, sections - 1):
        peer = lax.rem(section + step, sections)
        pl.semaphore_signal(barrier, inc=1, device_id=(peer, vertex, feat), device_id_type=MESH)
    if relayed:
        @pl.when(vertex == 0)
        def _():
            parts[:, 0] = jnp.zeros((spans, span_rows, width), jnp.bfloat16)

        @pl.when(vertex == last)
        def _():
            parts[:, last - 1] = jnp.zeros((spans, span_rows, width), jnp.bfloat16)

    pl.semaphore_wait(barrier, vertices - 1 + 1 + 2)

    def half_of(half):
        return slice(half * piece, (half + 1) * piece)

    def row_copy(span, half):
        rows = pl.ds(half * piece, piece)
        return pltpu.make_async_remote_copy(
            src_ref=result.at[span, rows], dst_ref=arrived.at[span, rows],
            send_sem=x_send.at[span, half], recv_sem=x_recv.at[span, half],
            device_id=(lax.rem(section + 1, sections), vertex, feat), device_id_type=MESH,
        )

    def chunk_rows(peer, half):
        return pl.ds(pl.multiple_of(peer * span_rows + half * piece, piece), piece)

    def part_copy(span, step, half):
        peer = lax.rem(vertex + step, vertices)
        return pltpu.make_async_remote_copy(
            src_ref=partial.at[span, chunk_rows(peer, half)],
            dst_ref=parts.at[span, step - 1, pl.ds(half * piece, piece)],
            send_sem=p_send.at[span, step - 1, half], recv_sem=p_recv.at[span, step - 1, half],
            device_id=(section, peer, feat), device_id_type=MESH,
        )

    def pass_copy(span, half):
        far = jnp.where(vertex == 0, last, 0)
        near = jnp.where(vertex == 0, 1, last - 1)
        return pltpu.make_async_remote_copy(
            src_ref=partial.at[span, chunk_rows(far, half)],
            dst_ref=passing.at[span, pl.ds(half * piece, piece)],
            send_sem=h_send.at[span, half], recv_sem=h_recv.at[span, half],
            device_id=(section, near, feat), device_id_type=MESH,
        )

    def support_copy(span, half):
        rows = pl.ds(half * piece, piece)
        return pltpu.make_async_remote_copy(
            src_ref=support.at[span, rows], dst_ref=other.at[span, rows],
            send_sem=s_send.at[span, half], recv_sem=s_recv.at[span, half],
            device_id=(section, vertex, partner), device_id_type=MESH,
        )

    at_end = (vertex == 0) | (vertex == last)

    def is_direct(step):
        if not relayed:
            return vertex >= 0
        peer = lax.rem(vertex + step, vertices)
        ends = ((vertex == 0) & (peer == last)) | ((vertex == last) & (peer == 0))
        inner = ((vertex == 1) & (peer == last)) | ((vertex == last - 1) & (peer == 0))
        return jnp.logical_not(ends | inner)

    def is_sent(step):
        if not relayed:
            return vertex >= 0
        peer = lax.rem(vertex + step, vertices)
        return jnp.logical_not(((vertex == 0) & (peer == last)) | ((vertex == last) & (peer == 0)))

    def is_received(step):
        if not relayed:
            return vertex >= 0
        source = lax.rem(vertex + vertices - step, vertices)
        return jnp.logical_not(((vertex == 0) & (source == last)) | ((vertex == last) & (source == 0)))

    def local(span, leading):
        mine = slice(span * span_rows, (span + 1) * span_rows)
        used = (span + 1) * span_rows

        def clear(i, _):
            first = pl.multiple_of(i * chunk, chunk)
            here = pl.ds(first, chunk)
            hot = chosen(ids_ref[span : span + 1, :], chunk, first)
            select_ref[here, mine] = hot.astype(jnp.bfloat16)
            taken = jnp.max(hot, axis=1, keepdims=True) > 0.5
            filler = features_ref[here, :].astype(jnp.float32) if leading else 0.0
            kept_ref[here, :] = jnp.where(taken, filler, kept_ref[here, :].astype(jnp.float32)).astype(jnp.bfloat16)
            return 0

        lax.fori_loop(0, owned // chunk, clear, 0)
        load_dense(span).wait()

        def multiply(i, _):
            here = pl.ds(pl.multiple_of(i * group, group), group)
            block = dense[span % 2, here, :]
            product = jnp.dot(block, kept_ref[...], preferred_element_type=jnp.float32)
            if leading:
                partial[span, here, :] = product.astype(jnp.bfloat16)
            else:
                base_ref[span, here, :] = product
                picks_ref[span, here, :used] = jnp.dot(
                    block, select_ref[:, :used], preferred_element_type=jnp.float32
                ).astype(jnp.bfloat16)
            return 0

        lax.fori_loop(0, rows_whole // group, multiply, 0)
        if span + 2 < spans:
            load_dense(span + 2).start()

    def gather():
        initial_ref[...] = lax.dot_general(
            select_ref[...], features_ref[...], (((0,), (0,)), ((), ())), preferred_element_type=jnp.float32
        ).astype(jnp.bfloat16)

    def earlier(span):
        used = span * span_rows

        def add(i, _):
            here = pl.ds(pl.multiple_of(i * group, group), group)
            base_ref[span, here, :] += jnp.dot(
                picks_ref[span, here, :used], fresh_ref[:used, :], preferred_element_type=jnp.float32
            )
            return 0

        lax.fori_loop(0, rows_whole // group, add, 0)

    def scatter(span):
        mine = slice(span * span_rows, (span + 1) * span_rows)
        @pl.when(section > 0)
        def _():
            for half in range(halves):
                row_copy(span, half).wait_recv()
            fresh_ref[mine, :] = arrived[span]


        def compute(peer):
            here = pl.ds(pl.multiple_of(peer * span_rows, span_rows), span_rows)
            total = base_ref[span, here, :] + jnp.dot(
                picks_ref[span, here, mine], fresh_ref[mine, :], preferred_element_type=jnp.float32
            )
            partial[span, here, :] = total.astype(jnp.bfloat16)

        if relayed:
            @pl.when(at_end & (section > 0))
            def _():
                compute(jnp.where(vertex == 0, last, 0))

            @pl.when(at_end)
            def _():
                for half in range(halves):
                    pass_copy(span, half).start()

        for step in range(1, vertices):
            @pl.when(is_sent(step) & (section > 0))
            def _(step=step):
                compute(lax.rem(vertex + step, vertices))

            @pl.when(is_direct(step))
            def _(step=step):
                part_copy(span, step, 0).start()

        for half in range(1, halves):
            for step in range(1, vertices):
                @pl.when(is_direct(step))
                def _(step=step, half=half):
                    part_copy(span, step, half).start()

        @pl.when(section > 0)
        def _():
            compute(vertex)

    def pass_on(span):
        if relayed:
            for who, step in ((1, last - 1), (last - 1, 2)):
                @pl.when(vertex == who)
                def _(who=who, step=step):
                    far = last if who == 1 else 0
                    for half in range(halves):
                        pass_copy(span, half).wait_recv()
                        here = pl.ds(far * span_rows + half * piece, piece)
                        partial[span, here, :] = (
                            partial[span, here, :].astype(jnp.float32)
                            + passing[span, half_of(half), :].astype(jnp.float32)
                        ).astype(jnp.bfloat16)
                        part_copy(span, step, half).start()

    def finish(span, half):
        total = partial[span, chunk_rows(vertex, half), :].astype(jnp.float32)
        for step in range(1, vertices):
            @pl.when(is_received(step))
            def _(step=step):
                part_copy(span, step, half).wait_recv()

        for step in range(1, vertices):
            total += parts[span, step - 1, half_of(half), :].astype(jnp.float32)
        mixed = (
            (1.0 - RESIDUAL_SHARE) * total
            + RESIDUAL_SHARE * initial_ref[pl.ds(span * span_rows + half * piece, piece), :].astype(jnp.float32)
        ).astype(jnp.bfloat16)
        support[span, half_of(half), :] = mixed
        support_copy(span, half).start()
        mine = pl.ds(pl.multiple_of(feat * width, width), width)
        theirs = pl.ds(pl.multiple_of(partner * width, width), width)
        projected = jnp.dot(mixed, weight_ref[mine, :], preferred_element_type=jnp.float32)
        support_copy(span, half).wait_recv()
        projected += jnp.dot(other[span, half_of(half), :], weight_ref[theirs, :], preferred_element_type=jnp.float32)
        rows = jnp.maximum((1.0 - beta) * mixed.astype(jnp.float32) + beta * projected, 0.0).astype(jnp.bfloat16)
        result[span, half_of(half), :] = rows
        out_ref[span, half_of(half), :] = rows

        @pl.when(section < sections - 1)
        def _():
            row_copy(span, half).start()

    def finish_all(span):
        for half in range(halves):
            finish(span, half)

    load_kept.wait()
    load_features.wait()

    @pl.when(section == 0)
    def _():
        for span in range(spans):
            local(span, True)
            scatter(span)
            if span:
                pass_on(span - 1)
        gather()
        load_weight.wait()
        for span in range(spans - 1):
            finish_all(span)
            if span == 0:
                pass_on(spans - 1)

    @pl.when(section > 0)
    def _():
        for span in range(spans):
            local(span, False)
        gather()
        load_weight.wait()
        for span in range(spans):
            scatter(span)
            pass_on(span)
            if span:
                finish_all(span - 1)
            if span + 1 < spans:
                earlier(span + 1)

    def merge(i, _):
        here = pl.ds(pl.multiple_of(i * chunk, chunk), chunk)
        moved = jnp.dot(select_ref[here, :], fresh_ref[...], preferred_element_type=jnp.float32)
        kept_ref[here, :] = (kept_ref[here, :].astype(jnp.float32) + moved).astype(jnp.bfloat16)
        return 0

    @pl.when(section > 0)
    def _():
        lax.fori_loop(0, owned // chunk, merge, 0)

    store = pltpu.make_async_copy(kept_ref, table_hbm, table_sem)
    store.start()
    finish_all(spans - 1)

    for span in range(spans):
        for half in range(halves):
            support_copy(span, half).wait_send()
            for step in range(1, vertices):
                @pl.when(is_sent(step))
                def _(span=span, step=step, half=half):
                    part_copy(span, step, half).wait_send()

            if relayed:
                @pl.when(at_end)
                def _(span=span, half=half):
                    pass_copy(span, half).wait_send()

            @pl.when(section < sections - 1)
            def _(span=span, half=half):
                row_copy(span, half).wait_send()

    store.wait()

LINE = 4


def stream(
    sections, vertices, feats,
    rows_ref, cols_ref, counts_ref, ids_ref, tiles_hbm, weight_hbm, kept_hbm, features_hbm, out_ref, table_hbm,
    tiles, left, right, right_select, base_ref, picks_ref, weight_ref, kept_ref, features_ref, select_ref, initial_ref,
    fresh_ref, partial, parts, passing, transit, support, other, result,
    load_sem, table_sem, x_send, x_recv, p_send, p_recv, h_send, h_recv, s_send, s_recv, d_send, d_recv, t_send,
):
    section = lax.axis_index("section")
    vertex = lax.axis_index("vertex")
    feat = lax.axis_index("feat")
    spans, pieces, span_rows, part = result.shape
    slots, side = tiles.shape[1:3]
    row_blocks = left.shape[0] // side
    width = pieces * part
    rows_all = spans * span_rows
    last = vertices - 1
    partner = lax.rem(feat + 1, feats)
    beside = lax.rem(section + sections // 2, sections)
    opposite = lax.rem(vertex + last - 1, vertices)
    beta = jnp.log(BETA_SCALE / (section + 1).astype(jnp.float32) + 1.0)
    col_blocks = kept_ref.shape[0]

    def load_tiles(span):
        return pltpu.make_async_copy(tiles_hbm.at[span], tiles.at[span], load_sem.at[span])

    load_weight = pltpu.make_async_copy(weight_hbm, weight_ref, load_sem.at[spans])
    load_kept = pltpu.make_async_copy(kept_hbm, kept_ref, load_sem.at[spans + 1])
    load_features = pltpu.make_async_copy(features_hbm, features_ref, load_sem.at[spans + 2])
    load_kept.start()
    load_features.start()
    for span in range(spans):
        load_tiles(span).start()
    load_weight.start()

    barrier = pltpu.get_barrier_semaphore()
    for step in range(1, vertices):
        peer = lax.rem(vertex + step, vertices)
        pl.semaphore_signal(barrier, inc=1, device_id=(section, peer, feat), device_id_type=MESH)
    pl.semaphore_signal(barrier, inc=1, device_id=(section, vertex, partner), device_id_type=MESH)
    for step in (1, sections - 1):
        peer = lax.rem(section + step, sections)
        pl.semaphore_signal(barrier, inc=1, device_id=(peer, vertex, feat), device_id_type=MESH)
    for peer in (vertex, opposite):
        pl.semaphore_signal(barrier, inc=1, device_id=(beside, peer, feat), device_id_type=MESH)

    def meet():
        pl.semaphore_wait(barrier, vertices - 1 + 1 + 2 + 2)

    at_end = (vertex == 0) | (vertex == last)

    @pl.when(vertex == 0)
    def _():
        parts[:, 0] = jnp.zeros(parts.shape[:1] + parts.shape[2:], jnp.bfloat16)

    @pl.when(vertex == last)
    def _():
        parts[:, last - 1] = jnp.zeros(parts.shape[:1] + parts.shape[2:], jnp.bfloat16)

    def columns(j):
        return slice(j * part, (j + 1) * part)

    def span_of(span):
        return slice(span * span_rows, (span + 1) * span_rows)

    def row_copy(span, j):
        return pltpu.make_async_remote_copy(
            src_ref=result.at[span, j], dst_ref=fresh_ref.at[j, pl.ds(span * span_rows, span_rows)],
            send_sem=x_send.at[span, j], recv_sem=x_recv.at[span, j],
            device_id=(lax.rem(section + 1, sections), vertex, feat), device_id_type=MESH,
        )

    def rows_of(peer):
        return pl.ds(pl.multiple_of(peer * span_rows, span_rows), span_rows)

    def part_copy(span, step, j):
        peer = lax.rem(vertex + step, vertices)
        return pltpu.make_async_remote_copy(
            src_ref=partial.at[span, j, rows_of(peer)], dst_ref=parts.at[span, step - 1, j],
            send_sem=p_send.at[span, step - 1, j], recv_sem=p_recv.at[span, step - 1, j],
            device_id=(section, peer, feat), device_id_type=MESH,
        )

    def pass_copy(span, j):
        far = jnp.where(vertex == 0, last, 0)
        near = jnp.where(vertex == 0, 1, last - 1)
        return pltpu.make_async_remote_copy(
            src_ref=partial.at[span, j, rows_of(far)], dst_ref=passing.at[span, j],
            send_sem=h_send.at[span, j], recv_sem=h_recv.at[span, j],
            device_id=(section, near, feat), device_id_type=MESH,
        )

    def detour_copy(span, j):
        return pltpu.make_async_remote_copy(
            src_ref=partial.at[span, j, rows_of(opposite)], dst_ref=transit.at[span, j],
            send_sem=d_send.at[span, j], recv_sem=d_recv.at[span, j],
            device_id=(beside, vertex, feat), device_id_type=MESH,
        )

    def return_copy(span, j):
        return pltpu.make_async_remote_copy(
            src_ref=transit.at[span, j], dst_ref=parts.at[span, last - 2, j],
            send_sem=t_send.at[span, j], recv_sem=p_recv.at[span, last - 2, j],
            device_id=(beside, opposite, feat), device_id_type=MESH,
        )

    def support_copy(span, j):
        return pltpu.make_async_remote_copy(
            src_ref=support.at[span, j], dst_ref=other.at[span, j],
            send_sem=s_send.at[span, j], recv_sem=s_recv.at[span, j],
            device_id=(section, vertex, partner), device_id_type=MESH,
        )

    def ends_meet(here, there):
        return ((here == 0) & (there == last)) | ((here == last) & (there == 0))

    def is_sent(step):
        far = ends_meet(vertex, lax.rem(vertex + step, vertices))
        return jnp.logical_not(far | at_end) if step == last - 1 else jnp.logical_not(far)

    def is_received(step):
        return jnp.logical_not(ends_meet(lax.rem(vertex + vertices - step, vertices), vertex))

    def mark(span, leading):
        def clear(i, _):
            hot = chosen(ids_ref[span : span + 1, :], side, i * side)
            select_ref[i, :, span_of(span)] = hot.astype(jnp.bfloat16)
            taken = jnp.max(hot, axis=1, keepdims=True) > 0.5
            filler = features_ref[i].astype(jnp.float32) if leading else 0.0
            kept_ref[i] = jnp.where(taken, filler, kept_ref[i].astype(jnp.float32)).astype(jnp.bfloat16)
            return 0

        lax.fori_loop(0, col_blocks, clear, 0)

    def lay(span, leading):
        used = (span + 1) * span_rows
        load_tiles(span).wait()
        lives = jnp.full((side, side), counts_ref[0, span], jnp.int32)

        def place(t, _):
            col = cols_ref[span, t]
            here = pl.ds(pl.multiple_of(t * side, side), side)
            tile = tiles[span, t].astype(jnp.float32)
            rows = jnp.where(lives > t, jnp.full(tile.shape, rows_ref[span, t], jnp.int32), row_blocks)
            for block in range(row_blocks):
                left[block * side : (block + 1) * side, here] = jnp.where(rows == block, tile, 0.0).astype(left.dtype)
            right[here, :] = kept_ref[col]
            if not leading:
                right_select[here, :] = select_ref[col]
            return 0

        lax.fori_loop(0, slots, place, 0)

    def gather():
        initial_ref[...] = lax.dot_general(
            select_ref[...].reshape(col_blocks * side, rows_all),
            features_ref[...].reshape(col_blocks * side, width),
            (((0,), (0,)), ((), ())),
            preferred_element_type=jnp.float32,
        ).astype(jnp.bfloat16)

    def product(j):
        return jnp.dot(left[...], right[:, columns(j)], preferred_element_type=jnp.float32)

    def first_sums(span, j):
        partial[span, j] = product(j).astype(jnp.bfloat16)

    def later_sums(span, j):
        row_copy(span, j).wait_recv()
        partial[span, j] = (
            base_ref[span, j]
            + jnp.dot(picks_ref[span, :, span_of(span)], fresh_ref[j, span_of(span), :], preferred_element_type=jnp.float32)
        ).astype(jnp.bfloat16)

    def scatter(span, sums):
        for j in range(pieces):
            sums(span, j)

            @pl.when(at_end)
            def _(j=j):
                pass_copy(span, j).start()
                detour_copy(span, j).start()

            @pl.when(jnp.logical_not(at_end))
            def _(j=j):
                for step in (1, last):
                    part_copy(span, step, j).start()

        for j in range(pieces):
            for step in (1, last):
                @pl.when(at_end & is_sent(step))
                def _(step=step, j=j):
                    part_copy(span, step, j).start()

    def pass_on(span):
        for who, step in ((1, last - 1), (last - 1, 2)):
            @pl.when(vertex == who)
            def _(who=who, step=step):
                far = last if who == 1 else 0
                here = pl.ds(far * span_rows, span_rows)
                for j in range(pieces):
                    pass_copy(span, j).wait_recv()
                    partial[span, j, here] = (
                        partial[span, j, here].astype(jnp.float32) + passing[span, j].astype(jnp.float32)
                    ).astype(jnp.bfloat16)
                    part_copy(span, step, j).start()

    def hand_on(span):
        @pl.when(at_end)
        def _():
            for j in range(pieces):
                detour_copy(span, j).wait_recv()
                return_copy(span, j).start()

    def keep(span):
        used = (span + 1) * span_rows
        for j in range(pieces):
            base_ref[span, j] = product(j)
        picks_ref[span, :, :used] = jnp.dot(
            left[...], right_select[:, :used], preferred_element_type=jnp.float32
        ).astype(jnp.bfloat16)

    def earlier(span):
        used = span * span_rows
        for j in range(pieces):
            base_ref[span, j] += jnp.dot(
                picks_ref[span, :, :used], fresh_ref[j, :used, :], preferred_element_type=jnp.float32
            )

    def weight_rows(which, j):
        return pl.ds(pl.multiple_of(which * width + j * part, part), part)

    def finish(span):
        for j in range(pieces):
            for step in range(1, vertices):
                @pl.when(is_received(step))
                def _(step=step, j=j):
                    part_copy(span, step, j).wait_recv()

            total = partial[span, j, rows_of(vertex)].astype(jnp.float32)
            for step in range(1, vertices):
                total += parts[span, step - 1, j].astype(jnp.float32)
            support[span, j] = (
                (1.0 - RESIDUAL_SHARE) * total
                + RESIDUAL_SHARE * initial_ref[span_of(span), columns(j)].astype(jnp.float32)
            ).astype(jnp.bfloat16)
            support_copy(span, j).start()

        projected = [
            sum(
                jnp.dot(support[span, k], weight_ref[weight_rows(feat, k), columns(j)], preferred_element_type=jnp.float32)
                for k in range(pieces)
            )
            for j in range(pieces)
        ]
        for j in range(pieces):
            support_copy(span, j).wait_recv()
        for j in range(pieces):
            for k in range(pieces):
                projected[j] += jnp.dot(
                    other[span, k], weight_ref[weight_rows(partner, k), columns(j)], preferred_element_type=jnp.float32
                )
            rows = jnp.maximum(
                (1.0 - beta) * support[span, j].astype(jnp.float32) + beta * projected[j], 0.0
            ).astype(jnp.bfloat16)
            result[span, j] = rows

            @pl.when(section < sections - 1)
            def _(j=j):
                row_copy(span, j).start()

            out_ref[span, :, columns(j)] = rows

    load_kept.wait()
    load_features.wait()

    @pl.when(section == 0)
    def _():
        for span in range(spans):
            mark(span, True)
            lay(span, True)
            if span == 0:
                meet()
            scatter(span, first_sums)
            if span:
                pass_on(span - 1)
        gather()
        load_weight.wait()
        for span in range(spans - 1):
            finish(span)
            if span == spans - 2:
                pass_on(spans - 1)

    @pl.when(section > 0)
    def _():
        for span in range(spans):
            mark(span, False)
            lay(span, False)
            keep(span)
            if span == 0:
                meet()

            @pl.when(section >= sections // 2)
            def _(span=span):
                hand_on(span)

        gather()
        load_weight.wait()
        for span in range(spans):
            scatter(span, later_sums)
            if span:
                finish(span - 1)
            pass_on(span)
            if span + 1 < spans:
                earlier(span + 1)

    def merge(i, _):
        for j in range(pieces):
            moved = jnp.dot(select_ref[i], fresh_ref[j], preferred_element_type=jnp.float32)
            kept_ref[i, :, columns(j)] = (kept_ref[i, :, columns(j)].astype(jnp.float32) + moved).astype(jnp.bfloat16)
        return 0

    @pl.when(section > 0)
    def _():
        lax.fori_loop(0, col_blocks, merge, 0)

    store = pltpu.make_async_copy(kept_ref, table_hbm, table_sem)
    store.start()
    finish(spans - 1)

    @pl.when(section < sections // 2)
    def _():
        for span in range(spans):
            hand_on(span)

    for span in range(spans):
        for j in range(pieces):
            support_copy(span, j).wait_send()
            for step in range(1, vertices):
                @pl.when(is_sent(step))
                def _(span=span, step=step, j=j):
                    part_copy(span, step, j).wait_send()

            @pl.when(at_end)
            def _(span=span, j=j):
                pass_copy(span, j).wait_send()
                detour_copy(span, j).wait_send()
                return_copy(span, j).wait_send()

            @pl.when(section < sections - 1)
            def _(span=span, j=j):
                row_copy(span, j).wait_send()

    store.wait()


def deliver(rows_hbm, table_hbm, rows_out, table_out, rows_ref, table_ref, in_sem, out_sem):
    chunks = in_sem.shape[0] - 1
    size = table_ref.shape[0] // chunks
    moves = []
    for i in range(chunks):
        here = pl.ds(i * size, size)
        moves.append((
            pltpu.make_async_copy(table_hbm.at[here], table_ref.at[here], in_sem.at[i]),
            pltpu.make_async_copy(table_ref.at[here], table_out.at[here], out_sem.at[i]),
        ))
    moves.append((
        pltpu.make_async_copy(rows_hbm, rows_ref, in_sem.at[chunks]),
        pltpu.make_async_copy(rows_ref, rows_out, out_sem.at[chunks]),
    ))
    for get, _ in moves:
        get.start()
    for get, put in moves:
        get.wait()
        put.start()
    for _, put in moves:
        put.wait()


def long_line(sizes, features, history, weights, tile_values, tile_rows, tile_cols, tile_counts, span_ids):
    sections, vertices, feats = sizes
    spans, span_rows = span_ids.shape
    owned, width = features.shape
    rows_whole = span_rows * vertices
    rows_all = spans * span_rows
    vmem = pl.BlockSpec(memory_space=pltpu.VMEM)
    smem = pl.BlockSpec(memory_space=pltpu.SMEM)
    anywhere = pl.BlockSpec(memory_space=pl.ANY)

    dense = pl.pallas_call(
        prepare,
        name="prepare",
        out_shape=jax.ShapeDtypeStruct((spans, rows_whole, owned), jnp.bfloat16),
        in_specs=[smem, smem, smem, vmem],
        out_specs=anywhere,
        scratch_shapes=[
            pltpu.VMEM((spans, rows_whole, owned), jnp.bfloat16),
            pltpu.SemaphoreType.DMA((spans,)),
        ],
        compiler_params=pltpu.CompilerParams(vmem_limit_bytes=VMEM_BYTES),
    )(tile_rows, tile_cols, tile_counts.reshape(1, spans), tile_values)

    rows_type = jax.ShapeDtypeStruct((spans, span_rows, width), jnp.bfloat16)
    table_type = jax.ShapeDtypeStruct((owned, width), jnp.bfloat16)
    block = pltpu.VMEM(rows_type.shape, jnp.bfloat16)
    halves = 2
    pair = pltpu.SemaphoreType.DMA((spans, halves))
    return pl.pallas_call(
        functools.partial(relay, sections, vertices, feats),
        name="relay",
        out_shape=(rows_type, table_type),
        in_specs=[anywhere, vmem, anywhere, anywhere, anywhere],
        out_specs=(vmem, anywhere),
        scratch_shapes=[
            pltpu.VMEM((min(2, spans), rows_whole, owned), jnp.bfloat16),
            pltpu.VMEM((spans, rows_whole, width), jnp.float32),
            pltpu.VMEM((spans, rows_whole, rows_all), jnp.bfloat16),
            pltpu.VMEM(weights.shape[1:], weights.dtype),
            pltpu.VMEM((owned, width), jnp.bfloat16),
            pltpu.VMEM((owned, width), jnp.bfloat16),
            pltpu.VMEM((owned, rows_all), jnp.bfloat16),
            pltpu.VMEM((rows_all, width), jnp.bfloat16),
            pltpu.VMEM((rows_all, width), jnp.bfloat16),
            block,
            pltpu.VMEM((spans, rows_whole, width), jnp.bfloat16),
            pltpu.VMEM((spans, vertices - 1, span_rows, width), jnp.bfloat16),
            block, block, block, block,
            pltpu.SemaphoreType.DMA((spans + 3,)),
            pltpu.SemaphoreType.DMA,
            pair, pair,
            pltpu.SemaphoreType.DMA((spans, vertices - 1, halves)),
            pltpu.SemaphoreType.DMA((spans, vertices - 1, halves)),
            pair, pair, pair, pair,
        ],
        compiler_params=pltpu.CompilerParams(
            vmem_limit_bytes=VMEM_BYTES, collective_id=0, has_side_effects=True
        ),
    )(dense, span_ids, weights[0], history[0], features)


def short_line(sizes, features, history, weights, tile_values, tile_rows, tile_cols, tile_counts, span_ids):
    sections, vertices, feats = sizes
    spans, span_rows = span_ids.shape
    slots, side = tile_values.shape[1:3]
    owned, width = features.shape
    rows_whole = span_rows * vertices
    rows_all = spans * span_rows
    pieces = 2
    part = width // pieces
    vmem = pl.BlockSpec(memory_space=pltpu.VMEM)
    smem = pl.BlockSpec(memory_space=pltpu.SMEM)
    anywhere = pl.BlockSpec(memory_space=pl.ANY)
    block = pltpu.VMEM((spans, pieces, span_rows, part), jnp.bfloat16)
    pair = pltpu.SemaphoreType.DMA((spans, pieces))
    triple = pltpu.SemaphoreType.DMA((spans, vertices - 1, pieces))
    table = history[0].reshape(owned // side, side, width)
    layer_rows, table_new = pl.pallas_call(
        functools.partial(stream, sections, vertices, feats),
        name="stream",
        out_shape=(
            jax.ShapeDtypeStruct((spans, span_rows, width), jnp.bfloat16),
            jax.ShapeDtypeStruct(table.shape, jnp.bfloat16),
        ),
        in_specs=[smem, smem, smem, vmem, anywhere, anywhere, anywhere, anywhere],
        out_specs=(vmem, anywhere),
        scratch_shapes=[
            pltpu.VMEM(tile_values.shape, jnp.bfloat16),
            pltpu.VMEM((rows_whole, slots * side), jnp.bfloat16),
            pltpu.VMEM((slots * side, width), jnp.bfloat16),
            pltpu.VMEM((slots * side, rows_all), jnp.bfloat16),
            pltpu.VMEM((spans, pieces, rows_whole, part), jnp.float32),
            pltpu.VMEM((spans, rows_whole, rows_all), jnp.bfloat16),
            pltpu.VMEM(weights.shape[1:], weights.dtype),
            pltpu.VMEM(table.shape, jnp.bfloat16),
            pltpu.VMEM(table.shape, jnp.bfloat16),
            pltpu.VMEM((owned // side, side, rows_all), jnp.bfloat16),
            pltpu.VMEM((rows_all, width), jnp.bfloat16),
            pltpu.VMEM((pieces, rows_all, part), jnp.bfloat16),
            pltpu.VMEM((spans, pieces, rows_whole, part), jnp.bfloat16),
            pltpu.VMEM((spans, vertices - 1, pieces, span_rows, part), jnp.bfloat16),
            block, block, block, block, block,
            pltpu.SemaphoreType.DMA((spans + 3,)),
            pltpu.SemaphoreType.DMA,
            pair, pair, triple, triple, pair, pair, pair, pair, pair, pair, pair,
        ],
        compiler_params=pltpu.CompilerParams(
            vmem_limit_bytes=VMEM_BYTES, collective_id=0, has_side_effects=True
        ),
    )(tile_rows, tile_cols, tile_counts.reshape(1, spans), span_ids, tile_values, weights[0], table,
      features.reshape(table.shape))
    return layer_rows, table_new.reshape(owned, width)


def shards(sizes, features, history, weights, tile_values, tile_rows, tile_cols, tile_counts, span_ids):
    spans, span_rows = span_ids.shape
    owned, width = features.shape
    rows_type = jax.ShapeDtypeStruct((spans, span_rows, width), jnp.bfloat16)
    table_type = jax.ShapeDtypeStruct((owned, width), jnp.bfloat16)
    anywhere = pl.BlockSpec(memory_space=pl.ANY)
    layers = short_line if sizes[0] == sizes[1] == LINE else long_line
    layer_rows, table_new = layers(
        sizes, features, history, weights, tile_values, tile_rows, tile_cols, tile_counts, span_ids
    )

    chunks = 8
    layer_rows, table_new = pl.pallas_call(
        deliver,
        name="deliver",
        out_shape=(rows_type, table_type),
        in_specs=[anywhere, anywhere],
        out_specs=(anywhere, anywhere),
        scratch_shapes=[
            pltpu.VMEM(rows_type.shape, jnp.bfloat16),
            pltpu.VMEM(table_type.shape, jnp.bfloat16),
            pltpu.SemaphoreType.DMA((chunks + 1,)),
            pltpu.SemaphoreType.DMA((chunks + 1,)),
        ],
        compiler_params=pltpu.CompilerParams(vmem_limit_bytes=VMEM_BYTES),
    )(layer_rows, table_new)
    return (layer_rows[None], table_new[None])


def solution(mesh):
    placed = (
        P("vertex", "feat"),
        P("section", "vertex", "feat"),
        P("section", None, "feat"),
        P(None, "vertex", None, None),
        P(None, "vertex"),
        P(None, "vertex"),
        P(None, "vertex"),
        P(None, "vertex"),
    )
    sizes = (mesh.shape["section"], mesh.shape["vertex"], mesh.shape["feat"])
    return jax.shard_map(
        functools.partial(shards, sizes),
        mesh=mesh,
        in_specs=placed,
        out_specs=(P("section", None, "vertex", "feat"), P("section", "vertex", "feat")),
        check_vma=False,
    )
```

```python
import functools

import jax
import jax.numpy as jnp
from jax import lax
from jax.experimental import pallas as pl
from jax.experimental.pallas import tpu as pltpu
from jax.sharding import PartitionSpec as P

RESIDUAL_SHARE = 0.2
BETA_SCALE = 0.5
MESH = pl.DeviceIdType.MESH
VMEM_BYTES = 60_000 * 1024


def chosen(ids_row, rows, first=0):
    shape = (rows, ids_row.shape[1])
    return (lax.broadcasted_iota(jnp.int32, shape, 0) + first == ids_row).astype(jnp.float32)


def prepare(rows_ref, cols_ref, counts_ref, tiles_ref, dense_hbm, dense, dense_sem):
    spans, _, side, _ = tiles_ref.shape
    copies = []
    for span in range(spans):
        dense[span] = jnp.zeros(dense.shape[1:], dense.dtype)

        def place(t, _, span=span):
            row = pl.multiple_of(rows_ref[span, t] * side, side)
            col = pl.multiple_of(cols_ref[span, t] * side, side)
            dense[span, pl.ds(row, side), pl.ds(col, side)] = tiles_ref[span, t]
            return 0

        lax.fori_loop(0, counts_ref[0, span], place, 0)
        copies.append(pltpu.make_async_copy(dense.at[span], dense_hbm.at[span], dense_sem.at[span]))
        copies[-1].start()
    for copy in copies:
        copy.wait()


def relay(
    sections, vertices, feats,
    dense_hbm, ids_ref, weight_hbm, kept_hbm, features_hbm, out_ref, table_hbm,
    dense, base_ref, picks_ref, weight_ref, kept_ref, features_ref, select_ref, initial_ref, fresh_ref,
    arrived, partial, parts, passing, support, other, result,
    load_sem, table_sem, x_send, x_recv, p_send, p_recv, h_send, h_recv, s_send, s_recv,
):
    section = lax.axis_index("section")
    vertex = lax.axis_index("vertex")
    feat = lax.axis_index("feat")
    spans, span_rows, width = arrived.shape
    last = vertices - 1
    partner = lax.rem(feat + 1, feats)
    beta = jnp.log(BETA_SCALE / (section + 1).astype(jnp.float32) + 1.0)
    halves = 2
    piece = span_rows // halves
    relayed = vertices > 3

    rows_whole = dense.shape[1]
    owned = kept_ref.shape[0]
    group = min(512, rows_whole)
    chunk = min(256, owned)

    def load_dense(span):
        return pltpu.make_async_copy(dense_hbm.at[span], dense.at[span % 2], load_sem.at[span])

    load_weight = pltpu.make_async_copy(weight_hbm, weight_ref, load_sem.at[spans])
    load_kept = pltpu.make_async_copy(kept_hbm, kept_ref, load_sem.at[spans + 1])
    load_features = pltpu.make_async_copy(features_hbm, features_ref, load_sem.at[spans + 2])
    load_kept.start()
    load_features.start()
    for span in range(min(2, spans)):
        load_dense(span).start()
    load_weight.start()

    barrier = pltpu.get_barrier_semaphore()
    for step in range(1, vertices):
        peer = lax.rem(vertex + step, vertices)
        pl.semaphore_signal(barrier, inc=1, device_id=(section, peer, feat), device_id_type=MESH)
    pl.semaphore_signal(barrier, inc=1, device_id=(section, vertex, partner), device_id_type=MESH)
    for step in (1, sections - 1):
        peer = lax.rem(section + step, sections)
        pl.semaphore_signal(barrier, inc=1, device_id=(peer, vertex, feat), device_id_type=MESH)
    if relayed:
        @pl.when(vertex == 0)
        def _():
            parts[:, 0] = jnp.zeros((spans, span_rows, width), jnp.bfloat16)

        @pl.when(vertex == last)
        def _():
            parts[:, last - 1] = jnp.zeros((spans, span_rows, width), jnp.bfloat16)

    pl.semaphore_wait(barrier, vertices - 1 + 1 + 2)

    def half_of(half):
        return slice(half * piece, (half + 1) * piece)

    def row_copy(span, half):
        rows = pl.ds(half * piece, piece)
        return pltpu.make_async_remote_copy(
            src_ref=result.at[span, rows], dst_ref=arrived.at[span, rows],
            send_sem=x_send.at[span, half], recv_sem=x_recv.at[span, half],
            device_id=(lax.rem(section + 1, sections), vertex, feat), device_id_type=MESH,
        )

    def chunk_rows(peer, half):
        return pl.ds(pl.multiple_of(peer * span_rows + half * piece, piece), piece)

    def part_copy(span, step, half):
        peer = lax.rem(vertex + step, vertices)
        return pltpu.make_async_remote_copy(
            src_ref=partial.at[span, chunk_rows(peer, half)],
            dst_ref=parts.at[span, step - 1, pl.ds(half * piece, piece)],
            send_sem=p_send.at[span, step - 1, half], recv_sem=p_recv.at[span, step - 1, half],
            device_id=(section, peer, feat), device_id_type=MESH,
        )

    def pass_copy(span, half):
        far = jnp.where(vertex == 0, last, 0)
        near = jnp.where(vertex == 0, 1, last - 1)
        return pltpu.make_async_remote_copy(
            src_ref=partial.at[span, chunk_rows(far, half)],
            dst_ref=passing.at[span, pl.ds(half * piece, piece)],
            send_sem=h_send.at[span, half], recv_sem=h_recv.at[span, half],
            device_id=(section, near, feat), device_id_type=MESH,
        )

    def support_copy(span, half):
        rows = pl.ds(half * piece, piece)
        return pltpu.make_async_remote_copy(
            src_ref=support.at[span, rows], dst_ref=other.at[span, rows],
            send_sem=s_send.at[span, half], recv_sem=s_recv.at[span, half],
            device_id=(section, vertex, partner), device_id_type=MESH,
        )

    at_end = (vertex == 0) | (vertex == last)

    def is_direct(step):
        if not relayed:
            return vertex >= 0
        peer = lax.rem(vertex + step, vertices)
        ends = ((vertex == 0) & (peer == last)) | ((vertex == last) & (peer == 0))
        inner = ((vertex == 1) & (peer == last)) | ((vertex == last - 1) & (peer == 0))
        return jnp.logical_not(ends | inner)

    def is_sent(step):
        if not relayed:
            return vertex >= 0
        peer = lax.rem(vertex + step, vertices)
        return jnp.logical_not(((vertex == 0) & (peer == last)) | ((vertex == last) & (peer == 0)))

    def is_received(step):
        if not relayed:
            return vertex >= 0
        source = lax.rem(vertex + vertices - step, vertices)
        return jnp.logical_not(((vertex == 0) & (source == last)) | ((vertex == last) & (source == 0)))

    def local(span, leading):
        mine = slice(span * span_rows, (span + 1) * span_rows)
        used = (span + 1) * span_rows

        def clear(i, _):
            first = pl.multiple_of(i * chunk, chunk)
            here = pl.ds(first, chunk)
            hot = chosen(ids_ref[span : span + 1, :], chunk, first)
            select_ref[here, mine] = hot.astype(jnp.bfloat16)
            taken = jnp.max(hot, axis=1, keepdims=True) > 0.5
            filler = features_ref[here, :].astype(jnp.float32) if leading else 0.0
            kept_ref[here, :] = jnp.where(taken, filler, kept_ref[here, :].astype(jnp.float32)).astype(jnp.bfloat16)
            return 0

        lax.fori_loop(0, owned // chunk, clear, 0)
        load_dense(span).wait()

        def multiply(i, _):
            here = pl.ds(pl.multiple_of(i * group, group), group)
            block = dense[span % 2, here, :]
            product = jnp.dot(block, kept_ref[...], preferred_element_type=jnp.float32)
            if leading:
                partial[span, here, :] = product.astype(jnp.bfloat16)
            else:
                base_ref[span, here, :] = product
                picks_ref[span, here, :used] = jnp.dot(
                    block, select_ref[:, :used], preferred_element_type=jnp.float32
                ).astype(jnp.bfloat16)
            return 0

        lax.fori_loop(0, rows_whole // group, multiply, 0)
        if span + 2 < spans:
            load_dense(span + 2).start()

    def gather():
        initial_ref[...] = lax.dot_general(
            select_ref[...], features_ref[...], (((0,), (0,)), ((), ())), preferred_element_type=jnp.float32
        ).astype(jnp.bfloat16)

    def earlier(span):
        used = span * span_rows

        def add(i, _):
            here = pl.ds(pl.multiple_of(i * group, group), group)
            base_ref[span, here, :] += jnp.dot(
                picks_ref[span, here, :used], fresh_ref[:used, :], preferred_element_type=jnp.float32
            )
            return 0

        lax.fori_loop(0, rows_whole // group, add, 0)

    def scatter(span):
        mine = slice(span * span_rows, (span + 1) * span_rows)
        @pl.when(section > 0)
        def _():
            for half in range(halves):
                row_copy(span, half).wait_recv()
            fresh_ref[mine, :] = arrived[span]


        def compute(peer):
            here = pl.ds(pl.multiple_of(peer * span_rows, span_rows), span_rows)
            total = base_ref[span, here, :] + jnp.dot(
                picks_ref[span, here, mine], fresh_ref[mine, :], preferred_element_type=jnp.float32
            )
            partial[span, here, :] = total.astype(jnp.bfloat16)

        if relayed:
            @pl.when(at_end & (section > 0))
            def _():
                compute(jnp.where(vertex == 0, last, 0))

            @pl.when(at_end)
            def _():
                for half in range(halves):
                    pass_copy(span, half).start()

        for step in range(1, vertices):
            @pl.when(is_sent(step) & (section > 0))
            def _(step=step):
                compute(lax.rem(vertex + step, vertices))

            @pl.when(is_direct(step))
            def _(step=step):
                part_copy(span, step, 0).start()

        for half in range(1, halves):
            for step in range(1, vertices):
                @pl.when(is_direct(step))
                def _(step=step, half=half):
                    part_copy(span, step, half).start()

        @pl.when(section > 0)
        def _():
            compute(vertex)

    def pass_on(span):
        if relayed:
            for who, step in ((1, last - 1), (last - 1, 2)):
                @pl.when(vertex == who)
                def _(who=who, step=step):
                    far = last if who == 1 else 0
                    for half in range(halves):
                        pass_copy(span, half).wait_recv()
                        here = pl.ds(far * span_rows + half * piece, piece)
                        partial[span, here, :] = (
                            partial[span, here, :].astype(jnp.float32)
                            + passing[span, half_of(half), :].astype(jnp.float32)
                        ).astype(jnp.bfloat16)
                        part_copy(span, step, half).start()

    def finish(span, half):
        total = partial[span, chunk_rows(vertex, half), :].astype(jnp.float32)
        for step in range(1, vertices):
            @pl.when(is_received(step))
            def _(step=step):
                part_copy(span, step, half).wait_recv()

        for step in range(1, vertices):
            total += parts[span, step - 1, half_of(half), :].astype(jnp.float32)
        mixed = (
            (1.0 - RESIDUAL_SHARE) * total
            + RESIDUAL_SHARE * initial_ref[pl.ds(span * span_rows + half * piece, piece), :].astype(jnp.float32)
        ).astype(jnp.bfloat16)
        support[span, half_of(half), :] = mixed
        support_copy(span, half).start()
        mine = pl.ds(pl.multiple_of(feat * width, width), width)
        theirs = pl.ds(pl.multiple_of(partner * width, width), width)
        projected = jnp.dot(mixed, weight_ref[mine, :], preferred_element_type=jnp.float32)
        support_copy(span, half).wait_recv()
        projected += jnp.dot(other[span, half_of(half), :], weight_ref[theirs, :], preferred_element_type=jnp.float32)
        rows = jnp.maximum((1.0 - beta) * mixed.astype(jnp.float32) + beta * projected, 0.0).astype(jnp.bfloat16)
        result[span, half_of(half), :] = rows
        out_ref[span, half_of(half), :] = rows

        @pl.when(section < sections - 1)
        def _():
            row_copy(span, half).start()

    def finish_all(span):
        for half in range(halves):
            finish(span, half)

    load_kept.wait()
    load_features.wait()

    @pl.when(section == 0)
    def _():
        for span in range(spans):
            local(span, True)
            scatter(span)
            if span:
                pass_on(span - 1)
        gather()
        load_weight.wait()
        for span in range(spans - 1):
            finish_all(span)
            if span == 0:
                pass_on(spans - 1)

    @pl.when(section > 0)
    def _():
        for span in range(spans):
            local(span, False)
        gather()
        load_weight.wait()
        for span in range(spans):
            scatter(span)
            pass_on(span)
            if span:
                finish_all(span - 1)
            if span + 1 < spans:
                earlier(span + 1)

    def merge(i, _):
        here = pl.ds(pl.multiple_of(i * chunk, chunk), chunk)
        moved = jnp.dot(select_ref[here, :], fresh_ref[...], preferred_element_type=jnp.float32)
        kept_ref[here, :] = (kept_ref[here, :].astype(jnp.float32) + moved).astype(jnp.bfloat16)
        return 0

    @pl.when(section > 0)
    def _():
        lax.fori_loop(0, owned // chunk, merge, 0)

    store = pltpu.make_async_copy(kept_ref, table_hbm, table_sem)
    store.start()
    finish_all(spans - 1)

    for span in range(spans):
        for half in range(halves):
            support_copy(span, half).wait_send()
            for step in range(1, vertices):
                @pl.when(is_sent(step))
                def _(span=span, step=step, half=half):
                    part_copy(span, step, half).wait_send()

            if relayed:
                @pl.when(at_end)
                def _(span=span, half=half):
                    pass_copy(span, half).wait_send()

            @pl.when(section < sections - 1)
            def _(span=span, half=half):
                row_copy(span, half).wait_send()

    store.wait()

LINE = 4


def write(rows_ref, table_ref, rows_out, table_out, sem):
    chunks = sem.shape[0] - 1
    size = table_ref.shape[0] // chunks
    moves = [pltpu.make_async_copy(rows_ref, rows_out, sem.at[chunks])]
    for i in range(chunks):
        here = pl.ds(i * size, size)
        moves.append(pltpu.make_async_copy(table_ref.at[here], table_out.at[here], sem.at[i]))
    for move in moves:
        move.start()
    for move in moves:
        move.wait()


def stream(
    sections, vertices, feats,
    rows_ref, cols_ref, counts_ref, ids_ref, tiles_hbm, weight_hbm, kept_hbm, features_hbm, out_ref, kept_ref,
    tiles, left, right, right_select, base_ref, picks_ref, weight_ref, features_ref, select_ref, initial_ref,
    fresh_ref, partial, parts, passing, transit, support, other, result,
    load_sem, x_send, x_recv, p_send, p_recv, h_send, h_recv, s_send, s_recv, d_send, d_recv, t_send,
):
    section = lax.axis_index("section")
    vertex = lax.axis_index("vertex")
    feat = lax.axis_index("feat")
    spans, span_rows, width = result.shape
    pieces = x_send.shape[1]
    part = width // pieces
    wide = min(256, width)
    slots, side = tiles.shape[1:3]
    row_blocks = left.shape[0] // side
    rows_all = spans * span_rows
    last = vertices - 1
    partner = lax.rem(feat + 1, feats)
    beside = lax.rem(section + sections // 2, sections)
    opposite = lax.rem(vertex + last - 1, vertices)
    beta = jnp.log(BETA_SCALE / (section + 1).astype(jnp.float32) + 1.0)
    col_blocks = kept_ref.shape[0]

    def load_tiles(span):
        return pltpu.make_async_copy(tiles_hbm.at[span], tiles.at[span], load_sem.at[span])

    load_weight = pltpu.make_async_copy(weight_hbm, weight_ref, load_sem.at[spans])
    load_kept = pltpu.make_async_copy(kept_hbm, kept_ref, load_sem.at[spans + 1])
    load_features = pltpu.make_async_copy(features_hbm, features_ref, load_sem.at[spans + 2])
    load_kept.start()
    load_features.start()
    for span in range(spans):
        load_tiles(span).start()
    load_weight.start()

    barrier = pltpu.get_barrier_semaphore()
    for step in range(1, vertices):
        peer = lax.rem(vertex + step, vertices)
        pl.semaphore_signal(barrier, inc=1, device_id=(section, peer, feat), device_id_type=MESH)
    pl.semaphore_signal(barrier, inc=1, device_id=(section, vertex, partner), device_id_type=MESH)
    for step in (1, sections - 1):
        peer = lax.rem(section + step, sections)
        pl.semaphore_signal(barrier, inc=1, device_id=(peer, vertex, feat), device_id_type=MESH)
    for peer in (vertex, opposite):
        pl.semaphore_signal(barrier, inc=1, device_id=(beside, peer, feat), device_id_type=MESH)

    def meet():
        pl.semaphore_wait(barrier, vertices - 1 + 1 + 2 + 2)

    at_end = (vertex == 0) | (vertex == last)

    @pl.when(vertex == 0)
    def _():
        parts[:, 0] = jnp.zeros((spans, span_rows, width), jnp.bfloat16)

    @pl.when(vertex == last)
    def _():
        parts[:, last - 1] = jnp.zeros((spans, span_rows, width), jnp.bfloat16)

    def columns(j):
        return slice(j * part, (j + 1) * part)

    def lanes(j):
        return pl.ds(j * part, part)

    def span_of(span):
        return slice(span * span_rows, (span + 1) * span_rows)

    def row_copy(span, j):
        return pltpu.make_async_remote_copy(
            src_ref=result.at[span, :, lanes(j)],
            dst_ref=fresh_ref.at[pl.ds(span * span_rows, span_rows), lanes(j)],
            send_sem=x_send.at[span, j], recv_sem=x_recv.at[span, j],
            device_id=(lax.rem(section + 1, sections), vertex, feat), device_id_type=MESH,
        )

    def rows_of(peer):
        return pl.ds(pl.multiple_of(peer * span_rows, span_rows), span_rows)

    def part_copy(span, step, j):
        peer = lax.rem(vertex + step, vertices)
        return pltpu.make_async_remote_copy(
            src_ref=partial.at[span, rows_of(peer), lanes(j)], dst_ref=parts.at[span, step - 1, :, lanes(j)],
            send_sem=p_send.at[span, step - 1, j], recv_sem=p_recv.at[span, step - 1, j],
            device_id=(section, peer, feat), device_id_type=MESH,
        )

    def pass_copy(span, j):
        far = jnp.where(vertex == 0, last, 0)
        near = jnp.where(vertex == 0, 1, last - 1)
        return pltpu.make_async_remote_copy(
            src_ref=partial.at[span, rows_of(far), lanes(j)], dst_ref=passing.at[span, :, lanes(j)],
            send_sem=h_send.at[span, j], recv_sem=h_recv.at[span, j],
            device_id=(section, near, feat), device_id_type=MESH,
        )

    def detour_copy(span, j):
        return pltpu.make_async_remote_copy(
            src_ref=partial.at[span, rows_of(opposite), lanes(j)], dst_ref=transit.at[span, :, lanes(j)],
            send_sem=d_send.at[span, j], recv_sem=d_recv.at[span, j],
            device_id=(beside, vertex, feat), device_id_type=MESH,
        )

    def return_copy(span, j):
        return pltpu.make_async_remote_copy(
            src_ref=transit.at[span, :, lanes(j)], dst_ref=parts.at[span, last - 2, :, lanes(j)],
            send_sem=t_send.at[span, j], recv_sem=p_recv.at[span, last - 2, j],
            device_id=(beside, opposite, feat), device_id_type=MESH,
        )

    def support_copy(span, j):
        return pltpu.make_async_remote_copy(
            src_ref=support.at[span, :, lanes(j)], dst_ref=other.at[span, :, lanes(j)],
            send_sem=s_send.at[span, j], recv_sem=s_recv.at[span, j],
            device_id=(section, vertex, partner), device_id_type=MESH,
        )

    def ends_meet(here, there):
        return ((here == 0) & (there == last)) | ((here == last) & (there == 0))

    def is_sent(step):
        far = ends_meet(vertex, lax.rem(vertex + step, vertices))
        return jnp.logical_not(far | at_end) if step == last - 1 else jnp.logical_not(far)

    def is_received(step):
        return jnp.logical_not(ends_meet(lax.rem(vertex + vertices - step, vertices), vertex))

    def choose():
        def one_hot(i, _):
            for span in range(spans):
                hot = chosen(ids_ref[span : span + 1, :], side, i * side)
                select_ref[i, :, span_of(span)] = hot.astype(jnp.bfloat16)
            return 0

        lax.fori_loop(0, col_blocks, one_hot, 0)

    def mark(span, leading):
        ones = jnp.ones((span_rows, side), jnp.bfloat16)

        def clear(i, _):
            taken = jnp.dot(select_ref[i, :, span_of(span)], ones, preferred_element_type=jnp.float32)
            here = taken.astype(jnp.bfloat16)
            rest = (1.0 - taken).astype(jnp.bfloat16)
            for first in range(0, width, side):
                group = slice(first, first + side)
                row = kept_ref[i, :, group] * rest
                kept_ref[i, :, group] = row + features_ref[i, :, group] * here if leading else row
            return 0

        lax.fori_loop(0, col_blocks, clear, 0)

    def lay(span, leading):
        used = (span + 1) * span_rows
        load_tiles(span).wait()
        lives = jnp.full((side, side), counts_ref[0, span], jnp.int32)

        def place(t, _):
            col = cols_ref[span, t]
            here = pl.ds(pl.multiple_of(t * side, side), side)
            tile = tiles[span, t].astype(jnp.float32)
            rows = jnp.where(lives > t, jnp.full(tile.shape, rows_ref[span, t], jnp.int32), row_blocks)
            for block in range(row_blocks):
                left[block * side : (block + 1) * side, here] = jnp.where(rows == block, tile, 0.0).astype(left.dtype)
            right[here, :] = kept_ref[col]
            if not leading:
                right_select[here, :] = select_ref[col]
            return 0

        lax.fori_loop(0, slots, place, 0)

    def gather():
        initial_ref[...] = lax.dot_general(
            select_ref[...].reshape(col_blocks * side, rows_all),
            features_ref[...].reshape(col_blocks * side, width),
            (((0,), (0,)), ((), ())),
            preferred_element_type=jnp.float32,
        ).astype(jnp.bfloat16)

    def groups():
        return [slice(first, first + wide) for first in range(0, width, wide)]

    def product(group):
        return jnp.dot(left[...], right[:, group], preferred_element_type=jnp.float32)

    def first_sums(span, j):
        if j * part % wide == 0:
            group = slice(j * part, j * part + wide)
            partial[span, :, group] = product(group).astype(jnp.bfloat16)

    def later_sums(span, j):
        row_copy(span, j).wait_recv()
        partial[span, :, columns(j)] = (
            base_ref[span, :, columns(j)]
            + jnp.dot(
                picks_ref[span, :, span_of(span)], fresh_ref[span_of(span), columns(j)],
                preferred_element_type=jnp.float32,
            )
        ).astype(jnp.bfloat16)

    def scatter(span, sums):
        for j in range(pieces):
            sums(span, j)

            @pl.when(at_end)
            def _(j=j):
                pass_copy(span, j).start()
                detour_copy(span, j).start()

            @pl.when(jnp.logical_not(at_end))
            def _(j=j):
                for step in (1, last):
                    part_copy(span, step, j).start()

        for j in range(pieces):
            for step in (1, last):
                @pl.when(at_end & is_sent(step))
                def _(step=step, j=j):
                    part_copy(span, step, j).start()

    def pass_on(span):
        for who, step in ((1, last - 1), (last - 1, 2)):
            @pl.when(vertex == who)
            def _(who=who, step=step):
                far = last if who == 1 else 0
                here = pl.ds(far * span_rows, span_rows)
                for j in range(pieces):
                    pass_copy(span, j).wait_recv()
                    partial[span, here, columns(j)] = (
                        partial[span, here, columns(j)].astype(jnp.float32)
                        + passing[span, :, columns(j)].astype(jnp.float32)
                    ).astype(jnp.bfloat16)
                    part_copy(span, step, j).start()

    def hand_on(span):
        @pl.when(at_end)
        def _():
            for j in range(pieces):
                detour_copy(span, j).wait_recv()
                return_copy(span, j).start()

    def keep(span):
        used = (span + 1) * span_rows
        for group in groups():
            base_ref[span, :, group] = product(group)
        picks_ref[span, :, :used] = jnp.dot(
            left[...], right_select[:, :used], preferred_element_type=jnp.float32
        ).astype(jnp.bfloat16)

    def earlier(span):
        used = span * span_rows
        for group in groups():
            base_ref[span, :, group] += jnp.dot(
                picks_ref[span, :, :used], fresh_ref[:used, group], preferred_element_type=jnp.float32
            )

    def weight_rows(which):
        return pl.ds(pl.multiple_of(which * width, width), width)

    def finish(span):
        for j in range(pieces):
            for step in range(1, vertices):
                @pl.when(is_received(step))
                def _(step=step, j=j):
                    part_copy(span, step, j).wait_recv()

            total = partial[span, rows_of(vertex), columns(j)].astype(jnp.float32)
            for step in range(1, vertices):
                total += parts[span, step - 1, :, columns(j)].astype(jnp.float32)
            support[span, :, columns(j)] = (
                (1.0 - RESIDUAL_SHARE) * total
                + RESIDUAL_SHARE * initial_ref[span_of(span), columns(j)].astype(jnp.float32)
            ).astype(jnp.bfloat16)
            support_copy(span, j).start()

        projected = [
            jnp.dot(support[span], weight_ref[weight_rows(feat), group], preferred_element_type=jnp.float32)
            for group in groups()
        ]
        for j in range(pieces):
            support_copy(span, j).wait_recv()
        for k, group in enumerate(groups()):
            whole = projected[k] + jnp.dot(
                other[span], weight_ref[weight_rows(partner), group], preferred_element_type=jnp.float32
            )
            rows = jnp.maximum(
                (1.0 - beta) * support[span, :, group].astype(jnp.float32) + beta * whole, 0.0
            ).astype(jnp.bfloat16)
            result[span, :, group] = rows

            @pl.when(section < sections - 1)
            def _(group=group):
                for j in range(group.start // part, group.stop // part):
                    row_copy(span, j).start()

            out_ref[span, :, group] = rows

    choose()
    load_kept.wait()
    load_features.wait()

    @pl.when(section == 0)
    def _():
        for span in range(spans):
            mark(span, True)
            lay(span, True)
            if span == 0:
                meet()
            scatter(span, first_sums)
            if span:
                pass_on(span - 1)
        gather()
        load_weight.wait()
        for span in range(spans - 1):
            finish(span)
            if span == spans - 2:
                pass_on(spans - 1)

    @pl.when(section > 0)
    def _():
        for span in range(spans):
            mark(span, False)
            lay(span, False)
            keep(span)
            if span == 0:
                meet()

            @pl.when(section >= sections // 2)
            def _(span=span):
                hand_on(span)

        gather()
        load_weight.wait()
        for span in range(spans):
            scatter(span, later_sums)
            if span:
                finish(span - 1)
            pass_on(span)
            if span + 1 < spans:
                earlier(span + 1)

    def merge(i, _):
        for group in groups():
            moved = jnp.dot(select_ref[i], fresh_ref[:, group], preferred_element_type=jnp.float32)
            kept_ref[i, :, group] = (kept_ref[i, :, group].astype(jnp.float32) + moved).astype(jnp.bfloat16)
        return 0

    @pl.when(section > 0)
    def _():
        lax.fori_loop(0, col_blocks, merge, 0)

    finish(spans - 1)

    @pl.when(section < sections // 2)
    def _():
        for span in range(spans):
            hand_on(span)

    for span in range(spans):
        for j in range(pieces):
            support_copy(span, j).wait_send()
            for step in range(1, vertices):
                @pl.when(is_sent(step))
                def _(span=span, step=step, j=j):
                    part_copy(span, step, j).wait_send()

            @pl.when(at_end)
            def _(span=span, j=j):
                pass_copy(span, j).wait_send()
                detour_copy(span, j).wait_send()
                return_copy(span, j).wait_send()

            @pl.when(section < sections - 1)
            def _(span=span, j=j):
                row_copy(span, j).wait_send()


def deliver(rows_hbm, table_hbm, rows_out, table_out, rows_ref, table_ref, in_sem, out_sem):
    chunks = in_sem.shape[0] - 1
    size = table_ref.shape[0] // chunks
    moves = []
    for i in range(chunks):
        here = pl.ds(i * size, size)
        moves.append((
            pltpu.make_async_copy(table_hbm.at[here], table_ref.at[here], in_sem.at[i]),
            pltpu.make_async_copy(table_ref.at[here], table_out.at[here], out_sem.at[i]),
        ))
    moves.append((
        pltpu.make_async_copy(rows_hbm, rows_ref, in_sem.at[chunks]),
        pltpu.make_async_copy(rows_ref, rows_out, out_sem.at[chunks]),
    ))
    for get, _ in moves:
        get.start()
    for get, put in moves:
        get.wait()
        put.start()
    for _, put in moves:
        put.wait()


def long_line(sizes, features, history, weights, tile_values, tile_rows, tile_cols, tile_counts, span_ids):
    sections, vertices, feats = sizes
    spans, span_rows = span_ids.shape
    owned, width = features.shape
    rows_whole = span_rows * vertices
    rows_all = spans * span_rows
    vmem = pl.BlockSpec(memory_space=pltpu.VMEM)
    smem = pl.BlockSpec(memory_space=pltpu.SMEM)
    anywhere = pl.BlockSpec(memory_space=pl.ANY)

    dense = pl.pallas_call(
        prepare,
        name="prepare",
        out_shape=jax.ShapeDtypeStruct((spans, rows_whole, owned), jnp.bfloat16),
        in_specs=[smem, smem, smem, vmem],
        out_specs=anywhere,
        scratch_shapes=[
            pltpu.VMEM((spans, rows_whole, owned), jnp.bfloat16),
            pltpu.SemaphoreType.DMA((spans,)),
        ],
        compiler_params=pltpu.CompilerParams(vmem_limit_bytes=VMEM_BYTES),
    )(tile_rows, tile_cols, tile_counts.reshape(1, spans), tile_values)

    rows_type = jax.ShapeDtypeStruct((spans, span_rows, width), jnp.bfloat16)
    table_type = jax.ShapeDtypeStruct((owned, width), jnp.bfloat16)
    block = pltpu.VMEM(rows_type.shape, jnp.bfloat16)
    halves = 2
    pair = pltpu.SemaphoreType.DMA((spans, halves))
    layer_rows, table_new = pl.pallas_call(
        functools.partial(relay, sections, vertices, feats),
        name="relay",
        out_shape=(rows_type, table_type),
        in_specs=[anywhere, vmem, anywhere, anywhere, anywhere],
        out_specs=(vmem, anywhere),
        scratch_shapes=[
            pltpu.VMEM((min(2, spans), rows_whole, owned), jnp.bfloat16),
            pltpu.VMEM((spans, rows_whole, width), jnp.float32),
            pltpu.VMEM((spans, rows_whole, rows_all), jnp.bfloat16),
            pltpu.VMEM(weights.shape[1:], weights.dtype),
            pltpu.VMEM((owned, width), jnp.bfloat16),
            pltpu.VMEM((owned, width), jnp.bfloat16),
            pltpu.VMEM((owned, rows_all), jnp.bfloat16),
            pltpu.VMEM((rows_all, width), jnp.bfloat16),
            pltpu.VMEM((rows_all, width), jnp.bfloat16),
            block,
            pltpu.VMEM((spans, rows_whole, width), jnp.bfloat16),
            pltpu.VMEM((spans, vertices - 1, span_rows, width), jnp.bfloat16),
            block, block, block, block,
            pltpu.SemaphoreType.DMA((spans + 3,)),
            pltpu.SemaphoreType.DMA,
            pair, pair,
            pltpu.SemaphoreType.DMA((spans, vertices - 1, halves)),
            pltpu.SemaphoreType.DMA((spans, vertices - 1, halves)),
            pair, pair, pair, pair,
        ],
        compiler_params=pltpu.CompilerParams(
            vmem_limit_bytes=VMEM_BYTES, collective_id=0, has_side_effects=True
        ),
    )(dense, span_ids, weights[0], history[0], features)

    table_type = jax.ShapeDtypeStruct((owned, width), jnp.bfloat16)
    chunks = 8
    return pl.pallas_call(
        deliver,
        name="deliver",
        out_shape=(rows_type, table_type),
        in_specs=[anywhere, anywhere],
        out_specs=(anywhere, anywhere),
        scratch_shapes=[
            pltpu.VMEM(rows_type.shape, jnp.bfloat16),
            pltpu.VMEM(table_type.shape, jnp.bfloat16),
            pltpu.SemaphoreType.DMA((chunks + 1,)),
            pltpu.SemaphoreType.DMA((chunks + 1,)),
        ],
        compiler_params=pltpu.CompilerParams(vmem_limit_bytes=VMEM_BYTES),
    )(layer_rows, table_new)


def short_line(sizes, features, history, weights, tile_values, tile_rows, tile_cols, tile_counts, span_ids):
    sections, vertices, feats = sizes
    spans, span_rows = span_ids.shape
    slots, side = tile_values.shape[1:3]
    owned, width = features.shape
    rows_whole = span_rows * vertices
    rows_all = spans * span_rows
    pieces = 4
    vmem = pl.BlockSpec(memory_space=pltpu.VMEM)
    smem = pl.BlockSpec(memory_space=pltpu.SMEM)
    anywhere = pl.BlockSpec(memory_space=pl.ANY)
    block = pltpu.VMEM((spans, span_rows, width), jnp.bfloat16)
    pair = pltpu.SemaphoreType.DMA((spans, pieces))
    triple = pltpu.SemaphoreType.DMA((spans, vertices - 1, pieces))
    table = history[0].reshape(owned // side, side, width)
    layer_rows, table_new = pl.pallas_call(
        functools.partial(stream, sections, vertices, feats),
        name="stream",
        out_shape=(
            pltpu.VMEM((spans, span_rows, width), jnp.bfloat16),
            pltpu.VMEM(table.shape, jnp.bfloat16),
        ),
        in_specs=[smem, smem, smem, vmem, anywhere, anywhere, anywhere, anywhere],
        out_specs=(vmem, vmem),
        scratch_shapes=[
            pltpu.VMEM(tile_values.shape, jnp.bfloat16),
            pltpu.VMEM((rows_whole, slots * side), jnp.bfloat16),
            pltpu.VMEM((slots * side, width), jnp.bfloat16),
            pltpu.VMEM((slots * side, rows_all), jnp.bfloat16),
            pltpu.VMEM((spans, rows_whole, width), jnp.float32),
            pltpu.VMEM((spans, rows_whole, rows_all), jnp.bfloat16),
            pltpu.VMEM(weights.shape[1:], weights.dtype),
            pltpu.VMEM(table.shape, jnp.bfloat16),
            pltpu.VMEM((owned // side, side, rows_all), jnp.bfloat16),
            pltpu.VMEM((rows_all, width), jnp.bfloat16),
            pltpu.VMEM((rows_all, width), jnp.bfloat16),
            pltpu.VMEM((spans, rows_whole, width), jnp.bfloat16),
            pltpu.VMEM((spans, vertices - 1, span_rows, width), jnp.bfloat16),
            block, block, block, block, block,
            pltpu.SemaphoreType.DMA((spans + 3,)),
            pair, pair, triple, triple, pair, pair, pair, pair, pair, pair, pair,
        ],
        compiler_params=pltpu.CompilerParams(
            vmem_limit_bytes=VMEM_BYTES, collective_id=0, has_side_effects=True
        ),
    )(tile_rows, tile_cols, tile_counts.reshape(1, spans), span_ids, tile_values, weights[0], table,
      features.reshape(table.shape))
    chunks = 4
    layer_rows, table_new = pl.pallas_call(
        write,
        name="write",
        out_shape=(
            jax.ShapeDtypeStruct((spans, span_rows, width), jnp.bfloat16),
            jax.ShapeDtypeStruct(table.shape, jnp.bfloat16),
        ),
        in_specs=[vmem, vmem],
        out_specs=(anywhere, anywhere),
        scratch_shapes=[pltpu.SemaphoreType.DMA((chunks + 1,))],
        compiler_params=pltpu.CompilerParams(vmem_limit_bytes=VMEM_BYTES),
    )(layer_rows, table_new)
    return layer_rows, table_new.reshape(owned, width)


def shards(sizes, *arrays):
    layers = short_line if sizes[0] == sizes[1] == LINE else long_line
    layer_rows, table_new = layers(sizes, *arrays)
    return (layer_rows[None], table_new[None])


def solution(mesh):
    placed = (
        P("vertex", "feat"),
        P("section", "vertex", "feat"),
        P("section", None, "feat"),
        P(None, "vertex", None, None),
        P(None, "vertex"),
        P(None, "vertex"),
        P(None, "vertex"),
        P(None, "vertex"),
    )
    sizes = (mesh.shape["section"], mesh.shape["vertex"], mesh.shape["feat"])
    return jax.shard_map(
        functools.partial(shards, sizes),
        mesh=mesh,
        in_specs=placed,
        out_specs=(P("section", None, "vertex", "feat"), P("section", "vertex", "feat")),
        check_vma=False,
    )
```

```python
import functools

import jax
import jax.numpy as jnp
from jax import lax
from jax.experimental import pallas as pl
from jax.experimental.pallas import tpu as pltpu
from jax.sharding import PartitionSpec as P

RESIDUAL_SHARE = 0.2
BETA_SCALE = 0.5
MESH = pl.DeviceIdType.MESH
VMEM_BYTES = 60_000 * 1024


def chosen(ids_row, rows, first=0):
    shape = (rows, ids_row.shape[1])
    return (lax.broadcasted_iota(jnp.int32, shape, 0) + first == ids_row).astype(jnp.float32)


def prepare(rows_ref, cols_ref, counts_ref, tiles_ref, dense_hbm, dense, dense_sem):
    spans, _, side, _ = tiles_ref.shape
    copies = []
    for span in range(spans):
        dense[span] = jnp.zeros(dense.shape[1:], dense.dtype)

        def place(t, _, span=span):
            row = pl.multiple_of(rows_ref[span, t] * side, side)
            col = pl.multiple_of(cols_ref[span, t] * side, side)
            dense[span, pl.ds(row, side), pl.ds(col, side)] = tiles_ref[span, t]
            return 0

        lax.fori_loop(0, counts_ref[0, span], place, 0)
        copies.append(pltpu.make_async_copy(dense.at[span], dense_hbm.at[span], dense_sem.at[span]))
        copies[-1].start()
    for copy in copies:
        copy.wait()


def relay(
    sections, vertices, feats,
    dense_hbm, ids_ref, weight_hbm, kept_hbm, features_hbm, out_ref, table_hbm,
    dense, base_ref, picks_ref, weight_ref, kept_ref, features_ref, select_ref, initial_ref, fresh_ref,
    arrived, partial, parts, passing, support, other, result,
    load_sem, table_sem, x_send, x_recv, p_send, p_recv, h_send, h_recv, s_send, s_recv,
):
    section = lax.axis_index("section")
    vertex = lax.axis_index("vertex")
    feat = lax.axis_index("feat")
    spans, span_rows, width = arrived.shape
    last = vertices - 1
    partner = lax.rem(feat + 1, feats)
    beta = jnp.log(BETA_SCALE / (section + 1).astype(jnp.float32) + 1.0)
    halves = 2
    piece = span_rows // halves
    relayed = vertices > 3

    rows_whole = dense.shape[1]
    owned = kept_ref.shape[0]
    group = min(512, rows_whole)
    chunk = min(256, owned)

    def load_dense(span):
        return pltpu.make_async_copy(dense_hbm.at[span], dense.at[span % 2], load_sem.at[span])

    load_weight = pltpu.make_async_copy(weight_hbm, weight_ref, load_sem.at[spans])
    load_kept = pltpu.make_async_copy(kept_hbm, kept_ref, load_sem.at[spans + 1])
    load_features = pltpu.make_async_copy(features_hbm, features_ref, load_sem.at[spans + 2])
    load_kept.start()
    load_features.start()
    for span in range(min(2, spans)):
        load_dense(span).start()
    load_weight.start()

    barrier = pltpu.get_barrier_semaphore()
    for step in range(1, vertices):
        peer = lax.rem(vertex + step, vertices)
        pl.semaphore_signal(barrier, inc=1, device_id=(section, peer, feat), device_id_type=MESH)
    pl.semaphore_signal(barrier, inc=1, device_id=(section, vertex, partner), device_id_type=MESH)
    for step in (1, sections - 1):
        peer = lax.rem(section + step, sections)
        pl.semaphore_signal(barrier, inc=1, device_id=(peer, vertex, feat), device_id_type=MESH)
    if relayed:
        @pl.when(vertex == 0)
        def _():
            parts[:, 0] = jnp.zeros((spans, span_rows, width), jnp.bfloat16)

        @pl.when(vertex == last)
        def _():
            parts[:, last - 1] = jnp.zeros((spans, span_rows, width), jnp.bfloat16)

    pl.semaphore_wait(barrier, vertices - 1 + 1 + 2)

    def half_of(half):
        return slice(half * piece, (half + 1) * piece)

    def row_copy(span, half):
        rows = pl.ds(half * piece, piece)
        return pltpu.make_async_remote_copy(
            src_ref=result.at[span, rows], dst_ref=arrived.at[span, rows],
            send_sem=x_send.at[span, half], recv_sem=x_recv.at[span, half],
            device_id=(lax.rem(section + 1, sections), vertex, feat), device_id_type=MESH,
        )

    def chunk_rows(peer, half):
        return pl.ds(pl.multiple_of(peer * span_rows + half * piece, piece), piece)

    def part_copy(span, step, half):
        peer = lax.rem(vertex + step, vertices)
        return pltpu.make_async_remote_copy(
            src_ref=partial.at[span, chunk_rows(peer, half)],
            dst_ref=parts.at[span, step - 1, pl.ds(half * piece, piece)],
            send_sem=p_send.at[span, step - 1, half], recv_sem=p_recv.at[span, step - 1, half],
            device_id=(section, peer, feat), device_id_type=MESH,
        )

    def pass_copy(span, half):
        far = jnp.where(vertex == 0, last, 0)
        near = jnp.where(vertex == 0, 1, last - 1)
        return pltpu.make_async_remote_copy(
            src_ref=partial.at[span, chunk_rows(far, half)],
            dst_ref=passing.at[span, pl.ds(half * piece, piece)],
            send_sem=h_send.at[span, half], recv_sem=h_recv.at[span, half],
            device_id=(section, near, feat), device_id_type=MESH,
        )

    def support_copy(span, half):
        rows = pl.ds(half * piece, piece)
        return pltpu.make_async_remote_copy(
            src_ref=support.at[span, rows], dst_ref=other.at[span, rows],
            send_sem=s_send.at[span, half], recv_sem=s_recv.at[span, half],
            device_id=(section, vertex, partner), device_id_type=MESH,
        )

    at_end = (vertex == 0) | (vertex == last)

    def is_direct(step):
        if not relayed:
            return vertex >= 0
        peer = lax.rem(vertex + step, vertices)
        ends = ((vertex == 0) & (peer == last)) | ((vertex == last) & (peer == 0))
        inner = ((vertex == 1) & (peer == last)) | ((vertex == last - 1) & (peer == 0))
        return jnp.logical_not(ends | inner)

    def is_sent(step):
        if not relayed:
            return vertex >= 0
        peer = lax.rem(vertex + step, vertices)
        return jnp.logical_not(((vertex == 0) & (peer == last)) | ((vertex == last) & (peer == 0)))

    def is_received(step):
        if not relayed:
            return vertex >= 0
        source = lax.rem(vertex + vertices - step, vertices)
        return jnp.logical_not(((vertex == 0) & (source == last)) | ((vertex == last) & (source == 0)))

    def local(span, leading):
        mine = slice(span * span_rows, (span + 1) * span_rows)
        used = (span + 1) * span_rows

        def clear(i, _):
            first = pl.multiple_of(i * chunk, chunk)
            here = pl.ds(first, chunk)
            hot = chosen(ids_ref[span : span + 1, :], chunk, first)
            select_ref[here, mine] = hot.astype(jnp.bfloat16)
            taken = jnp.max(hot, axis=1, keepdims=True) > 0.5
            filler = features_ref[here, :].astype(jnp.float32) if leading else 0.0
            kept_ref[here, :] = jnp.where(taken, filler, kept_ref[here, :].astype(jnp.float32)).astype(jnp.bfloat16)
            return 0

        lax.fori_loop(0, owned // chunk, clear, 0)
        load_dense(span).wait()

        def multiply(i, _):
            here = pl.ds(pl.multiple_of(i * group, group), group)
            block = dense[span % 2, here, :]
            product = jnp.dot(block, kept_ref[...], preferred_element_type=jnp.float32)
            if leading:
                partial[span, here, :] = product.astype(jnp.bfloat16)
            else:
                base_ref[span, here, :] = product
                picks_ref[span, here, :used] = jnp.dot(
                    block, select_ref[:, :used], preferred_element_type=jnp.float32
                ).astype(jnp.bfloat16)
            return 0

        lax.fori_loop(0, rows_whole // group, multiply, 0)
        if span + 2 < spans:
            load_dense(span + 2).start()

    def gather():
        initial_ref[...] = lax.dot_general(
            select_ref[...], features_ref[...], (((0,), (0,)), ((), ())), preferred_element_type=jnp.float32
        ).astype(jnp.bfloat16)

    def earlier(span):
        used = span * span_rows

        def add(i, _):
            here = pl.ds(pl.multiple_of(i * group, group), group)
            base_ref[span, here, :] += jnp.dot(
                picks_ref[span, here, :used], fresh_ref[:used, :], preferred_element_type=jnp.float32
            )
            return 0

        lax.fori_loop(0, rows_whole // group, add, 0)

    def scatter(span):
        mine = slice(span * span_rows, (span + 1) * span_rows)
        @pl.when(section > 0)
        def _():
            for half in range(halves):
                row_copy(span, half).wait_recv()
            fresh_ref[mine, :] = arrived[span]


        def compute(peer):
            here = pl.ds(pl.multiple_of(peer * span_rows, span_rows), span_rows)
            total = base_ref[span, here, :] + jnp.dot(
                picks_ref[span, here, mine], fresh_ref[mine, :], preferred_element_type=jnp.float32
            )
            partial[span, here, :] = total.astype(jnp.bfloat16)

        if relayed:
            @pl.when(at_end & (section > 0))
            def _():
                compute(jnp.where(vertex == 0, last, 0))

            @pl.when(at_end)
            def _():
                for half in range(halves):
                    pass_copy(span, half).start()

        for step in range(1, vertices):
            @pl.when(is_sent(step) & (section > 0))
            def _(step=step):
                compute(lax.rem(vertex + step, vertices))

            @pl.when(is_direct(step))
            def _(step=step):
                part_copy(span, step, 0).start()

        for half in range(1, halves):
            for step in range(1, vertices):
                @pl.when(is_direct(step))
                def _(step=step, half=half):
                    part_copy(span, step, half).start()

        @pl.when(section > 0)
        def _():
            compute(vertex)

    def pass_on(span):
        if relayed:
            for who, step in ((1, last - 1), (last - 1, 2)):
                @pl.when(vertex == who)
                def _(who=who, step=step):
                    far = last if who == 1 else 0
                    for half in range(halves):
                        pass_copy(span, half).wait_recv()
                        here = pl.ds(far * span_rows + half * piece, piece)
                        partial[span, here, :] = (
                            partial[span, here, :].astype(jnp.float32)
                            + passing[span, half_of(half), :].astype(jnp.float32)
                        ).astype(jnp.bfloat16)
                        part_copy(span, step, half).start()

    def finish(span, half):
        total = partial[span, chunk_rows(vertex, half), :].astype(jnp.float32)
        for step in range(1, vertices):
            @pl.when(is_received(step))
            def _(step=step):
                part_copy(span, step, half).wait_recv()

        for step in range(1, vertices):
            total += parts[span, step - 1, half_of(half), :].astype(jnp.float32)
        mixed = (
            (1.0 - RESIDUAL_SHARE) * total
            + RESIDUAL_SHARE * initial_ref[pl.ds(span * span_rows + half * piece, piece), :].astype(jnp.float32)
        ).astype(jnp.bfloat16)
        support[span, half_of(half), :] = mixed
        support_copy(span, half).start()
        mine = pl.ds(pl.multiple_of(feat * width, width), width)
        theirs = pl.ds(pl.multiple_of(partner * width, width), width)
        projected = jnp.dot(mixed, weight_ref[mine, :], preferred_element_type=jnp.float32)
        support_copy(span, half).wait_recv()
        projected += jnp.dot(other[span, half_of(half), :], weight_ref[theirs, :], preferred_element_type=jnp.float32)
        rows = jnp.maximum((1.0 - beta) * mixed.astype(jnp.float32) + beta * projected, 0.0).astype(jnp.bfloat16)
        result[span, half_of(half), :] = rows
        out_ref[span, half_of(half), :] = rows

        @pl.when(section < sections - 1)
        def _():
            row_copy(span, half).start()

    def finish_all(span):
        for half in range(halves):
            finish(span, half)

    load_kept.wait()
    load_features.wait()

    @pl.when(section == 0)
    def _():
        for span in range(spans):
            local(span, True)
            scatter(span)
            if span:
                pass_on(span - 1)
        gather()
        load_weight.wait()
        for span in range(spans - 1):
            finish_all(span)
            if span == 0:
                pass_on(spans - 1)

    @pl.when(section > 0)
    def _():
        for span in range(spans):
            local(span, False)
        gather()
        load_weight.wait()
        for span in range(spans):
            scatter(span)
            pass_on(span)
            if span:
                finish_all(span - 1)
            if span + 1 < spans:
                earlier(span + 1)

    def merge(i, _):
        here = pl.ds(pl.multiple_of(i * chunk, chunk), chunk)
        moved = jnp.dot(select_ref[here, :], fresh_ref[...], preferred_element_type=jnp.float32)
        kept_ref[here, :] = (kept_ref[here, :].astype(jnp.float32) + moved).astype(jnp.bfloat16)
        return 0

    @pl.when(section > 0)
    def _():
        lax.fori_loop(0, owned // chunk, merge, 0)

    store = pltpu.make_async_copy(kept_ref, table_hbm, table_sem)
    store.start()
    finish_all(spans - 1)

    for span in range(spans):
        for half in range(halves):
            support_copy(span, half).wait_send()
            for step in range(1, vertices):
                @pl.when(is_sent(step))
                def _(span=span, step=step, half=half):
                    part_copy(span, step, half).wait_send()

            if relayed:
                @pl.when(at_end)
                def _(span=span, half=half):
                    pass_copy(span, half).wait_send()

            @pl.when(section < sections - 1)
            def _(span=span, half=half):
                row_copy(span, half).wait_send()

    store.wait()

LINE = 4


def write(rows_ref, table_ref, rows_out, table_out, sem):
    chunks = sem.shape[0] - 1
    size = table_ref.shape[0] // chunks
    moves = [pltpu.make_async_copy(rows_ref, rows_out, sem.at[chunks])]
    for i in range(chunks):
        here = pl.ds(i * size, size)
        moves.append(pltpu.make_async_copy(table_ref.at[here], table_out.at[here], sem.at[i]))
    for move in moves:
        move.start()
    for move in moves:
        move.wait()


def stream(
    sections, vertices, feats,
    rows_ref, cols_ref, counts_ref, ids_ref, tiles_hbm, weight_hbm, kept_hbm, features_hbm, out_ref, kept_ref,
    tiles, left, right, right_select, base_ref, picks_ref, weight_ref, features_ref, select_ref, taken_ref, initial_ref,
    fresh_ref, partial, parts, passing, transit, support, other, result,
    load_sem, x_send, x_recv, p_send, p_recv, h_send, h_recv, s_send, s_recv, d_send, d_recv, t_send,
):
    section = lax.axis_index("section")
    vertex = lax.axis_index("vertex")
    feat = lax.axis_index("feat")
    spans, span_rows, width = result.shape
    pieces = x_send.shape[1]
    part = width // pieces
    wide = min(256, width)
    slots, side = tiles.shape[1:3]
    row_blocks = left.shape[0] // side
    rows_all = spans * span_rows
    last = vertices - 1
    partner = lax.rem(feat + 1, feats)
    beside = lax.rem(section + sections // 2, sections)
    opposite = lax.rem(vertex + last - 1, vertices)
    beta = jnp.log(BETA_SCALE / (section + 1).astype(jnp.float32) + 1.0)
    col_blocks = kept_ref.shape[0]

    def load_tiles(span):
        return pltpu.make_async_copy(tiles_hbm.at[span], tiles.at[span], load_sem.at[span])

    load_weight = pltpu.make_async_copy(weight_hbm, weight_ref, load_sem.at[spans])
    load_kept = pltpu.make_async_copy(kept_hbm, kept_ref, load_sem.at[spans + 1])
    load_features = pltpu.make_async_copy(features_hbm, features_ref, load_sem.at[spans + 2])
    load_kept.start()
    load_features.start()
    for span in range(spans):
        load_tiles(span).start()
    load_weight.start()

    barrier = pltpu.get_barrier_semaphore()
    for step in range(1, vertices):
        peer = lax.rem(vertex + step, vertices)
        pl.semaphore_signal(barrier, inc=1, device_id=(section, peer, feat), device_id_type=MESH)
    pl.semaphore_signal(barrier, inc=1, device_id=(section, vertex, partner), device_id_type=MESH)
    for step in (1, sections - 1):
        peer = lax.rem(section + step, sections)
        pl.semaphore_signal(barrier, inc=1, device_id=(peer, vertex, feat), device_id_type=MESH)
    for peer in (vertex, opposite):
        pl.semaphore_signal(barrier, inc=1, device_id=(beside, peer, feat), device_id_type=MESH)

    def meet():
        pl.semaphore_wait(barrier, vertices - 1 + 1 + 2 + 2)

    at_end = (vertex == 0) | (vertex == last)

    @pl.when(vertex == 0)
    def _():
        parts[:, 0] = jnp.zeros((spans, span_rows, width), jnp.bfloat16)

    @pl.when(vertex == last)
    def _():
        parts[:, last - 1] = jnp.zeros((spans, span_rows, width), jnp.bfloat16)

    def columns(j):
        return slice(j * part, (j + 1) * part)

    def lanes(j):
        return pl.ds(j * part, part)

    def span_of(span):
        return slice(span * span_rows, (span + 1) * span_rows)

    def row_copy(span, j):
        return pltpu.make_async_remote_copy(
            src_ref=result.at[span, :, lanes(j)],
            dst_ref=fresh_ref.at[pl.ds(span * span_rows, span_rows), lanes(j)],
            send_sem=x_send.at[span, j], recv_sem=x_recv.at[span, j],
            device_id=(lax.rem(section + 1, sections), vertex, feat), device_id_type=MESH,
        )

    def rows_of(peer):
        return pl.ds(pl.multiple_of(peer * span_rows, span_rows), span_rows)

    def part_copy(span, step, j):
        peer = lax.rem(vertex + step, vertices)
        return pltpu.make_async_remote_copy(
            src_ref=partial.at[span, rows_of(peer), lanes(j)], dst_ref=parts.at[span, step - 1, :, lanes(j)],
            send_sem=p_send.at[span, step - 1, j], recv_sem=p_recv.at[span, step - 1, j],
            device_id=(section, peer, feat), device_id_type=MESH,
        )

    def pass_copy(span, j):
        far = jnp.where(vertex == 0, last, 0)
        near = jnp.where(vertex == 0, 1, last - 1)
        return pltpu.make_async_remote_copy(
            src_ref=partial.at[span, rows_of(far), lanes(j)], dst_ref=passing.at[span, :, lanes(j)],
            send_sem=h_send.at[span, j], recv_sem=h_recv.at[span, j],
            device_id=(section, near, feat), device_id_type=MESH,
        )

    def detour_copy(span, j):
        return pltpu.make_async_remote_copy(
            src_ref=partial.at[span, rows_of(opposite), lanes(j)], dst_ref=transit.at[span, :, lanes(j)],
            send_sem=d_send.at[span, j], recv_sem=d_recv.at[span, j],
            device_id=(beside, vertex, feat), device_id_type=MESH,
        )

    def return_copy(span, j):
        return pltpu.make_async_remote_copy(
            src_ref=transit.at[span, :, lanes(j)], dst_ref=parts.at[span, last - 2, :, lanes(j)],
            send_sem=t_send.at[span, j], recv_sem=p_recv.at[span, last - 2, j],
            device_id=(beside, opposite, feat), device_id_type=MESH,
        )

    def support_copy(span, j):
        return pltpu.make_async_remote_copy(
            src_ref=support.at[span, :, lanes(j)], dst_ref=other.at[span, :, lanes(j)],
            send_sem=s_send.at[span, j], recv_sem=s_recv.at[span, j],
            device_id=(section, vertex, partner), device_id_type=MESH,
        )

    def ends_meet(here, there):
        return ((here == 0) & (there == last)) | ((here == last) & (there == 0))

    def is_sent(step):
        far = ends_meet(vertex, lax.rem(vertex + step, vertices))
        return jnp.logical_not(far | at_end) if step == last - 1 else jnp.logical_not(far)

    def is_received(step):
        return jnp.logical_not(ends_meet(lax.rem(vertex + vertices - step, vertices), vertex))

    def choose():
        def one_hot(i, _):
            for span in range(spans):
                hot = chosen(ids_ref[span : span + 1, :], side, i * side)
                select_ref[i, :, span_of(span)] = hot.astype(jnp.bfloat16)
            return 0

        lax.fori_loop(0, col_blocks, one_hot, 0)

    def count(span):
        taken_ref[span] = jnp.dot(
            select_ref[...].reshape(col_blocks * side, rows_all)[:, span_of(span)],
            jnp.ones((span_rows, side), jnp.bfloat16),
            preferred_element_type=jnp.float32,
        ).astype(jnp.bfloat16).reshape(col_blocks, side, side)

    def mark(span, leading):
        def clear(i, _):
            taken = taken_ref[span, i]
            rest = 1.0 - taken
            for first in range(0, width, side):
                group = slice(first, first + side)
                row = kept_ref[i, :, group] * rest
                kept_ref[i, :, group] = row + features_ref[i, :, group] * taken if leading else row
            return 0

        lax.fori_loop(0, col_blocks, clear, 0)

    def lay(span, leading):
        used = (span + 1) * span_rows
        load_tiles(span).wait()
        lives = jnp.full((side, side), counts_ref[0, span], jnp.int32)

        def place(t, _):
            col = cols_ref[span, t]
            here = pl.ds(pl.multiple_of(t * side, side), side)
            tile = tiles[span, t].astype(jnp.float32)
            rows = jnp.where(lives > t, jnp.full(tile.shape, rows_ref[span, t], jnp.int32), row_blocks)
            for block in range(row_blocks):
                left[block * side : (block + 1) * side, here] = jnp.where(rows == block, tile, 0.0).astype(left.dtype)
            right[here, :] = kept_ref[col]
            if not leading:
                right_select[here, :] = select_ref[col]
            return 0

        lax.fori_loop(0, slots, place, 0)

    def gather():
        initial_ref[...] = lax.dot_general(
            select_ref[...].reshape(col_blocks * side, rows_all),
            features_ref[...].reshape(col_blocks * side, width),
            (((0,), (0,)), ((), ())),
            preferred_element_type=jnp.float32,
        ).astype(jnp.bfloat16)

    def groups():
        return [slice(first, first + wide) for first in range(0, width, wide)]

    def product(group):
        return jnp.dot(left[...], right[:, group], preferred_element_type=jnp.float32)

    def first_sums(span, j):
        if j * part % wide == 0:
            group = slice(j * part, j * part + wide)
            partial[span, :, group] = product(group).astype(jnp.bfloat16)

    def later_sums(span, j):
        row_copy(span, j).wait_recv()
        partial[span, :, columns(j)] = (
            base_ref[span, :, columns(j)]
            + jnp.dot(
                picks_ref[span, :, span_of(span)], fresh_ref[span_of(span), columns(j)],
                preferred_element_type=jnp.float32,
            )
        ).astype(jnp.bfloat16)

    def scatter(span, sums):
        for j in range(pieces):
            sums(span, j)

            @pl.when(at_end)
            def _(j=j):
                pass_copy(span, j).start()
                detour_copy(span, j).start()

            @pl.when(jnp.logical_not(at_end))
            def _(j=j):
                for step in (1, last):
                    part_copy(span, step, j).start()

        for j in range(pieces):
            for step in (1, last):
                @pl.when(at_end & is_sent(step))
                def _(step=step, j=j):
                    part_copy(span, step, j).start()

    def pass_on(span):
        for who, step in ((1, last - 1), (last - 1, 2)):
            @pl.when(vertex == who)
            def _(who=who, step=step):
                far = last if who == 1 else 0
                here = pl.ds(far * span_rows, span_rows)
                for j in range(pieces):
                    pass_copy(span, j).wait_recv()
                    partial[span, here, columns(j)] = (
                        partial[span, here, columns(j)].astype(jnp.float32)
                        + passing[span, :, columns(j)].astype(jnp.float32)
                    ).astype(jnp.bfloat16)
                    part_copy(span, step, j).start()

    def hand_on(span):
        @pl.when(at_end)
        def _():
            for j in range(pieces):
                detour_copy(span, j).wait_recv()
                return_copy(span, j).start()

    def keep(span):
        used = (span + 1) * span_rows
        for group in groups():
            base_ref[span, :, group] = product(group)
        picks_ref[span, :, :used] = jnp.dot(
            left[...], right_select[:, :used], preferred_element_type=jnp.float32
        ).astype(jnp.bfloat16)

    def earlier(span):
        used = span * span_rows
        for group in groups():
            base_ref[span, :, group] += jnp.dot(
                picks_ref[span, :, :used], fresh_ref[:used, group], preferred_element_type=jnp.float32
            )

    def weight_rows(which):
        return pl.ds(pl.multiple_of(which * width, width), width)

    def finish(span):
        for j in range(pieces):
            for step in range(1, vertices):
                @pl.when(is_received(step))
                def _(step=step, j=j):
                    part_copy(span, step, j).wait_recv()

            total = partial[span, rows_of(vertex), columns(j)].astype(jnp.float32)
            for step in range(1, vertices):
                total += parts[span, step - 1, :, columns(j)].astype(jnp.float32)
            support[span, :, columns(j)] = (
                (1.0 - RESIDUAL_SHARE) * total
                + RESIDUAL_SHARE * initial_ref[span_of(span), columns(j)].astype(jnp.float32)
            ).astype(jnp.bfloat16)
            support_copy(span, j).start()

        projected = [
            jnp.dot(support[span], weight_ref[weight_rows(feat), group], preferred_element_type=jnp.float32)
            for group in groups()
        ]
        for j in range(pieces):
            support_copy(span, j).wait_recv()
        for k, group in enumerate(groups()):
            whole = projected[k] + jnp.dot(
                other[span], weight_ref[weight_rows(partner), group], preferred_element_type=jnp.float32
            )
            rows = jnp.maximum(
                (1.0 - beta) * support[span, :, group].astype(jnp.float32) + beta * whole, 0.0
            ).astype(jnp.bfloat16)
            result[span, :, group] = rows

            @pl.when(section < sections - 1)
            def _(group=group):
                for j in range(group.start // part, group.stop // part):
                    row_copy(span, j).start()

            out_ref[span, :, group] = rows

    choose()
    count(0)
    load_kept.wait()
    load_features.wait()

    @pl.when(section == 0)
    def _():
        for span in range(spans):
            if span:
                count(span)
            mark(span, True)
            lay(span, True)
            if span == 0:
                meet()
            scatter(span, first_sums)
            if span == min(1, spans - 1):
                gather()
                load_weight.wait()
            if span == 1:
                pass_on(0)
        for span in range(spans - 1):
            finish(span)
            pass_on(span + 1)

    @pl.when(section > 0)
    def _():
        for span in range(spans):
            if span:
                count(span)
            mark(span, False)
            lay(span, False)
            keep(span)
            if span == 0:
                meet()

            @pl.when(section >= sections // 2)
            def _(span=span):
                hand_on(span)

        gather()
        load_weight.wait()
        for span in range(spans):
            scatter(span, later_sums)
            if span:
                finish(span - 1)
            pass_on(span)
            if span + 1 < spans:
                earlier(span + 1)

    def merge():
        blocks = max(1, 512 // side)
        for first in range(0, col_blocks, blocks):
            picked = select_ref[first : first + blocks].reshape(blocks * side, rows_all)
            for group in groups():
                moved = jnp.dot(picked, fresh_ref[:, group], preferred_element_type=jnp.float32).astype(jnp.bfloat16)
                kept_ref[first : first + blocks, :, group] += moved.reshape(blocks, side, wide)

    @pl.when(section > 0)
    def _():
        merge()

    finish(spans - 1)

    @pl.when(section < sections // 2)
    def _():
        for span in range(spans):
            hand_on(span)

    for span in range(spans):
        for j in range(pieces):
            support_copy(span, j).wait_send()
            for step in range(1, vertices):
                @pl.when(is_sent(step))
                def _(span=span, step=step, j=j):
                    part_copy(span, step, j).wait_send()

            @pl.when(at_end)
            def _(span=span, j=j):
                pass_copy(span, j).wait_send()
                detour_copy(span, j).wait_send()
                return_copy(span, j).wait_send()

            @pl.when(section < sections - 1)
            def _(span=span, j=j):
                row_copy(span, j).wait_send()


def deliver(rows_hbm, table_hbm, rows_out, table_out, rows_ref, table_ref, in_sem, out_sem):
    chunks = in_sem.shape[0] - 1
    size = table_ref.shape[0] // chunks
    moves = []
    for i in range(chunks):
        here = pl.ds(i * size, size)
        moves.append((
            pltpu.make_async_copy(table_hbm.at[here], table_ref.at[here], in_sem.at[i]),
            pltpu.make_async_copy(table_ref.at[here], table_out.at[here], out_sem.at[i]),
        ))
    moves.append((
        pltpu.make_async_copy(rows_hbm, rows_ref, in_sem.at[chunks]),
        pltpu.make_async_copy(rows_ref, rows_out, out_sem.at[chunks]),
    ))
    for get, _ in moves:
        get.start()
    for get, put in moves:
        get.wait()
        put.start()
    for _, put in moves:
        put.wait()


def long_line(sizes, features, history, weights, tile_values, tile_rows, tile_cols, tile_counts, span_ids):
    sections, vertices, feats = sizes
    spans, span_rows = span_ids.shape
    owned, width = features.shape
    rows_whole = span_rows * vertices
    rows_all = spans * span_rows
    vmem = pl.BlockSpec(memory_space=pltpu.VMEM)
    smem = pl.BlockSpec(memory_space=pltpu.SMEM)
    anywhere = pl.BlockSpec(memory_space=pl.ANY)

    dense = pl.pallas_call(
        prepare,
        name="prepare",
        out_shape=jax.ShapeDtypeStruct((spans, rows_whole, owned), jnp.bfloat16),
        in_specs=[smem, smem, smem, vmem],
        out_specs=anywhere,
        scratch_shapes=[
            pltpu.VMEM((spans, rows_whole, owned), jnp.bfloat16),
            pltpu.SemaphoreType.DMA((spans,)),
        ],
        compiler_params=pltpu.CompilerParams(vmem_limit_bytes=VMEM_BYTES),
    )(tile_rows, tile_cols, tile_counts.reshape(1, spans), tile_values)

    rows_type = jax.ShapeDtypeStruct((spans, span_rows, width), jnp.bfloat16)
    table_type = jax.ShapeDtypeStruct((owned, width), jnp.bfloat16)
    block = pltpu.VMEM(rows_type.shape, jnp.bfloat16)
    halves = 2
    pair = pltpu.SemaphoreType.DMA((spans, halves))
    layer_rows, table_new = pl.pallas_call(
        functools.partial(relay, sections, vertices, feats),
        name="relay",
        out_shape=(rows_type, table_type),
        in_specs=[anywhere, vmem, anywhere, anywhere, anywhere],
        out_specs=(vmem, anywhere),
        scratch_shapes=[
            pltpu.VMEM((min(2, spans), rows_whole, owned), jnp.bfloat16),
            pltpu.VMEM((spans, rows_whole, width), jnp.float32),
            pltpu.VMEM((spans, rows_whole, rows_all), jnp.bfloat16),
            pltpu.VMEM(weights.shape[1:], weights.dtype),
            pltpu.VMEM((owned, width), jnp.bfloat16),
            pltpu.VMEM((owned, width), jnp.bfloat16),
            pltpu.VMEM((owned, rows_all), jnp.bfloat16),
            pltpu.VMEM((rows_all, width), jnp.bfloat16),
            pltpu.VMEM((rows_all, width), jnp.bfloat16),
            block,
            pltpu.VMEM((spans, rows_whole, width), jnp.bfloat16),
            pltpu.VMEM((spans, vertices - 1, span_rows, width), jnp.bfloat16),
            block, block, block, block,
            pltpu.SemaphoreType.DMA((spans + 3,)),
            pltpu.SemaphoreType.DMA,
            pair, pair,
            pltpu.SemaphoreType.DMA((spans, vertices - 1, halves)),
            pltpu.SemaphoreType.DMA((spans, vertices - 1, halves)),
            pair, pair, pair, pair,
        ],
        compiler_params=pltpu.CompilerParams(
            vmem_limit_bytes=VMEM_BYTES, collective_id=0, has_side_effects=True
        ),
    )(dense, span_ids, weights[0], history[0], features)

    table_type = jax.ShapeDtypeStruct((owned, width), jnp.bfloat16)
    chunks = 8
    return pl.pallas_call(
        deliver,
        name="deliver",
        out_shape=(rows_type, table_type),
        in_specs=[anywhere, anywhere],
        out_specs=(anywhere, anywhere),
        scratch_shapes=[
            pltpu.VMEM(rows_type.shape, jnp.bfloat16),
            pltpu.VMEM(table_type.shape, jnp.bfloat16),
            pltpu.SemaphoreType.DMA((chunks + 1,)),
            pltpu.SemaphoreType.DMA((chunks + 1,)),
        ],
        compiler_params=pltpu.CompilerParams(vmem_limit_bytes=VMEM_BYTES),
    )(layer_rows, table_new)


def short_line(sizes, features, history, weights, tile_values, tile_rows, tile_cols, tile_counts, span_ids):
    sections, vertices, feats = sizes
    spans, span_rows = span_ids.shape
    slots, side = tile_values.shape[1:3]
    owned, width = features.shape
    rows_whole = span_rows * vertices
    rows_all = spans * span_rows
    pieces = 4
    vmem = pl.BlockSpec(memory_space=pltpu.VMEM)
    smem = pl.BlockSpec(memory_space=pltpu.SMEM)
    anywhere = pl.BlockSpec(memory_space=pl.ANY)
    block = pltpu.VMEM((spans, span_rows, width), jnp.bfloat16)
    pair = pltpu.SemaphoreType.DMA((spans, pieces))
    triple = pltpu.SemaphoreType.DMA((spans, vertices - 1, pieces))
    table = history[0].reshape(owned // side, side, width)
    layer_rows, table_new = pl.pallas_call(
        functools.partial(stream, sections, vertices, feats),
        name="stream",
        out_shape=(
            pltpu.VMEM((spans, span_rows, width), jnp.bfloat16),
            pltpu.VMEM(table.shape, jnp.bfloat16),
        ),
        in_specs=[smem, smem, smem, vmem, anywhere, anywhere, anywhere, anywhere],
        out_specs=(vmem, vmem),
        scratch_shapes=[
            pltpu.VMEM(tile_values.shape, jnp.bfloat16),
            pltpu.VMEM((rows_whole, slots * side), jnp.bfloat16),
            pltpu.VMEM((slots * side, width), jnp.bfloat16),
            pltpu.VMEM((slots * side, rows_all), jnp.bfloat16),
            pltpu.VMEM((spans, rows_whole, width), jnp.float32),
            pltpu.VMEM((spans, rows_whole, rows_all), jnp.bfloat16),
            pltpu.VMEM(weights.shape[1:], weights.dtype),
            pltpu.VMEM(table.shape, jnp.bfloat16),
            pltpu.VMEM((owned // side, side, rows_all), jnp.bfloat16),
            pltpu.VMEM((spans, owned // side, side, side), jnp.bfloat16),
            pltpu.VMEM((rows_all, width), jnp.bfloat16),
            pltpu.VMEM((rows_all, width), jnp.bfloat16),
            pltpu.VMEM((spans, rows_whole, width), jnp.bfloat16),
            pltpu.VMEM((spans, vertices - 1, span_rows, width), jnp.bfloat16),
            block, block, block, block, block,
            pltpu.SemaphoreType.DMA((spans + 3,)),
            pair, pair, triple, triple, pair, pair, pair, pair, pair, pair, pair,
        ],
        compiler_params=pltpu.CompilerParams(
            vmem_limit_bytes=VMEM_BYTES, collective_id=0, has_side_effects=True
        ),
    )(tile_rows, tile_cols, tile_counts.reshape(1, spans), span_ids, tile_values, weights[0], table,
      features.reshape(table.shape))
    chunks = 4
    layer_rows, table_new = pl.pallas_call(
        write,
        name="write",
        out_shape=(
            jax.ShapeDtypeStruct((spans, span_rows, width), jnp.bfloat16),
            jax.ShapeDtypeStruct(table.shape, jnp.bfloat16),
        ),
        in_specs=[vmem, vmem],
        out_specs=(anywhere, anywhere),
        scratch_shapes=[pltpu.SemaphoreType.DMA((chunks + 1,))],
        compiler_params=pltpu.CompilerParams(vmem_limit_bytes=VMEM_BYTES),
    )(
        pltpu.with_memory_space_constraint(layer_rows, pltpu.VMEM),
        pltpu.with_memory_space_constraint(table_new, pltpu.VMEM),
    )
    return layer_rows, table_new.reshape(owned, width)


def shards(sizes, *arrays):
    layers = short_line if sizes[0] == sizes[1] == LINE else long_line
    layer_rows, table_new = layers(sizes, *arrays)
    return (layer_rows[None], table_new[None])


def solution(mesh):
    placed = (
        P("vertex", "feat"),
        P("section", "vertex", "feat"),
        P("section", None, "feat"),
        P(None, "vertex", None, None),
        P(None, "vertex"),
        P(None, "vertex"),
        P(None, "vertex"),
        P(None, "vertex"),
    )
    sizes = (mesh.shape["section"], mesh.shape["vertex"], mesh.shape["feat"])
    return jax.shard_map(
        functools.partial(shards, sizes),
        mesh=mesh,
        in_specs=placed,
        out_specs=(P("section", None, "vertex", "feat"), P("section", "vertex", "feat")),
        check_vma=False,
    )
```

```python
import functools

import jax
import jax.numpy as jnp
from jax import lax
from jax.experimental import pallas as pl
from jax.experimental.pallas import tpu as pltpu
from jax.sharding import PartitionSpec as P

RESIDUAL_SHARE = 0.2
BETA_SCALE = 0.5
MESH = pl.DeviceIdType.MESH
VMEM_BYTES = 60_000 * 1024


def chosen(ids_row, rows, first=0):
    shape = (rows, ids_row.shape[1])
    return (lax.broadcasted_iota(jnp.int32, shape, 0) + first == ids_row).astype(jnp.float32)


def prepare(rows_ref, cols_ref, counts_ref, tiles_ref, dense_hbm, dense, dense_sem):
    spans, _, side, _ = tiles_ref.shape
    copies = []
    for span in range(spans):
        dense[span] = jnp.zeros(dense.shape[1:], dense.dtype)

        def place(t, _, span=span):
            row = pl.multiple_of(rows_ref[span, t] * side, side)
            col = pl.multiple_of(cols_ref[span, t] * side, side)
            dense[span, pl.ds(row, side), pl.ds(col, side)] = tiles_ref[span, t]
            return 0

        lax.fori_loop(0, counts_ref[0, span], place, 0)
        copies.append(pltpu.make_async_copy(dense.at[span], dense_hbm.at[span], dense_sem.at[span]))
        copies[-1].start()
    for copy in copies:
        copy.wait()


def relay(
    sections, vertices, feats,
    dense_hbm, ids_ref, weight_hbm, kept_hbm, features_hbm, out_ref, table_hbm,
    dense, base_ref, picks_ref, weight_ref, kept_ref, features_ref, select_ref, initial_ref, fresh_ref,
    arrived, partial, parts, passing, support, other, result,
    load_sem, table_sem, x_send, x_recv, p_send, p_recv, h_send, h_recv, s_send, s_recv,
):
    section = lax.axis_index("section")
    vertex = lax.axis_index("vertex")
    feat = lax.axis_index("feat")
    spans, span_rows, width = arrived.shape
    last = vertices - 1
    partner = lax.rem(feat + 1, feats)
    beta = jnp.log(BETA_SCALE / (section + 1).astype(jnp.float32) + 1.0)
    halves = 2
    piece = span_rows // halves
    relayed = vertices > 3

    rows_whole = dense.shape[1]
    owned = kept_ref.shape[0]
    group = min(512, rows_whole)
    chunk = min(256, owned)

    def load_dense(span):
        return pltpu.make_async_copy(dense_hbm.at[span], dense.at[span % 2], load_sem.at[span])

    load_weight = pltpu.make_async_copy(weight_hbm, weight_ref, load_sem.at[spans])
    load_kept = pltpu.make_async_copy(kept_hbm, kept_ref, load_sem.at[spans + 1])
    load_features = pltpu.make_async_copy(features_hbm, features_ref, load_sem.at[spans + 2])
    load_kept.start()
    load_features.start()
    for span in range(min(2, spans)):
        load_dense(span).start()
    load_weight.start()

    barrier = pltpu.get_barrier_semaphore()
    for step in range(1, vertices):
        peer = lax.rem(vertex + step, vertices)
        pl.semaphore_signal(barrier, inc=1, device_id=(section, peer, feat), device_id_type=MESH)
    pl.semaphore_signal(barrier, inc=1, device_id=(section, vertex, partner), device_id_type=MESH)
    for step in (1, sections - 1):
        peer = lax.rem(section + step, sections)
        pl.semaphore_signal(barrier, inc=1, device_id=(peer, vertex, feat), device_id_type=MESH)
    if relayed:
        @pl.when(vertex == 0)
        def _():
            parts[:, 0] = jnp.zeros((spans, span_rows, width), jnp.bfloat16)

        @pl.when(vertex == last)
        def _():
            parts[:, last - 1] = jnp.zeros((spans, span_rows, width), jnp.bfloat16)

    pl.semaphore_wait(barrier, vertices - 1 + 1 + 2)

    def half_of(half):
        return slice(half * piece, (half + 1) * piece)

    def row_copy(span, half):
        rows = pl.ds(half * piece, piece)
        return pltpu.make_async_remote_copy(
            src_ref=result.at[span, rows], dst_ref=arrived.at[span, rows],
            send_sem=x_send.at[span, half], recv_sem=x_recv.at[span, half],
            device_id=(lax.rem(section + 1, sections), vertex, feat), device_id_type=MESH,
        )

    def chunk_rows(peer, half):
        return pl.ds(pl.multiple_of(peer * span_rows + half * piece, piece), piece)

    def part_copy(span, step, half):
        peer = lax.rem(vertex + step, vertices)
        return pltpu.make_async_remote_copy(
            src_ref=partial.at[span, chunk_rows(peer, half)],
            dst_ref=parts.at[span, step - 1, pl.ds(half * piece, piece)],
            send_sem=p_send.at[span, step - 1, half], recv_sem=p_recv.at[span, step - 1, half],
            device_id=(section, peer, feat), device_id_type=MESH,
        )

    def pass_copy(span, half):
        far = jnp.where(vertex == 0, last, 0)
        near = jnp.where(vertex == 0, 1, last - 1)
        return pltpu.make_async_remote_copy(
            src_ref=partial.at[span, chunk_rows(far, half)],
            dst_ref=passing.at[span, pl.ds(half * piece, piece)],
            send_sem=h_send.at[span, half], recv_sem=h_recv.at[span, half],
            device_id=(section, near, feat), device_id_type=MESH,
        )

    def support_copy(span, half):
        rows = pl.ds(half * piece, piece)
        return pltpu.make_async_remote_copy(
            src_ref=support.at[span, rows], dst_ref=other.at[span, rows],
            send_sem=s_send.at[span, half], recv_sem=s_recv.at[span, half],
            device_id=(section, vertex, partner), device_id_type=MESH,
        )

    at_end = (vertex == 0) | (vertex == last)

    def is_direct(step):
        if not relayed:
            return vertex >= 0
        peer = lax.rem(vertex + step, vertices)
        ends = ((vertex == 0) & (peer == last)) | ((vertex == last) & (peer == 0))
        inner = ((vertex == 1) & (peer == last)) | ((vertex == last - 1) & (peer == 0))
        return jnp.logical_not(ends | inner)

    def is_sent(step):
        if not relayed:
            return vertex >= 0
        peer = lax.rem(vertex + step, vertices)
        return jnp.logical_not(((vertex == 0) & (peer == last)) | ((vertex == last) & (peer == 0)))

    def is_received(step):
        if not relayed:
            return vertex >= 0
        source = lax.rem(vertex + vertices - step, vertices)
        return jnp.logical_not(((vertex == 0) & (source == last)) | ((vertex == last) & (source == 0)))

    def local(span, leading):
        mine = slice(span * span_rows, (span + 1) * span_rows)
        used = (span + 1) * span_rows

        def clear(i, _):
            first = pl.multiple_of(i * chunk, chunk)
            here = pl.ds(first, chunk)
            hot = chosen(ids_ref[span : span + 1, :], chunk, first)
            select_ref[here, mine] = hot.astype(jnp.bfloat16)
            taken = jnp.max(hot, axis=1, keepdims=True) > 0.5
            filler = features_ref[here, :].astype(jnp.float32) if leading else 0.0
            kept_ref[here, :] = jnp.where(taken, filler, kept_ref[here, :].astype(jnp.float32)).astype(jnp.bfloat16)
            return 0

        lax.fori_loop(0, owned // chunk, clear, 0)
        load_dense(span).wait()

        def multiply(i, _):
            here = pl.ds(pl.multiple_of(i * group, group), group)
            block = dense[span % 2, here, :]
            product = jnp.dot(block, kept_ref[...], preferred_element_type=jnp.float32)
            if leading:
                partial[span, here, :] = product.astype(jnp.bfloat16)
            else:
                base_ref[span, here, :] = product
                picks_ref[span, here, :used] = jnp.dot(
                    block, select_ref[:, :used], preferred_element_type=jnp.float32
                ).astype(jnp.bfloat16)
            return 0

        lax.fori_loop(0, rows_whole // group, multiply, 0)
        if span + 2 < spans:
            load_dense(span + 2).start()

    def gather():
        initial_ref[...] = lax.dot_general(
            select_ref[...], features_ref[...], (((0,), (0,)), ((), ())), preferred_element_type=jnp.float32
        ).astype(jnp.bfloat16)

    def earlier(span):
        used = span * span_rows

        def add(i, _):
            here = pl.ds(pl.multiple_of(i * group, group), group)
            base_ref[span, here, :] += jnp.dot(
                picks_ref[span, here, :used], fresh_ref[:used, :], preferred_element_type=jnp.float32
            )
            return 0

        lax.fori_loop(0, rows_whole // group, add, 0)

    def scatter(span):
        mine = slice(span * span_rows, (span + 1) * span_rows)
        @pl.when(section > 0)
        def _():
            for half in range(halves):
                row_copy(span, half).wait_recv()
            fresh_ref[mine, :] = arrived[span]


        def compute(peer):
            here = pl.ds(pl.multiple_of(peer * span_rows, span_rows), span_rows)
            total = base_ref[span, here, :] + jnp.dot(
                picks_ref[span, here, mine], fresh_ref[mine, :], preferred_element_type=jnp.float32
            )
            partial[span, here, :] = total.astype(jnp.bfloat16)

        if relayed:
            @pl.when(at_end & (section > 0))
            def _():
                compute(jnp.where(vertex == 0, last, 0))

            @pl.when(at_end)
            def _():
                for half in range(halves):
                    pass_copy(span, half).start()

        for step in range(1, vertices):
            @pl.when(is_sent(step) & (section > 0))
            def _(step=step):
                compute(lax.rem(vertex + step, vertices))

            @pl.when(is_direct(step))
            def _(step=step):
                part_copy(span, step, 0).start()

        for half in range(1, halves):
            for step in range(1, vertices):
                @pl.when(is_direct(step))
                def _(step=step, half=half):
                    part_copy(span, step, half).start()

        @pl.when(section > 0)
        def _():
            compute(vertex)

    def pass_on(span):
        if relayed:
            for who, step in ((1, last - 1), (last - 1, 2)):
                @pl.when(vertex == who)
                def _(who=who, step=step):
                    far = last if who == 1 else 0
                    for half in range(halves):
                        pass_copy(span, half).wait_recv()
                        here = pl.ds(far * span_rows + half * piece, piece)
                        partial[span, here, :] = (
                            partial[span, here, :].astype(jnp.float32)
                            + passing[span, half_of(half), :].astype(jnp.float32)
                        ).astype(jnp.bfloat16)
                        part_copy(span, step, half).start()

    def finish(span, half):
        total = partial[span, chunk_rows(vertex, half), :].astype(jnp.float32)
        for step in range(1, vertices):
            @pl.when(is_received(step))
            def _(step=step):
                part_copy(span, step, half).wait_recv()

        for step in range(1, vertices):
            total += parts[span, step - 1, half_of(half), :].astype(jnp.float32)
        mixed = (
            (1.0 - RESIDUAL_SHARE) * total
            + RESIDUAL_SHARE * initial_ref[pl.ds(span * span_rows + half * piece, piece), :].astype(jnp.float32)
        ).astype(jnp.bfloat16)
        support[span, half_of(half), :] = mixed
        support_copy(span, half).start()
        mine = pl.ds(pl.multiple_of(feat * width, width), width)
        theirs = pl.ds(pl.multiple_of(partner * width, width), width)
        projected = jnp.dot(mixed, weight_ref[mine, :], preferred_element_type=jnp.float32)
        support_copy(span, half).wait_recv()
        projected += jnp.dot(other[span, half_of(half), :], weight_ref[theirs, :], preferred_element_type=jnp.float32)
        rows = jnp.maximum((1.0 - beta) * mixed.astype(jnp.float32) + beta * projected, 0.0).astype(jnp.bfloat16)
        result[span, half_of(half), :] = rows
        out_ref[span, half_of(half), :] = rows

        @pl.when(section < sections - 1)
        def _():
            row_copy(span, half).start()

    def finish_all(span):
        for half in range(halves):
            finish(span, half)

    load_kept.wait()
    load_features.wait()

    @pl.when(section == 0)
    def _():
        for span in range(spans):
            local(span, True)
            scatter(span)
            if span:
                pass_on(span - 1)
        gather()
        load_weight.wait()
        for span in range(spans - 1):
            finish_all(span)
            if span == 0:
                pass_on(spans - 1)

    @pl.when(section > 0)
    def _():
        for span in range(spans):
            local(span, False)
        gather()
        load_weight.wait()
        for span in range(spans):
            scatter(span)
            pass_on(span)
            if span:
                finish_all(span - 1)
            if span + 1 < spans:
                earlier(span + 1)

    def merge(i, _):
        here = pl.ds(pl.multiple_of(i * chunk, chunk), chunk)
        moved = jnp.dot(select_ref[here, :], fresh_ref[...], preferred_element_type=jnp.float32)
        kept_ref[here, :] = (kept_ref[here, :].astype(jnp.float32) + moved).astype(jnp.bfloat16)
        return 0

    @pl.when(section > 0)
    def _():
        lax.fori_loop(0, owned // chunk, merge, 0)

    store = pltpu.make_async_copy(kept_ref, table_hbm, table_sem)
    store.start()
    finish_all(spans - 1)

    for span in range(spans):
        for half in range(halves):
            support_copy(span, half).wait_send()
            for step in range(1, vertices):
                @pl.when(is_sent(step))
                def _(span=span, step=step, half=half):
                    part_copy(span, step, half).wait_send()

            if relayed:
                @pl.when(at_end)
                def _(span=span, half=half):
                    pass_copy(span, half).wait_send()

            @pl.when(section < sections - 1)
            def _(span=span, half=half):
                row_copy(span, half).wait_send()

    store.wait()

LINE = 4


def write(rows_ref, table_ref, rows_out, table_out, sem):
    chunks = sem.shape[0] - 1
    size = table_ref.shape[0] // chunks
    moves = [pltpu.make_async_copy(rows_ref, rows_out, sem.at[chunks])]
    for i in range(chunks):
        here = pl.ds(i * size, size)
        moves.append(pltpu.make_async_copy(table_ref.at[here], table_out.at[here], sem.at[i]))
    for move in moves:
        move.start()
    for move in moves:
        move.wait()


def stream(
    sections, vertices, feats,
    rows_ref, cols_ref, counts_ref, ids_ref, tiles_hbm, weight_hbm, kept_hbm, features_hbm, out_ref, kept_ref,
    tiles, left, right, right_select, base_ref, picks_ref, weight_ref, features_ref, select_ref, taken_ref, initial_ref,
    fresh_ref, partial, parts, passing, transit, support, other, result,
    load_sem, x_send, x_recv, p_send, p_recv, h_send, h_recv, s_send, s_recv, d_send, d_recv, t_send,
):
    section = lax.axis_index("section")
    vertex = lax.axis_index("vertex")
    feat = lax.axis_index("feat")
    spans, span_rows, width = result.shape
    pieces = x_send.shape[1]
    part = width // pieces
    wide = min(256, width)
    slots, side = tiles.shape[1:3]
    row_blocks = left.shape[0] // side
    rows_all = spans * span_rows
    last = vertices - 1
    partner = lax.rem(feat + 1, feats)
    beside = lax.rem(section + sections // 2, sections)
    opposite = lax.rem(vertex + last - 1, vertices)
    beta = jnp.log(BETA_SCALE / (section + 1).astype(jnp.float32) + 1.0)
    col_blocks = kept_ref.shape[0]

    def load_tiles(span):
        return pltpu.make_async_copy(tiles_hbm.at[span], tiles.at[span], load_sem.at[span])

    quarters = min(4, col_blocks)
    quarter = col_blocks // quarters

    def load_table(q):
        here = pl.ds(q * quarter, quarter)
        return (
            pltpu.make_async_copy(kept_hbm.at[here], kept_ref.at[here], load_sem.at[spans + 1 + q]),
            pltpu.make_async_copy(features_hbm.at[here], features_ref.at[here], load_sem.at[spans + 1 + quarters + q]),
        )

    load_weight = pltpu.make_async_copy(weight_hbm, weight_ref, load_sem.at[spans])
    load_tiles(0).start()
    for q in range(quarters):
        for copy in load_table(q):
            copy.start()
    for span in range(1, spans):
        load_tiles(span).start()
    load_weight.start()

    barrier = pltpu.get_barrier_semaphore()
    for step in range(1, vertices):
        peer = lax.rem(vertex + step, vertices)
        pl.semaphore_signal(barrier, inc=1, device_id=(section, peer, feat), device_id_type=MESH)
    pl.semaphore_signal(barrier, inc=1, device_id=(section, vertex, partner), device_id_type=MESH)
    for step in (1, sections - 1):
        peer = lax.rem(section + step, sections)
        pl.semaphore_signal(barrier, inc=1, device_id=(peer, vertex, feat), device_id_type=MESH)
    for peer in (vertex, opposite):
        pl.semaphore_signal(barrier, inc=1, device_id=(beside, peer, feat), device_id_type=MESH)

    def meet():
        pl.semaphore_wait(barrier, vertices - 1 + 1 + 2 + 2)

    at_end = (vertex == 0) | (vertex == last)

    @pl.when(vertex == 0)
    def _():
        parts[:, 0] = jnp.zeros((spans, span_rows, width), jnp.bfloat16)

    @pl.when(vertex == last)
    def _():
        parts[:, last - 1] = jnp.zeros((spans, span_rows, width), jnp.bfloat16)

    def columns(j):
        return slice(j * part, (j + 1) * part)

    def lanes(j):
        return pl.ds(j * part, part)

    def span_of(span):
        return slice(span * span_rows, (span + 1) * span_rows)

    def row_copy(span, j):
        return pltpu.make_async_remote_copy(
            src_ref=result.at[span, :, lanes(j)],
            dst_ref=fresh_ref.at[pl.ds(span * span_rows, span_rows), lanes(j)],
            send_sem=x_send.at[span, j], recv_sem=x_recv.at[span, j],
            device_id=(lax.rem(section + 1, sections), vertex, feat), device_id_type=MESH,
        )

    def rows_of(peer):
        return pl.ds(pl.multiple_of(peer * span_rows, span_rows), span_rows)

    def part_copy(span, step, j):
        peer = lax.rem(vertex + step, vertices)
        return pltpu.make_async_remote_copy(
            src_ref=partial.at[span, rows_of(peer), lanes(j)], dst_ref=parts.at[span, step - 1, :, lanes(j)],
            send_sem=p_send.at[span, step - 1, j], recv_sem=p_recv.at[span, step - 1, j],
            device_id=(section, peer, feat), device_id_type=MESH,
        )

    def pass_copy(span, j):
        far = jnp.where(vertex == 0, last, 0)
        near = jnp.where(vertex == 0, 1, last - 1)
        return pltpu.make_async_remote_copy(
            src_ref=partial.at[span, rows_of(far), lanes(j)], dst_ref=passing.at[span, :, lanes(j)],
            send_sem=h_send.at[span, j], recv_sem=h_recv.at[span, j],
            device_id=(section, near, feat), device_id_type=MESH,
        )

    def detour_copy(span, j):
        return pltpu.make_async_remote_copy(
            src_ref=partial.at[span, rows_of(opposite), lanes(j)], dst_ref=transit.at[span, :, lanes(j)],
            send_sem=d_send.at[span, j], recv_sem=d_recv.at[span, j],
            device_id=(beside, vertex, feat), device_id_type=MESH,
        )

    def return_copy(span, j):
        return pltpu.make_async_remote_copy(
            src_ref=transit.at[span, :, lanes(j)], dst_ref=parts.at[span, last - 2, :, lanes(j)],
            send_sem=t_send.at[span, j], recv_sem=p_recv.at[span, last - 2, j],
            device_id=(beside, opposite, feat), device_id_type=MESH,
        )

    def support_copy(span, j):
        return pltpu.make_async_remote_copy(
            src_ref=support.at[span, :, lanes(j)], dst_ref=other.at[span, :, lanes(j)],
            send_sem=s_send.at[span, j], recv_sem=s_recv.at[span, j],
            device_id=(section, vertex, partner), device_id_type=MESH,
        )

    def ends_meet(here, there):
        return ((here == 0) & (there == last)) | ((here == last) & (there == 0))

    def is_sent(step):
        far = ends_meet(vertex, lax.rem(vertex + step, vertices))
        return jnp.logical_not(far | at_end) if step == last - 1 else jnp.logical_not(far)

    def is_received(step):
        return jnp.logical_not(ends_meet(lax.rem(vertex + vertices - step, vertices), vertex))

    def choose():
        def one_hot(i, _):
            for span in range(spans):
                hot = chosen(ids_ref[span : span + 1, :], side, i * side)
                select_ref[i, :, span_of(span)] = hot.astype(jnp.bfloat16)
            return 0

        lax.fori_loop(0, col_blocks, one_hot, 0)

    def count(span):
        taken_ref[span] = jnp.dot(
            select_ref[...].reshape(col_blocks * side, rows_all)[:, span_of(span)],
            jnp.ones((span_rows, side), jnp.bfloat16),
            preferred_element_type=jnp.float32,
        ).astype(jnp.bfloat16).reshape(col_blocks, side, side)

    def mark(span, leading):
        def clear(i, _):
            taken = taken_ref[span, i]
            rest = 1.0 - taken
            for first in range(0, width, side):
                group = slice(first, first + side)
                row = kept_ref[i, :, group] * rest
                kept_ref[i, :, group] = row + features_ref[i, :, group] * taken if leading else row
            return 0

        if span:
            lax.fori_loop(0, col_blocks, clear, 0)
        else:
            for q in range(quarters):
                for copy in load_table(q):
                    copy.wait()
                lax.fori_loop(q * quarter, (q + 1) * quarter, clear, 0)

    def lay_left(span):
        load_tiles(span).wait()
        lives = jnp.full((side, side), counts_ref[0, span], jnp.int32)

        def place(t, _):
            here = pl.ds(pl.multiple_of(t * side, side), side)
            tile = tiles[span, t].astype(jnp.float32)
            rows = jnp.where(lives > t, jnp.full(tile.shape, rows_ref[span, t], jnp.int32), row_blocks)
            for block in range(row_blocks):
                left[block * side : (block + 1) * side, here] = jnp.where(rows == block, tile, 0.0).astype(left.dtype)
            return 0

        lax.fori_loop(0, slots, place, 0)

    def lay_right(span, leading):
        def place(t, _):
            col = cols_ref[span, t]
            here = pl.ds(pl.multiple_of(t * side, side), side)
            right[here, :] = kept_ref[col]
            if not leading:
                right_select[here, :] = select_ref[col]
            return 0

        lax.fori_loop(0, slots, place, 0)

    def prepare_span(span, leading):
        if span:
            count(span)
            lay_left(span)
        mark(span, leading)
        lay_right(span, leading)

    def gather():
        initial_ref[...] = lax.dot_general(
            select_ref[...].reshape(col_blocks * side, rows_all),
            features_ref[...].reshape(col_blocks * side, width),
            (((0,), (0,)), ((), ())),
            preferred_element_type=jnp.float32,
        ).astype(jnp.bfloat16)

    def groups():
        return [slice(first, first + wide) for first in range(0, width, wide)]

    def product(group):
        return jnp.dot(left[...], right[:, group], preferred_element_type=jnp.float32)

    def first_sums(span, j):
        if j * part % wide == 0:
            group = slice(j * part, j * part + wide)
            partial[span, :, group] = product(group).astype(jnp.bfloat16)

    def later_sums(span, j):
        row_copy(span, j).wait_recv()
        partial[span, :, columns(j)] = (
            base_ref[span, :, columns(j)]
            + jnp.dot(
                picks_ref[span, :, span_of(span)], fresh_ref[span_of(span), columns(j)],
                preferred_element_type=jnp.float32,
            )
        ).astype(jnp.bfloat16)

    def scatter(span, sums):
        for j in range(pieces):
            sums(span, j)

            @pl.when(at_end)
            def _(j=j):
                pass_copy(span, j).start()
                detour_copy(span, j).start()

            @pl.when(jnp.logical_not(at_end))
            def _(j=j):
                for step in (1, last):
                    part_copy(span, step, j).start()

        for j in range(pieces):
            for step in (1, last):
                @pl.when(at_end & is_sent(step))
                def _(step=step, j=j):
                    part_copy(span, step, j).start()

    def pass_on(span):
        for who, step in ((1, last - 1), (last - 1, 2)):
            @pl.when(vertex == who)
            def _(who=who, step=step):
                far = last if who == 1 else 0
                here = pl.ds(far * span_rows, span_rows)
                for j in range(pieces):
                    pass_copy(span, j).wait_recv()
                    partial[span, here, columns(j)] = (
                        partial[span, here, columns(j)].astype(jnp.float32)
                        + passing[span, :, columns(j)].astype(jnp.float32)
                    ).astype(jnp.bfloat16)
                    part_copy(span, step, j).start()

    def hand_on(span):
        @pl.when(at_end)
        def _():
            for j in range(pieces):
                detour_copy(span, j).wait_recv()
                return_copy(span, j).start()

    def keep(span):
        used = (span + 1) * span_rows
        for group in groups():
            base_ref[span, :, group] = product(group)
        picks_ref[span, :, :used] = jnp.dot(
            left[...], right_select[:, :used], preferred_element_type=jnp.float32
        ).astype(jnp.bfloat16)

    def earlier(span):
        used = span * span_rows
        for group in groups():
            base_ref[span, :, group] += jnp.dot(
                picks_ref[span, :, :used], fresh_ref[:used, group], preferred_element_type=jnp.float32
            )

    def weight_rows(which):
        return pl.ds(pl.multiple_of(which * width, width), width)

    def finish(span):
        halves = groups()
        whole = [0.0] * len(halves)
        for half in halves:
            here = range(half.start // part, half.stop // part)
            for j in here:
                for step in range(1, vertices):
                    @pl.when(is_received(step))
                    def _(step=step, j=j):
                        part_copy(span, step, j).wait_recv()

                total = partial[span, rows_of(vertex), columns(j)].astype(jnp.float32)
                for step in range(1, vertices):
                    total += parts[span, step - 1, :, columns(j)].astype(jnp.float32)
                support[span, :, columns(j)] = (
                    (1.0 - RESIDUAL_SHARE) * total
                    + RESIDUAL_SHARE * initial_ref[span_of(span), columns(j)].astype(jnp.float32)
                ).astype(jnp.bfloat16)
                support_copy(span, j).start()

        def project(source, which, half, group):
            rows = pl.ds(pl.multiple_of(which * width + half.start, wide), wide)
            return jnp.dot(source[span, :, half], weight_ref[rows, group], preferred_element_type=jnp.float32)

        for k, group in enumerate(halves):
            for half in halves:
                whole[k] += project(support, feat, half, group)
        for half in halves:
            for j in range(half.start // part, half.stop // part):
                support_copy(span, j).wait_recv()
            if half is not halves[-1]:
                for k, group in enumerate(halves):
                    whole[k] += project(other, partner, half, group)
        for k, group in enumerate(halves):
            rows = jnp.maximum(
                (1.0 - beta) * support[span, :, group].astype(jnp.float32)
                + beta * (whole[k] + project(other, partner, halves[-1], group)),
                0.0,
            ).astype(jnp.bfloat16)
            result[span, :, group] = rows

            @pl.when(section < sections - 1)
            def _(group=group):
                for j in range(group.start // part, group.stop // part):
                    row_copy(span, j).start()

            out_ref[span, :, group] = rows

    choose()
    count(0)
    lay_left(0)

    @pl.when(section == 0)
    def _():
        for span in range(spans):
            prepare_span(span, True)
            if span == 0:
                meet()
            scatter(span, first_sums)
            if span == min(1, spans - 1):
                gather()
                load_weight.wait()
            if span == 1:
                pass_on(0)
        for span in range(spans - 1):
            finish(span)
            pass_on(span + 1)

    @pl.when(section > 0)
    def _():
        for span in range(spans):
            prepare_span(span, False)
            keep(span)
            if span == 0:
                meet()

            @pl.when(section == sections // 2)
            def _(span=span):
                hand_on(span)

        gather()
        load_weight.wait()

        @pl.when(section > sections // 2)
        def _():
            for span in range(spans):
                hand_on(span)

        for span in range(spans):
            scatter(span, later_sums)
            if span:
                finish(span - 1)
            pass_on(span)
            if span + 1 < spans:
                earlier(span + 1)

    def merge():
        blocks = max(1, 512 // side)
        for first in range(0, col_blocks, blocks):
            picked = select_ref[first : first + blocks].reshape(blocks * side, rows_all)
            for group in groups():
                moved = jnp.dot(picked, fresh_ref[:, group], preferred_element_type=jnp.float32).astype(jnp.bfloat16)
                kept_ref[first : first + blocks, :, group] += moved.reshape(blocks, side, wide)

    @pl.when(section > 0)
    def _():
        merge()

    finish(spans - 1)

    @pl.when(section < sections // 2)
    def _():
        for span in range(spans):
            hand_on(span)

    for span in range(spans):
        for j in range(pieces):
            support_copy(span, j).wait_send()
            for step in range(1, vertices):
                @pl.when(is_sent(step))
                def _(span=span, step=step, j=j):
                    part_copy(span, step, j).wait_send()

            @pl.when(at_end)
            def _(span=span, j=j):
                pass_copy(span, j).wait_send()
                detour_copy(span, j).wait_send()
                return_copy(span, j).wait_send()

            @pl.when(section < sections - 1)
            def _(span=span, j=j):
                row_copy(span, j).wait_send()


def deliver(rows_hbm, table_hbm, rows_out, table_out, rows_ref, table_ref, in_sem, out_sem):
    chunks = in_sem.shape[0] - 1
    size = table_ref.shape[0] // chunks
    moves = []
    for i in range(chunks):
        here = pl.ds(i * size, size)
        moves.append((
            pltpu.make_async_copy(table_hbm.at[here], table_ref.at[here], in_sem.at[i]),
            pltpu.make_async_copy(table_ref.at[here], table_out.at[here], out_sem.at[i]),
        ))
    moves.append((
        pltpu.make_async_copy(rows_hbm, rows_ref, in_sem.at[chunks]),
        pltpu.make_async_copy(rows_ref, rows_out, out_sem.at[chunks]),
    ))
    for get, _ in moves:
        get.start()
    for get, put in moves:
        get.wait()
        put.start()
    for _, put in moves:
        put.wait()


def long_line(sizes, features, history, weights, tile_values, tile_rows, tile_cols, tile_counts, span_ids):
    sections, vertices, feats = sizes
    spans, span_rows = span_ids.shape
    owned, width = features.shape
    rows_whole = span_rows * vertices
    rows_all = spans * span_rows
    vmem = pl.BlockSpec(memory_space=pltpu.VMEM)
    smem = pl.BlockSpec(memory_space=pltpu.SMEM)
    anywhere = pl.BlockSpec(memory_space=pl.ANY)

    dense = pl.pallas_call(
        prepare,
        name="prepare",
        out_shape=jax.ShapeDtypeStruct((spans, rows_whole, owned), jnp.bfloat16),
        in_specs=[smem, smem, smem, vmem],
        out_specs=anywhere,
        scratch_shapes=[
            pltpu.VMEM((spans, rows_whole, owned), jnp.bfloat16),
            pltpu.SemaphoreType.DMA((spans,)),
        ],
        compiler_params=pltpu.CompilerParams(vmem_limit_bytes=VMEM_BYTES),
    )(tile_rows, tile_cols, tile_counts.reshape(1, spans), tile_values)

    rows_type = jax.ShapeDtypeStruct((spans, span_rows, width), jnp.bfloat16)
    table_type = jax.ShapeDtypeStruct((owned, width), jnp.bfloat16)
    block = pltpu.VMEM(rows_type.shape, jnp.bfloat16)
    halves = 2
    pair = pltpu.SemaphoreType.DMA((spans, halves))
    layer_rows, table_new = pl.pallas_call(
        functools.partial(relay, sections, vertices, feats),
        name="relay",
        out_shape=(rows_type, table_type),
        in_specs=[anywhere, vmem, anywhere, anywhere, anywhere],
        out_specs=(vmem, anywhere),
        scratch_shapes=[
            pltpu.VMEM((min(2, spans), rows_whole, owned), jnp.bfloat16),
            pltpu.VMEM((spans, rows_whole, width), jnp.float32),
            pltpu.VMEM((spans, rows_whole, rows_all), jnp.bfloat16),
            pltpu.VMEM(weights.shape[1:], weights.dtype),
            pltpu.VMEM((owned, width), jnp.bfloat16),
            pltpu.VMEM((owned, width), jnp.bfloat16),
            pltpu.VMEM((owned, rows_all), jnp.bfloat16),
            pltpu.VMEM((rows_all, width), jnp.bfloat16),
            pltpu.VMEM((rows_all, width), jnp.bfloat16),
            block,
            pltpu.VMEM((spans, rows_whole, width), jnp.bfloat16),
            pltpu.VMEM((spans, vertices - 1, span_rows, width), jnp.bfloat16),
            block, block, block, block,
            pltpu.SemaphoreType.DMA((spans + 3,)),
            pltpu.SemaphoreType.DMA,
            pair, pair,
            pltpu.SemaphoreType.DMA((spans, vertices - 1, halves)),
            pltpu.SemaphoreType.DMA((spans, vertices - 1, halves)),
            pair, pair, pair, pair,
        ],
        compiler_params=pltpu.CompilerParams(
            vmem_limit_bytes=VMEM_BYTES, collective_id=0, has_side_effects=True
        ),
    )(dense, span_ids, weights[0], history[0], features)

    table_type = jax.ShapeDtypeStruct((owned, width), jnp.bfloat16)
    chunks = 8
    return pl.pallas_call(
        deliver,
        name="deliver",
        out_shape=(rows_type, table_type),
        in_specs=[anywhere, anywhere],
        out_specs=(anywhere, anywhere),
        scratch_shapes=[
            pltpu.VMEM(rows_type.shape, jnp.bfloat16),
            pltpu.VMEM(table_type.shape, jnp.bfloat16),
            pltpu.SemaphoreType.DMA((chunks + 1,)),
            pltpu.SemaphoreType.DMA((chunks + 1,)),
        ],
        compiler_params=pltpu.CompilerParams(vmem_limit_bytes=VMEM_BYTES),
    )(layer_rows, table_new)


def short_line(sizes, features, history, weights, tile_values, tile_rows, tile_cols, tile_counts, span_ids):
    sections, vertices, feats = sizes
    spans, span_rows = span_ids.shape
    slots, side = tile_values.shape[1:3]
    owned, width = features.shape
    rows_whole = span_rows * vertices
    rows_all = spans * span_rows
    pieces = 4
    vmem = pl.BlockSpec(memory_space=pltpu.VMEM)
    smem = pl.BlockSpec(memory_space=pltpu.SMEM)
    anywhere = pl.BlockSpec(memory_space=pl.ANY)
    block = pltpu.VMEM((spans, span_rows, width), jnp.bfloat16)
    pair = pltpu.SemaphoreType.DMA((spans, pieces))
    triple = pltpu.SemaphoreType.DMA((spans, vertices - 1, pieces))
    table = history[0].reshape(owned // side, side, width)
    layer_rows, table_new = pl.pallas_call(
        functools.partial(stream, sections, vertices, feats),
        name="stream",
        out_shape=(
            pltpu.VMEM((spans, span_rows, width), jnp.bfloat16),
            pltpu.VMEM(table.shape, jnp.bfloat16),
        ),
        in_specs=[smem, smem, smem, vmem, anywhere, anywhere, anywhere, anywhere],
        out_specs=(vmem, vmem),
        scratch_shapes=[
            pltpu.VMEM(tile_values.shape, jnp.bfloat16),
            pltpu.VMEM((rows_whole, slots * side), jnp.bfloat16),
            pltpu.VMEM((slots * side, width), jnp.bfloat16),
            pltpu.VMEM((slots * side, rows_all), jnp.bfloat16),
            pltpu.VMEM((spans, rows_whole, width), jnp.float32),
            pltpu.VMEM((spans, rows_whole, rows_all), jnp.bfloat16),
            pltpu.VMEM(weights.shape[1:], weights.dtype),
            pltpu.VMEM(table.shape, jnp.bfloat16),
            pltpu.VMEM((owned // side, side, rows_all), jnp.bfloat16),
            pltpu.VMEM((spans, owned // side, side, side), jnp.bfloat16),
            pltpu.VMEM((rows_all, width), jnp.bfloat16),
            pltpu.VMEM((rows_all, width), jnp.bfloat16),
            pltpu.VMEM((spans, rows_whole, width), jnp.bfloat16),
            pltpu.VMEM((spans, vertices - 1, span_rows, width), jnp.bfloat16),
            block, block, block, block, block,
            pltpu.SemaphoreType.DMA((spans + 9,)),
            pair, pair, triple, triple, pair, pair, pair, pair, pair, pair, pair,
        ],
        compiler_params=pltpu.CompilerParams(
            vmem_limit_bytes=VMEM_BYTES, collective_id=0, has_side_effects=True
        ),
    )(tile_rows, tile_cols, tile_counts.reshape(1, spans), span_ids, tile_values, weights[0], table,
      features.reshape(table.shape))
    chunks = 4
    layer_rows, table_new = pl.pallas_call(
        write,
        name="write",
        out_shape=(
            jax.ShapeDtypeStruct((spans, span_rows, width), jnp.bfloat16),
            jax.ShapeDtypeStruct(table.shape, jnp.bfloat16),
        ),
        in_specs=[vmem, vmem],
        out_specs=(anywhere, anywhere),
        scratch_shapes=[pltpu.SemaphoreType.DMA((chunks + 1,))],
        compiler_params=pltpu.CompilerParams(vmem_limit_bytes=VMEM_BYTES),
    )(
        pltpu.with_memory_space_constraint(layer_rows, pltpu.VMEM),
        pltpu.with_memory_space_constraint(table_new, pltpu.VMEM),
    )
    return layer_rows, table_new.reshape(owned, width)


def shards(sizes, *arrays):
    layers = short_line if sizes[0] == sizes[1] == LINE else long_line
    layer_rows, table_new = layers(sizes, *arrays)
    return (layer_rows[None], table_new[None])


def solution(mesh):
    placed = (
        P("vertex", "feat"),
        P("section", "vertex", "feat"),
        P("section", None, "feat"),
        P(None, "vertex", None, None),
        P(None, "vertex"),
        P(None, "vertex"),
        P(None, "vertex"),
        P(None, "vertex"),
    )
    sizes = (mesh.shape["section"], mesh.shape["vertex"], mesh.shape["feat"])
    return jax.shard_map(
        functools.partial(shards, sizes),
        mesh=mesh,
        in_specs=placed,
        out_specs=(P("section", None, "vertex", "feat"), P("section", "vertex", "feat")),
        check_vma=False,
    )
```

```python
import functools

import jax
import jax.numpy as jnp
from jax import lax
from jax.experimental import pallas as pl
from jax.experimental.pallas import tpu as pltpu
from jax.sharding import PartitionSpec as P

RESIDUAL_SHARE = 0.2
BETA_SCALE = 0.5
MESH = pl.DeviceIdType.MESH
VMEM_BYTES = 60_000 * 1024


def chosen(ids_row, rows, first=0):
    shape = (rows, ids_row.shape[1])
    return (lax.broadcasted_iota(jnp.int32, shape, 0) + first == ids_row).astype(jnp.float32)


def prepare(rows_ref, cols_ref, counts_ref, tiles_ref, dense_hbm, dense, dense_sem):
    spans, _, side, _ = tiles_ref.shape
    copies = []
    for span in range(spans):
        dense[span] = jnp.zeros(dense.shape[1:], dense.dtype)

        def place(t, _, span=span):
            row = pl.multiple_of(rows_ref[span, t] * side, side)
            col = pl.multiple_of(cols_ref[span, t] * side, side)
            dense[span, pl.ds(row, side), pl.ds(col, side)] = tiles_ref[span, t]
            return 0

        lax.fori_loop(0, counts_ref[0, span], place, 0)
        copies.append(pltpu.make_async_copy(dense.at[span], dense_hbm.at[span], dense_sem.at[span]))
        copies[-1].start()
    for copy in copies:
        copy.wait()


def relay(
    sections, vertices, feats,
    dense_hbm, ids_ref, weight_hbm, kept_hbm, features_hbm, out_ref, table_hbm,
    dense, base_ref, picks_ref, weight_ref, kept_ref, features_ref, select_ref, initial_ref, fresh_ref,
    arrived, partial, parts, passing, support, other, result,
    load_sem, table_sem, x_send, x_recv, p_send, p_recv, h_send, h_recv, s_send, s_recv,
):
    section = lax.axis_index("section")
    vertex = lax.axis_index("vertex")
    feat = lax.axis_index("feat")
    spans, span_rows, width = arrived.shape
    last = vertices - 1
    partner = lax.rem(feat + 1, feats)
    beta = jnp.log(BETA_SCALE / (section + 1).astype(jnp.float32) + 1.0)
    halves = 2
    piece = span_rows // halves
    relayed = vertices > 3

    rows_whole = dense.shape[1]
    owned = kept_ref.shape[0]
    group = min(512, rows_whole)
    chunk = min(256, owned)

    def load_dense(span):
        return pltpu.make_async_copy(dense_hbm.at[span], dense.at[span % 2], load_sem.at[span])

    load_weight = pltpu.make_async_copy(weight_hbm, weight_ref, load_sem.at[spans])
    load_kept = pltpu.make_async_copy(kept_hbm, kept_ref, load_sem.at[spans + 1])
    load_features = pltpu.make_async_copy(features_hbm, features_ref, load_sem.at[spans + 2])
    load_kept.start()
    load_features.start()
    for span in range(min(2, spans)):
        load_dense(span).start()
    load_weight.start()

    barrier = pltpu.get_barrier_semaphore()
    for step in range(1, vertices):
        peer = lax.rem(vertex + step, vertices)
        pl.semaphore_signal(barrier, inc=1, device_id=(section, peer, feat), device_id_type=MESH)
    pl.semaphore_signal(barrier, inc=1, device_id=(section, vertex, partner), device_id_type=MESH)
    for step in (1, sections - 1):
        peer = lax.rem(section + step, sections)
        pl.semaphore_signal(barrier, inc=1, device_id=(peer, vertex, feat), device_id_type=MESH)
    if relayed:
        @pl.when(vertex == 0)
        def _():
            parts[:, 0] = jnp.zeros((spans, span_rows, width), jnp.bfloat16)

        @pl.when(vertex == last)
        def _():
            parts[:, last - 1] = jnp.zeros((spans, span_rows, width), jnp.bfloat16)

    pl.semaphore_wait(barrier, vertices - 1 + 1 + 2)

    def half_of(half):
        return slice(half * piece, (half + 1) * piece)

    def row_copy(span, half):
        rows = pl.ds(half * piece, piece)
        return pltpu.make_async_remote_copy(
            src_ref=result.at[span, rows], dst_ref=arrived.at[span, rows],
            send_sem=x_send.at[span, half], recv_sem=x_recv.at[span, half],
            device_id=(lax.rem(section + 1, sections), vertex, feat), device_id_type=MESH,
        )

    def chunk_rows(peer, half):
        return pl.ds(pl.multiple_of(peer * span_rows + half * piece, piece), piece)

    def part_copy(span, step, half):
        peer = lax.rem(vertex + step, vertices)
        return pltpu.make_async_remote_copy(
            src_ref=partial.at[span, chunk_rows(peer, half)],
            dst_ref=parts.at[span, step - 1, pl.ds(half * piece, piece)],
            send_sem=p_send.at[span, step - 1, half], recv_sem=p_recv.at[span, step - 1, half],
            device_id=(section, peer, feat), device_id_type=MESH,
        )

    def pass_copy(span, half):
        far = jnp.where(vertex == 0, last, 0)
        near = jnp.where(vertex == 0, 1, last - 1)
        return pltpu.make_async_remote_copy(
            src_ref=partial.at[span, chunk_rows(far, half)],
            dst_ref=passing.at[span, pl.ds(half * piece, piece)],
            send_sem=h_send.at[span, half], recv_sem=h_recv.at[span, half],
            device_id=(section, near, feat), device_id_type=MESH,
        )

    def support_copy(span, half):
        rows = pl.ds(half * piece, piece)
        return pltpu.make_async_remote_copy(
            src_ref=support.at[span, rows], dst_ref=other.at[span, rows],
            send_sem=s_send.at[span, half], recv_sem=s_recv.at[span, half],
            device_id=(section, vertex, partner), device_id_type=MESH,
        )

    at_end = (vertex == 0) | (vertex == last)

    def is_direct(step):
        if not relayed:
            return vertex >= 0
        peer = lax.rem(vertex + step, vertices)
        ends = ((vertex == 0) & (peer == last)) | ((vertex == last) & (peer == 0))
        inner = ((vertex == 1) & (peer == last)) | ((vertex == last - 1) & (peer == 0))
        return jnp.logical_not(ends | inner)

    def is_sent(step):
        if not relayed:
            return vertex >= 0
        peer = lax.rem(vertex + step, vertices)
        return jnp.logical_not(((vertex == 0) & (peer == last)) | ((vertex == last) & (peer == 0)))

    def is_received(step):
        if not relayed:
            return vertex >= 0
        source = lax.rem(vertex + vertices - step, vertices)
        return jnp.logical_not(((vertex == 0) & (source == last)) | ((vertex == last) & (source == 0)))

    def local(span, leading):
        mine = slice(span * span_rows, (span + 1) * span_rows)
        used = (span + 1) * span_rows

        def clear(i, _):
            first = pl.multiple_of(i * chunk, chunk)
            here = pl.ds(first, chunk)
            hot = chosen(ids_ref[span : span + 1, :], chunk, first)
            select_ref[here, mine] = hot.astype(jnp.bfloat16)
            taken = jnp.max(hot, axis=1, keepdims=True) > 0.5
            filler = features_ref[here, :].astype(jnp.float32) if leading else 0.0
            kept_ref[here, :] = jnp.where(taken, filler, kept_ref[here, :].astype(jnp.float32)).astype(jnp.bfloat16)
            return 0

        lax.fori_loop(0, owned // chunk, clear, 0)
        load_dense(span).wait()

        def multiply(i, _):
            here = pl.ds(pl.multiple_of(i * group, group), group)
            block = dense[span % 2, here, :]
            product = jnp.dot(block, kept_ref[...], preferred_element_type=jnp.float32)
            if leading:
                partial[span, here, :] = product.astype(jnp.bfloat16)
            else:
                base_ref[span, here, :] = product
                picks_ref[span, here, :used] = jnp.dot(
                    block, select_ref[:, :used], preferred_element_type=jnp.float32
                ).astype(jnp.bfloat16)
            return 0

        lax.fori_loop(0, rows_whole // group, multiply, 0)
        if span + 2 < spans:
            load_dense(span + 2).start()

    def gather():
        initial_ref[...] = lax.dot_general(
            select_ref[...], features_ref[...], (((0,), (0,)), ((), ())), preferred_element_type=jnp.float32
        ).astype(jnp.bfloat16)

    def earlier(span):
        used = span * span_rows

        def add(i, _):
            here = pl.ds(pl.multiple_of(i * group, group), group)
            base_ref[span, here, :] += jnp.dot(
                picks_ref[span, here, :used], fresh_ref[:used, :], preferred_element_type=jnp.float32
            )
            return 0

        lax.fori_loop(0, rows_whole // group, add, 0)

    def scatter(span):
        mine = slice(span * span_rows, (span + 1) * span_rows)
        @pl.when(section > 0)
        def _():
            for half in range(halves):
                row_copy(span, half).wait_recv()
            fresh_ref[mine, :] = arrived[span]


        def compute(peer):
            here = pl.ds(pl.multiple_of(peer * span_rows, span_rows), span_rows)
            total = base_ref[span, here, :] + jnp.dot(
                picks_ref[span, here, mine], fresh_ref[mine, :], preferred_element_type=jnp.float32
            )
            partial[span, here, :] = total.astype(jnp.bfloat16)

        if relayed:
            @pl.when(at_end & (section > 0))
            def _():
                compute(jnp.where(vertex == 0, last, 0))

            @pl.when(at_end)
            def _():
                for half in range(halves):
                    pass_copy(span, half).start()

        for step in range(1, vertices):
            @pl.when(is_sent(step) & (section > 0))
            def _(step=step):
                compute(lax.rem(vertex + step, vertices))

            @pl.when(is_direct(step))
            def _(step=step):
                part_copy(span, step, 0).start()

        for half in range(1, halves):
            for step in range(1, vertices):
                @pl.when(is_direct(step))
                def _(step=step, half=half):
                    part_copy(span, step, half).start()

        @pl.when(section > 0)
        def _():
            compute(vertex)

    def pass_on(span):
        if relayed:
            for who, step in ((1, last - 1), (last - 1, 2)):
                @pl.when(vertex == who)
                def _(who=who, step=step):
                    far = last if who == 1 else 0
                    for half in range(halves):
                        pass_copy(span, half).wait_recv()
                        here = pl.ds(far * span_rows + half * piece, piece)
                        partial[span, here, :] = (
                            partial[span, here, :].astype(jnp.float32)
                            + passing[span, half_of(half), :].astype(jnp.float32)
                        ).astype(jnp.bfloat16)
                        part_copy(span, step, half).start()

    def finish(span, half):
        total = partial[span, chunk_rows(vertex, half), :].astype(jnp.float32)
        for step in range(1, vertices):
            @pl.when(is_received(step))
            def _(step=step):
                part_copy(span, step, half).wait_recv()

        for step in range(1, vertices):
            total += parts[span, step - 1, half_of(half), :].astype(jnp.float32)
        mixed = (
            (1.0 - RESIDUAL_SHARE) * total
            + RESIDUAL_SHARE * initial_ref[pl.ds(span * span_rows + half * piece, piece), :].astype(jnp.float32)
        ).astype(jnp.bfloat16)
        support[span, half_of(half), :] = mixed
        support_copy(span, half).start()
        mine = pl.ds(pl.multiple_of(feat * width, width), width)
        theirs = pl.ds(pl.multiple_of(partner * width, width), width)
        projected = jnp.dot(mixed, weight_ref[mine, :], preferred_element_type=jnp.float32)
        support_copy(span, half).wait_recv()
        projected += jnp.dot(other[span, half_of(half), :], weight_ref[theirs, :], preferred_element_type=jnp.float32)
        rows = jnp.maximum((1.0 - beta) * mixed.astype(jnp.float32) + beta * projected, 0.0).astype(jnp.bfloat16)
        result[span, half_of(half), :] = rows
        out_ref[span, half_of(half), :] = rows

        @pl.when(section < sections - 1)
        def _():
            row_copy(span, half).start()

    def finish_all(span):
        for half in range(halves):
            finish(span, half)

    load_kept.wait()
    load_features.wait()

    @pl.when(section == 0)
    def _():
        for span in range(spans):
            local(span, True)
            scatter(span)
            if span:
                pass_on(span - 1)
        gather()
        load_weight.wait()
        for span in range(spans - 1):
            finish_all(span)
            if span == 0:
                pass_on(spans - 1)

    @pl.when(section > 0)
    def _():
        for span in range(spans):
            local(span, False)
        gather()
        load_weight.wait()
        for span in range(spans):
            scatter(span)
            pass_on(span)
            if span:
                finish_all(span - 1)
            if span + 1 < spans:
                earlier(span + 1)

    def merge(i, _):
        here = pl.ds(pl.multiple_of(i * chunk, chunk), chunk)
        moved = jnp.dot(select_ref[here, :], fresh_ref[...], preferred_element_type=jnp.float32)
        kept_ref[here, :] = (kept_ref[here, :].astype(jnp.float32) + moved).astype(jnp.bfloat16)
        return 0

    @pl.when(section > 0)
    def _():
        lax.fori_loop(0, owned // chunk, merge, 0)

    store = pltpu.make_async_copy(kept_ref, table_hbm, table_sem)
    store.start()
    finish_all(spans - 1)

    for span in range(spans):
        for half in range(halves):
            support_copy(span, half).wait_send()
            for step in range(1, vertices):
                @pl.when(is_sent(step))
                def _(span=span, step=step, half=half):
                    part_copy(span, step, half).wait_send()

            if relayed:
                @pl.when(at_end)
                def _(span=span, half=half):
                    pass_copy(span, half).wait_send()

            @pl.when(section < sections - 1)
            def _(span=span, half=half):
                row_copy(span, half).wait_send()

    store.wait()

LINE = 4


def write(rows_ref, table_ref, rows_out, table_out, sem):
    chunks = sem.shape[0] - 1
    size = table_ref.shape[0] // chunks
    moves = [pltpu.make_async_copy(rows_ref, rows_out, sem.at[chunks])]
    for i in range(chunks):
        here = pl.ds(i * size, size)
        moves.append(pltpu.make_async_copy(table_ref.at[here], table_out.at[here], sem.at[i]))
    for move in moves:
        move.start()
    for move in moves:
        move.wait()


def stream(
    sections, vertices, feats,
    rows_ref, cols_ref, counts_ref, ids_ref, tiles_hbm, weight_hbm, kept_hbm, features_hbm, out_ref, kept_ref,
    tiles, left, right, right_select, base_ref, picks_ref, weight_ref, features_ref, select_ref, taken_ref, initial_ref,
    fresh_ref, partial, parts, passing, transit, support, other, result,
    load_sem, x_send, x_recv, p_send, p_recv, h_send, h_recv, s_send, s_recv, d_send, d_recv, t_send,
):
    section = lax.axis_index("section")
    vertex = lax.axis_index("vertex")
    feat = lax.axis_index("feat")
    spans, span_rows, width = result.shape
    pieces = x_send.shape[1]
    part = width // pieces
    wide = min(256, width)
    slots, side = tiles.shape[1:3]
    row_blocks = left.shape[0] // side
    rows_all = spans * span_rows
    last = vertices - 1
    partner = lax.rem(feat + 1, feats)
    beside = lax.rem(section + sections // 2, sections)
    opposite = lax.rem(vertex + last - 1, vertices)
    beta = jnp.log(BETA_SCALE / (section + 1).astype(jnp.float32) + 1.0)
    col_blocks = kept_ref.shape[0]

    def load_tiles(span):
        return pltpu.make_async_copy(tiles_hbm.at[span], tiles.at[span], load_sem.at[span])

    quarters = min(4, col_blocks)
    quarter = col_blocks // quarters

    def load_table(q):
        here = pl.ds(q * quarter, quarter)
        return (
            pltpu.make_async_copy(kept_hbm.at[here], kept_ref.at[here], load_sem.at[spans + 1 + q]),
            pltpu.make_async_copy(features_hbm.at[here], features_ref.at[here], load_sem.at[spans + 1 + quarters + q]),
        )

    load_weight = pltpu.make_async_copy(weight_hbm, weight_ref, load_sem.at[spans])
    load_tiles(0).start()
    for q in range(quarters):
        for copy in load_table(q):
            copy.start()
    for span in range(1, spans):
        load_tiles(span).start()
    load_weight.start()

    barrier = pltpu.get_barrier_semaphore()
    for step in range(1, vertices):
        peer = lax.rem(vertex + step, vertices)
        pl.semaphore_signal(barrier, inc=1, device_id=(section, peer, feat), device_id_type=MESH)
    pl.semaphore_signal(barrier, inc=1, device_id=(section, vertex, partner), device_id_type=MESH)
    for step in (1, sections - 1):
        peer = lax.rem(section + step, sections)
        pl.semaphore_signal(barrier, inc=1, device_id=(peer, vertex, feat), device_id_type=MESH)
    for peer in (vertex, opposite):
        pl.semaphore_signal(barrier, inc=1, device_id=(beside, peer, feat), device_id_type=MESH)

    def meet():
        pl.semaphore_wait(barrier, vertices - 1 + 1 + 2 + 2)

    at_end = (vertex == 0) | (vertex == last)

    @pl.when(vertex == 0)
    def _():
        parts[:, 0] = jnp.zeros((spans, span_rows, width), jnp.bfloat16)

    @pl.when(vertex == last)
    def _():
        parts[:, last - 1] = jnp.zeros((spans, span_rows, width), jnp.bfloat16)

    def columns(j):
        return slice(j * part, (j + 1) * part)

    def lanes(j):
        return pl.ds(j * part, part)

    def span_of(span):
        return slice(span * span_rows, (span + 1) * span_rows)

    def row_copy(span, j):
        return pltpu.make_async_remote_copy(
            src_ref=result.at[span, :, lanes(j)],
            dst_ref=fresh_ref.at[pl.ds(span * span_rows, span_rows), lanes(j)],
            send_sem=x_send.at[span, j], recv_sem=x_recv.at[span, j],
            device_id=(lax.rem(section + 1, sections), vertex, feat), device_id_type=MESH,
        )

    def rows_of(peer):
        return pl.ds(pl.multiple_of(peer * span_rows, span_rows), span_rows)

    def part_copy(span, step, j):
        peer = lax.rem(vertex + step, vertices)
        return pltpu.make_async_remote_copy(
            src_ref=partial.at[span, rows_of(peer), lanes(j)], dst_ref=parts.at[span, step - 1, :, lanes(j)],
            send_sem=p_send.at[span, step - 1, j], recv_sem=p_recv.at[span, step - 1, j],
            device_id=(section, peer, feat), device_id_type=MESH,
        )

    def pass_copy(span, j):
        far = jnp.where(vertex == 0, last, 0)
        near = jnp.where(vertex == 0, 1, last - 1)
        return pltpu.make_async_remote_copy(
            src_ref=partial.at[span, rows_of(far), lanes(j)], dst_ref=passing.at[span, :, lanes(j)],
            send_sem=h_send.at[span, j], recv_sem=h_recv.at[span, j],
            device_id=(section, near, feat), device_id_type=MESH,
        )

    def detour_copy(span, j):
        return pltpu.make_async_remote_copy(
            src_ref=partial.at[span, rows_of(opposite), lanes(j)], dst_ref=transit.at[span, :, lanes(j)],
            send_sem=d_send.at[span, j], recv_sem=d_recv.at[span, j],
            device_id=(beside, vertex, feat), device_id_type=MESH,
        )

    def return_copy(span, j):
        return pltpu.make_async_remote_copy(
            src_ref=transit.at[span, :, lanes(j)], dst_ref=parts.at[span, last - 2, :, lanes(j)],
            send_sem=t_send.at[span, j], recv_sem=p_recv.at[span, last - 2, j],
            device_id=(beside, opposite, feat), device_id_type=MESH,
        )

    def support_copy(span, j):
        return pltpu.make_async_remote_copy(
            src_ref=support.at[span, :, lanes(j)], dst_ref=other.at[span, :, lanes(j)],
            send_sem=s_send.at[span, j], recv_sem=s_recv.at[span, j],
            device_id=(section, vertex, partner), device_id_type=MESH,
        )

    def ends_meet(here, there):
        return ((here == 0) & (there == last)) | ((here == last) & (there == 0))

    def is_sent(step):
        far = ends_meet(vertex, lax.rem(vertex + step, vertices))
        return jnp.logical_not(far | at_end) if step == last - 1 else jnp.logical_not(far)

    def is_received(step):
        return jnp.logical_not(ends_meet(lax.rem(vertex + vertices - step, vertices), vertex))

    def choose():
        def one_hot(i, _):
            for span in range(spans):
                hot = chosen(ids_ref[span : span + 1, :], side, i * side)
                select_ref[i, :, span_of(span)] = hot.astype(jnp.bfloat16)
            return 0

        lax.fori_loop(0, col_blocks, one_hot, 0)

    def count(span):
        taken_ref[span] = jnp.dot(
            select_ref[...].reshape(col_blocks * side, rows_all)[:, span_of(span)],
            jnp.ones((span_rows, side), jnp.bfloat16),
            preferred_element_type=jnp.float32,
        ).astype(jnp.bfloat16).reshape(col_blocks, side, side)

    def mark(span, leading):
        def clear(i, _):
            taken = taken_ref[span, i]
            rest = 1.0 - taken
            for first in range(0, width, side):
                group = slice(first, first + side)
                row = kept_ref[i, :, group] * rest
                kept_ref[i, :, group] = row + features_ref[i, :, group] * taken if leading else row
            return 0

        if span:
            lax.fori_loop(0, col_blocks, clear, 0)
        else:
            for q in range(quarters):
                for copy in load_table(q):
                    copy.wait()
                lax.fori_loop(q * quarter, (q + 1) * quarter, clear, 0)

    def lay_left(span):
        load_tiles(span).wait()
        lives = jnp.full((side, side), counts_ref[0, span], jnp.int32)

        def place(t, _):
            here = pl.ds(pl.multiple_of(t * side, side), side)
            tile = tiles[span, t].astype(jnp.float32)
            rows = jnp.where(lives > t, jnp.full(tile.shape, rows_ref[span, t], jnp.int32), row_blocks)
            for block in range(row_blocks):
                left[block * side : (block + 1) * side, here] = jnp.where(rows == block, tile, 0.0).astype(left.dtype)
            return 0

        lax.fori_loop(0, slots, place, 0)

    def lay_right(span, leading):
        def place(t, _):
            col = cols_ref[span, t]
            here = pl.ds(pl.multiple_of(t * side, side), side)
            right[here, :] = kept_ref[col]
            if not leading:
                right_select[here, :] = select_ref[col]
            return 0

        lax.fori_loop(0, slots, place, 0)

    def prepare_span(span, leading):
        if span:
            lay_left(span)
        mark(span, leading)
        lay_right(span, leading)

    def gather():
        initial_ref[...] = lax.dot_general(
            select_ref[...].reshape(col_blocks * side, rows_all),
            features_ref[...].reshape(col_blocks * side, width),
            (((0,), (0,)), ((), ())),
            preferred_element_type=jnp.float32,
        ).astype(jnp.bfloat16)

    def groups():
        return [slice(first, first + wide) for first in range(0, width, wide)]

    def product(group):
        return jnp.dot(left[...], right[:, group], preferred_element_type=jnp.float32)

    def first_sums(span, j):
        if j * part % wide == 0:
            group = slice(j * part, j * part + wide)
            partial[span, :, group] = product(group).astype(jnp.bfloat16)

    def later_sums(span, j):
        row_copy(span, j).wait_recv()
        partial[span, :, columns(j)] = (
            base_ref[span, :, columns(j)]
            + jnp.dot(
                picks_ref[span, :, span_of(span)], fresh_ref[span_of(span), columns(j)],
                preferred_element_type=jnp.float32,
            )
        ).astype(jnp.bfloat16)

    def scatter(span, sums):
        for j in range(pieces):
            sums(span, j)

            @pl.when(at_end)
            def _(j=j):
                pass_copy(span, j).start()
                detour_copy(span, j).start()

            @pl.when(jnp.logical_not(at_end))
            def _(j=j):
                for step in (1, last):
                    part_copy(span, step, j).start()

        for j in range(pieces):
            for step in (1, last):
                @pl.when(at_end & is_sent(step))
                def _(step=step, j=j):
                    part_copy(span, step, j).start()

    def pass_on(span):
        for who, step in ((1, last - 1), (last - 1, 2)):
            @pl.when(vertex == who)
            def _(who=who, step=step):
                far = last if who == 1 else 0
                here = pl.ds(far * span_rows, span_rows)
                for j in range(pieces):
                    pass_copy(span, j).wait_recv()
                    partial[span, here, columns(j)] = (
                        partial[span, here, columns(j)].astype(jnp.float32)
                        + passing[span, :, columns(j)].astype(jnp.float32)
                    ).astype(jnp.bfloat16)
                    part_copy(span, step, j).start()

    def hand_on(span):
        @pl.when(at_end)
        def _():
            for j in range(pieces):
                detour_copy(span, j).wait_recv()
                return_copy(span, j).start()

    def keep(span):
        used = (span + 1) * span_rows
        for group in groups():
            base_ref[span, :, group] = product(group)
        picks_ref[span, :, :used] = jnp.dot(
            left[...], right_select[:, :used], preferred_element_type=jnp.float32
        ).astype(jnp.bfloat16)

    def earlier(span):
        used = span * span_rows
        for group in groups():
            base_ref[span, :, group] += jnp.dot(
                picks_ref[span, :, :used], fresh_ref[:used, group], preferred_element_type=jnp.float32
            )

    def weight_rows(which):
        return pl.ds(pl.multiple_of(which * width, width), width)

    def finish(span):
        halves = groups()
        whole = [0.0] * len(halves)
        for half in halves:
            here = range(half.start // part, half.stop // part)
            for j in here:
                for step in range(1, vertices):
                    @pl.when(is_received(step))
                    def _(step=step, j=j):
                        part_copy(span, step, j).wait_recv()

                total = partial[span, rows_of(vertex), columns(j)].astype(jnp.float32)
                for step in range(1, vertices):
                    total += parts[span, step - 1, :, columns(j)].astype(jnp.float32)
                support[span, :, columns(j)] = (
                    (1.0 - RESIDUAL_SHARE) * total
                    + RESIDUAL_SHARE * initial_ref[span_of(span), columns(j)].astype(jnp.float32)
                ).astype(jnp.bfloat16)
                support_copy(span, j).start()

        def project(source, which, half, group):
            rows = pl.ds(pl.multiple_of(which * width + half.start, wide), wide)
            return jnp.dot(source[span, :, half], weight_ref[rows, group], preferred_element_type=jnp.float32)

        for k, group in enumerate(halves):
            for half in halves:
                whole[k] += project(support, feat, half, group)
        for half in halves:
            for j in range(half.start // part, half.stop // part):
                support_copy(span, j).wait_recv()
            if half is not halves[-1]:
                for k, group in enumerate(halves):
                    whole[k] += project(other, partner, half, group)
        for k, group in enumerate(halves):
            rows = jnp.maximum(
                (1.0 - beta) * support[span, :, group].astype(jnp.float32)
                + beta * (whole[k] + project(other, partner, halves[-1], group)),
                0.0,
            ).astype(jnp.bfloat16)
            result[span, :, group] = rows

            @pl.when(section < sections - 1)
            def _(group=group):
                for j in range(group.start // part, group.stop // part):
                    row_copy(span, j).start()

            out_ref[span, :, group] = rows

    choose()
    count(0)
    lay_left(0)
    for span in range(1, spans):
        count(span)

    @pl.when(section == 0)
    def _():
        for span in range(spans):
            prepare_span(span, True)
            if span == 0:
                meet()
            if span == 2:
                pass_on(0)
            scatter(span, first_sums)
        gather()
        load_weight.wait()
        if spans < 3:
            pass_on(0)
        for span in range(spans - 1):
            finish(span)
            pass_on(span + 1)

    @pl.when(section > 0)
    def _():
        for span in range(spans):
            prepare_span(span, False)
            keep(span)
            if span == 0:
                meet()

                @pl.when(section == sections // 2)
                def _():
                    for ahead in range(spans):
                        hand_on(ahead)

        gather()
        load_weight.wait()

        @pl.when(section > sections // 2)
        def _():
            for span in range(spans):
                hand_on(span)

        for span in range(spans):
            scatter(span, later_sums)
            if span:
                finish(span - 1)
            pass_on(span)
            if span + 1 < spans:
                earlier(span + 1)

    def merge():
        blocks = max(1, 512 // side)
        for first in range(0, col_blocks, blocks):
            picked = select_ref[first : first + blocks].reshape(blocks * side, rows_all)
            for group in groups():
                moved = jnp.dot(picked, fresh_ref[:, group], preferred_element_type=jnp.float32).astype(jnp.bfloat16)
                kept_ref[first : first + blocks, :, group] += moved.reshape(blocks, side, wide)

    @pl.when(section > 0)
    def _():
        merge()

    finish(spans - 1)

    @pl.when(section < sections // 2)
    def _():
        for span in range(spans):
            hand_on(span)

    for span in range(spans):
        for j in range(pieces):
            support_copy(span, j).wait_send()
            for step in range(1, vertices):
                @pl.when(is_sent(step))
                def _(span=span, step=step, j=j):
                    part_copy(span, step, j).wait_send()

            @pl.when(at_end)
            def _(span=span, j=j):
                pass_copy(span, j).wait_send()
                detour_copy(span, j).wait_send()
                return_copy(span, j).wait_send()

            @pl.when(section < sections - 1)
            def _(span=span, j=j):
                row_copy(span, j).wait_send()


def deliver(rows_hbm, table_hbm, rows_out, table_out, rows_ref, table_ref, in_sem, out_sem):
    chunks = in_sem.shape[0] - 1
    size = table_ref.shape[0] // chunks
    moves = []
    for i in range(chunks):
        here = pl.ds(i * size, size)
        moves.append((
            pltpu.make_async_copy(table_hbm.at[here], table_ref.at[here], in_sem.at[i]),
            pltpu.make_async_copy(table_ref.at[here], table_out.at[here], out_sem.at[i]),
        ))
    moves.append((
        pltpu.make_async_copy(rows_hbm, rows_ref, in_sem.at[chunks]),
        pltpu.make_async_copy(rows_ref, rows_out, out_sem.at[chunks]),
    ))
    for get, _ in moves:
        get.start()
    for get, put in moves:
        get.wait()
        put.start()
    for _, put in moves:
        put.wait()


def long_line(sizes, features, history, weights, tile_values, tile_rows, tile_cols, tile_counts, span_ids):
    sections, vertices, feats = sizes
    spans, span_rows = span_ids.shape
    owned, width = features.shape
    rows_whole = span_rows * vertices
    rows_all = spans * span_rows
    vmem = pl.BlockSpec(memory_space=pltpu.VMEM)
    smem = pl.BlockSpec(memory_space=pltpu.SMEM)
    anywhere = pl.BlockSpec(memory_space=pl.ANY)

    dense = pl.pallas_call(
        prepare,
        name="prepare",
        out_shape=jax.ShapeDtypeStruct((spans, rows_whole, owned), jnp.bfloat16),
        in_specs=[smem, smem, smem, vmem],
        out_specs=anywhere,
        scratch_shapes=[
            pltpu.VMEM((spans, rows_whole, owned), jnp.bfloat16),
            pltpu.SemaphoreType.DMA((spans,)),
        ],
        compiler_params=pltpu.CompilerParams(vmem_limit_bytes=VMEM_BYTES),
    )(tile_rows, tile_cols, tile_counts.reshape(1, spans), tile_values)

    rows_type = jax.ShapeDtypeStruct((spans, span_rows, width), jnp.bfloat16)
    table_type = jax.ShapeDtypeStruct((owned, width), jnp.bfloat16)
    block = pltpu.VMEM(rows_type.shape, jnp.bfloat16)
    halves = 2
    pair = pltpu.SemaphoreType.DMA((spans, halves))
    layer_rows, table_new = pl.pallas_call(
        functools.partial(relay, sections, vertices, feats),
        name="relay",
        out_shape=(rows_type, table_type),
        in_specs=[anywhere, vmem, anywhere, anywhere, anywhere],
        out_specs=(vmem, anywhere),
        scratch_shapes=[
            pltpu.VMEM((min(2, spans), rows_whole, owned), jnp.bfloat16),
            pltpu.VMEM((spans, rows_whole, width), jnp.float32),
            pltpu.VMEM((spans, rows_whole, rows_all), jnp.bfloat16),
            pltpu.VMEM(weights.shape[1:], weights.dtype),
            pltpu.VMEM((owned, width), jnp.bfloat16),
            pltpu.VMEM((owned, width), jnp.bfloat16),
            pltpu.VMEM((owned, rows_all), jnp.bfloat16),
            pltpu.VMEM((rows_all, width), jnp.bfloat16),
            pltpu.VMEM((rows_all, width), jnp.bfloat16),
            block,
            pltpu.VMEM((spans, rows_whole, width), jnp.bfloat16),
            pltpu.VMEM((spans, vertices - 1, span_rows, width), jnp.bfloat16),
            block, block, block, block,
            pltpu.SemaphoreType.DMA((spans + 3,)),
            pltpu.SemaphoreType.DMA,
            pair, pair,
            pltpu.SemaphoreType.DMA((spans, vertices - 1, halves)),
            pltpu.SemaphoreType.DMA((spans, vertices - 1, halves)),
            pair, pair, pair, pair,
        ],
        compiler_params=pltpu.CompilerParams(
            vmem_limit_bytes=VMEM_BYTES, collective_id=0, has_side_effects=True
        ),
    )(dense, span_ids, weights[0], history[0], features)

    table_type = jax.ShapeDtypeStruct((owned, width), jnp.bfloat16)
    chunks = 8
    return pl.pallas_call(
        deliver,
        name="deliver",
        out_shape=(rows_type, table_type),
        in_specs=[anywhere, anywhere],
        out_specs=(anywhere, anywhere),
        scratch_shapes=[
            pltpu.VMEM(rows_type.shape, jnp.bfloat16),
            pltpu.VMEM(table_type.shape, jnp.bfloat16),
            pltpu.SemaphoreType.DMA((chunks + 1,)),
            pltpu.SemaphoreType.DMA((chunks + 1,)),
        ],
        compiler_params=pltpu.CompilerParams(vmem_limit_bytes=VMEM_BYTES),
    )(layer_rows, table_new)


def short_line(sizes, features, history, weights, tile_values, tile_rows, tile_cols, tile_counts, span_ids):
    sections, vertices, feats = sizes
    spans, span_rows = span_ids.shape
    slots, side = tile_values.shape[1:3]
    owned, width = features.shape
    rows_whole = span_rows * vertices
    rows_all = spans * span_rows
    pieces = 4
    vmem = pl.BlockSpec(memory_space=pltpu.VMEM)
    smem = pl.BlockSpec(memory_space=pltpu.SMEM)
    anywhere = pl.BlockSpec(memory_space=pl.ANY)
    block = pltpu.VMEM((spans, span_rows, width), jnp.bfloat16)
    pair = pltpu.SemaphoreType.DMA((spans, pieces))
    triple = pltpu.SemaphoreType.DMA((spans, vertices - 1, pieces))
    table = history[0].reshape(owned // side, side, width)
    layer_rows, table_new = pl.pallas_call(
        functools.partial(stream, sections, vertices, feats),
        name="stream",
        out_shape=(
            pltpu.VMEM((spans, span_rows, width), jnp.bfloat16),
            pltpu.VMEM(table.shape, jnp.bfloat16),
        ),
        in_specs=[smem, smem, smem, vmem, anywhere, anywhere, anywhere, anywhere],
        out_specs=(vmem, vmem),
        scratch_shapes=[
            pltpu.VMEM(tile_values.shape, jnp.bfloat16),
            pltpu.VMEM((rows_whole, slots * side), jnp.bfloat16),
            pltpu.VMEM((slots * side, width), jnp.bfloat16),
            pltpu.VMEM((slots * side, rows_all), jnp.bfloat16),
            pltpu.VMEM((spans, rows_whole, width), jnp.float32),
            pltpu.VMEM((spans, rows_whole, rows_all), jnp.bfloat16),
            pltpu.VMEM(weights.shape[1:], weights.dtype),
            pltpu.VMEM(table.shape, jnp.bfloat16),
            pltpu.VMEM((owned // side, side, rows_all), jnp.bfloat16),
            pltpu.VMEM((spans, owned // side, side, side), jnp.bfloat16),
            pltpu.VMEM((rows_all, width), jnp.bfloat16),
            pltpu.VMEM((rows_all, width), jnp.bfloat16),
            pltpu.VMEM((spans, rows_whole, width), jnp.bfloat16),
            pltpu.VMEM((spans, vertices - 1, span_rows, width), jnp.bfloat16),
            block, block, block, block, block,
            pltpu.SemaphoreType.DMA((spans + 9,)),
            pair, pair, triple, triple, pair, pair, pair, pair, pair, pair, pair,
        ],
        compiler_params=pltpu.CompilerParams(
            vmem_limit_bytes=VMEM_BYTES, collective_id=0, has_side_effects=True
        ),
    )(tile_rows, tile_cols, tile_counts.reshape(1, spans), span_ids, tile_values, weights[0], table,
      features.reshape(table.shape))
    chunks = 4
    layer_rows, table_new = pl.pallas_call(
        write,
        name="write",
        out_shape=(
            jax.ShapeDtypeStruct((spans, span_rows, width), jnp.bfloat16),
            jax.ShapeDtypeStruct(table.shape, jnp.bfloat16),
        ),
        in_specs=[vmem, vmem],
        out_specs=(anywhere, anywhere),
        scratch_shapes=[pltpu.SemaphoreType.DMA((chunks + 1,))],
        compiler_params=pltpu.CompilerParams(vmem_limit_bytes=VMEM_BYTES),
    )(
        pltpu.with_memory_space_constraint(layer_rows, pltpu.VMEM),
        pltpu.with_memory_space_constraint(table_new, pltpu.VMEM),
    )
    return layer_rows, table_new.reshape(owned, width)


def shards(sizes, *arrays):
    layers = short_line if sizes[0] == sizes[1] == LINE else long_line
    layer_rows, table_new = layers(sizes, *arrays)
    return (layer_rows[None], table_new[None])


def solution(mesh):
    placed = (
        P("vertex", "feat"),
        P("section", "vertex", "feat"),
        P("section", None, "feat"),
        P(None, "vertex", None, None),
        P(None, "vertex"),
        P(None, "vertex"),
        P(None, "vertex"),
        P(None, "vertex"),
    )
    sizes = (mesh.shape["section"], mesh.shape["vertex"], mesh.shape["feat"])
    return jax.shard_map(
        functools.partial(shards, sizes),
        mesh=mesh,
        in_specs=placed,
        out_specs=(P("section", None, "vertex", "feat"), P("section", "vertex", "feat")),
        check_vma=False,
    )
```

```python
import functools

import jax
import jax.numpy as jnp
from jax import lax
from jax.experimental import pallas as pl
from jax.experimental.pallas import tpu as pltpu
from jax.sharding import PartitionSpec as P

RESIDUAL_SHARE = 0.2
BETA_SCALE = 0.5
MESH = pl.DeviceIdType.MESH
VMEM_BYTES = 60_000 * 1024


def chosen(ids_row, rows, first=0):
    shape = (rows, ids_row.shape[1])
    return (lax.broadcasted_iota(jnp.int32, shape, 0) + first == ids_row).astype(jnp.float32)


def prepare(rows_ref, cols_ref, counts_ref, tiles_ref, dense_hbm, dense, dense_sem):
    spans, _, side, _ = tiles_ref.shape
    copies = []
    for span in range(spans):
        dense[span] = jnp.zeros(dense.shape[1:], dense.dtype)

        def place(t, _, span=span):
            row = pl.multiple_of(rows_ref[span, t] * side, side)
            col = pl.multiple_of(cols_ref[span, t] * side, side)
            dense[span, pl.ds(row, side), pl.ds(col, side)] = tiles_ref[span, t]
            return 0

        lax.fori_loop(0, counts_ref[0, span], place, 0)
        copies.append(pltpu.make_async_copy(dense.at[span], dense_hbm.at[span], dense_sem.at[span]))
        copies[-1].start()
    for copy in copies:
        copy.wait()


def relay(
    sections, vertices, feats,
    dense_hbm, ids_ref, weight_hbm, kept_hbm, features_hbm, out_ref, table_hbm,
    dense, base_ref, picks_ref, weight_ref, kept_ref, features_ref, select_ref, initial_ref, fresh_ref,
    arrived, partial, parts, passing, support, other, result,
    load_sem, table_sem, x_send, x_recv, p_send, p_recv, h_send, h_recv, s_send, s_recv,
):
    section = lax.axis_index("section")
    vertex = lax.axis_index("vertex")
    feat = lax.axis_index("feat")
    spans, span_rows, width = arrived.shape
    last = vertices - 1
    partner = lax.rem(feat + 1, feats)
    beta = jnp.log(BETA_SCALE / (section + 1).astype(jnp.float32) + 1.0)
    halves = 2
    piece = span_rows // halves
    relayed = vertices > 3

    rows_whole = dense.shape[1]
    owned = kept_ref.shape[0]
    group = min(512, rows_whole)
    chunk = min(256, owned)

    def load_dense(span):
        return pltpu.make_async_copy(dense_hbm.at[span], dense.at[span % 2], load_sem.at[span])

    load_weight = pltpu.make_async_copy(weight_hbm, weight_ref, load_sem.at[spans])
    load_kept = pltpu.make_async_copy(kept_hbm, kept_ref, load_sem.at[spans + 1])
    load_features = pltpu.make_async_copy(features_hbm, features_ref, load_sem.at[spans + 2])
    load_kept.start()
    load_features.start()
    for span in range(min(2, spans)):
        load_dense(span).start()
    load_weight.start()

    barrier = pltpu.get_barrier_semaphore()
    for step in range(1, vertices):
        peer = lax.rem(vertex + step, vertices)
        pl.semaphore_signal(barrier, inc=1, device_id=(section, peer, feat), device_id_type=MESH)
    pl.semaphore_signal(barrier, inc=1, device_id=(section, vertex, partner), device_id_type=MESH)
    for step in (1, sections - 1):
        peer = lax.rem(section + step, sections)
        pl.semaphore_signal(barrier, inc=1, device_id=(peer, vertex, feat), device_id_type=MESH)
    if relayed:
        @pl.when(vertex == 0)
        def _():
            parts[:, 0] = jnp.zeros((spans, span_rows, width), jnp.bfloat16)

        @pl.when(vertex == last)
        def _():
            parts[:, last - 1] = jnp.zeros((spans, span_rows, width), jnp.bfloat16)

    pl.semaphore_wait(barrier, vertices - 1 + 1 + 2)

    def half_of(half):
        return slice(half * piece, (half + 1) * piece)

    def row_copy(span, half):
        rows = pl.ds(half * piece, piece)
        return pltpu.make_async_remote_copy(
            src_ref=result.at[span, rows], dst_ref=arrived.at[span, rows],
            send_sem=x_send.at[span, half], recv_sem=x_recv.at[span, half],
            device_id=(lax.rem(section + 1, sections), vertex, feat), device_id_type=MESH,
        )

    def chunk_rows(peer, half):
        return pl.ds(pl.multiple_of(peer * span_rows + half * piece, piece), piece)

    def part_copy(span, step, half):
        peer = lax.rem(vertex + step, vertices)
        return pltpu.make_async_remote_copy(
            src_ref=partial.at[span, chunk_rows(peer, half)],
            dst_ref=parts.at[span, step - 1, pl.ds(half * piece, piece)],
            send_sem=p_send.at[span, step - 1, half], recv_sem=p_recv.at[span, step - 1, half],
            device_id=(section, peer, feat), device_id_type=MESH,
        )

    def pass_copy(span, half):
        far = jnp.where(vertex == 0, last, 0)
        near = jnp.where(vertex == 0, 1, last - 1)
        return pltpu.make_async_remote_copy(
            src_ref=partial.at[span, chunk_rows(far, half)],
            dst_ref=passing.at[span, pl.ds(half * piece, piece)],
            send_sem=h_send.at[span, half], recv_sem=h_recv.at[span, half],
            device_id=(section, near, feat), device_id_type=MESH,
        )

    def support_copy(span, half):
        rows = pl.ds(half * piece, piece)
        return pltpu.make_async_remote_copy(
            src_ref=support.at[span, rows], dst_ref=other.at[span, rows],
            send_sem=s_send.at[span, half], recv_sem=s_recv.at[span, half],
            device_id=(section, vertex, partner), device_id_type=MESH,
        )

    at_end = (vertex == 0) | (vertex == last)

    def is_direct(step):
        if not relayed:
            return vertex >= 0
        peer = lax.rem(vertex + step, vertices)
        ends = ((vertex == 0) & (peer == last)) | ((vertex == last) & (peer == 0))
        inner = ((vertex == 1) & (peer == last)) | ((vertex == last - 1) & (peer == 0))
        return jnp.logical_not(ends | inner)

    def is_sent(step):
        if not relayed:
            return vertex >= 0
        peer = lax.rem(vertex + step, vertices)
        return jnp.logical_not(((vertex == 0) & (peer == last)) | ((vertex == last) & (peer == 0)))

    def is_received(step):
        if not relayed:
            return vertex >= 0
        source = lax.rem(vertex + vertices - step, vertices)
        return jnp.logical_not(((vertex == 0) & (source == last)) | ((vertex == last) & (source == 0)))

    def local(span, leading):
        mine = slice(span * span_rows, (span + 1) * span_rows)
        used = (span + 1) * span_rows

        def clear(i, _):
            first = pl.multiple_of(i * chunk, chunk)
            here = pl.ds(first, chunk)
            hot = chosen(ids_ref[span : span + 1, :], chunk, first)
            select_ref[here, mine] = hot.astype(jnp.bfloat16)
            taken = jnp.max(hot, axis=1, keepdims=True) > 0.5
            filler = features_ref[here, :].astype(jnp.float32) if leading else 0.0
            kept_ref[here, :] = jnp.where(taken, filler, kept_ref[here, :].astype(jnp.float32)).astype(jnp.bfloat16)
            return 0

        lax.fori_loop(0, owned // chunk, clear, 0)
        load_dense(span).wait()

        def multiply(i, _):
            here = pl.ds(pl.multiple_of(i * group, group), group)
            block = dense[span % 2, here, :]
            product = jnp.dot(block, kept_ref[...], preferred_element_type=jnp.float32)
            if leading:
                partial[span, here, :] = product.astype(jnp.bfloat16)
            else:
                base_ref[span, here, :] = product
                picks_ref[span, here, :used] = jnp.dot(
                    block, select_ref[:, :used], preferred_element_type=jnp.float32
                ).astype(jnp.bfloat16)
            return 0

        lax.fori_loop(0, rows_whole // group, multiply, 0)
        if span + 2 < spans:
            load_dense(span + 2).start()

    def gather():
        initial_ref[...] = lax.dot_general(
            select_ref[...], features_ref[...], (((0,), (0,)), ((), ())), preferred_element_type=jnp.float32
        ).astype(jnp.bfloat16)

    def earlier(span):
        used = span * span_rows

        def add(i, _):
            here = pl.ds(pl.multiple_of(i * group, group), group)
            base_ref[span, here, :] += jnp.dot(
                picks_ref[span, here, :used], fresh_ref[:used, :], preferred_element_type=jnp.float32
            )
            return 0

        lax.fori_loop(0, rows_whole // group, add, 0)

    def scatter(span):
        mine = slice(span * span_rows, (span + 1) * span_rows)
        @pl.when(section > 0)
        def _():
            for half in range(halves):
                row_copy(span, half).wait_recv()
            fresh_ref[mine, :] = arrived[span]


        def compute(peer):
            here = pl.ds(pl.multiple_of(peer * span_rows, span_rows), span_rows)
            total = base_ref[span, here, :] + jnp.dot(
                picks_ref[span, here, mine], fresh_ref[mine, :], preferred_element_type=jnp.float32
            )
            partial[span, here, :] = total.astype(jnp.bfloat16)

        if relayed:
            @pl.when(at_end & (section > 0))
            def _():
                compute(jnp.where(vertex == 0, last, 0))

            @pl.when(at_end)
            def _():
                for half in range(halves):
                    pass_copy(span, half).start()

        for step in range(1, vertices):
            @pl.when(is_sent(step) & (section > 0))
            def _(step=step):
                compute(lax.rem(vertex + step, vertices))

            @pl.when(is_direct(step))
            def _(step=step):
                part_copy(span, step, 0).start()

        for half in range(1, halves):
            for step in range(1, vertices):
                @pl.when(is_direct(step))
                def _(step=step, half=half):
                    part_copy(span, step, half).start()

        @pl.when(section > 0)
        def _():
            compute(vertex)

    def pass_on(span):
        if relayed:
            for who, step in ((1, last - 1), (last - 1, 2)):
                @pl.when(vertex == who)
                def _(who=who, step=step):
                    far = last if who == 1 else 0
                    for half in range(halves):
                        pass_copy(span, half).wait_recv()
                        here = pl.ds(far * span_rows + half * piece, piece)
                        partial[span, here, :] = (
                            partial[span, here, :].astype(jnp.float32)
                            + passing[span, half_of(half), :].astype(jnp.float32)
                        ).astype(jnp.bfloat16)
                        part_copy(span, step, half).start()

    def finish(span, half):
        total = partial[span, chunk_rows(vertex, half), :].astype(jnp.float32)
        for step in range(1, vertices):
            @pl.when(is_received(step))
            def _(step=step):
                part_copy(span, step, half).wait_recv()

        for step in range(1, vertices):
            total += parts[span, step - 1, half_of(half), :].astype(jnp.float32)
        mixed = (
            (1.0 - RESIDUAL_SHARE) * total
            + RESIDUAL_SHARE * initial_ref[pl.ds(span * span_rows + half * piece, piece), :].astype(jnp.float32)
        ).astype(jnp.bfloat16)
        support[span, half_of(half), :] = mixed
        support_copy(span, half).start()
        mine = pl.ds(pl.multiple_of(feat * width, width), width)
        theirs = pl.ds(pl.multiple_of(partner * width, width), width)
        projected = jnp.dot(mixed, weight_ref[mine, :], preferred_element_type=jnp.float32)
        support_copy(span, half).wait_recv()
        projected += jnp.dot(other[span, half_of(half), :], weight_ref[theirs, :], preferred_element_type=jnp.float32)
        rows = jnp.maximum((1.0 - beta) * mixed.astype(jnp.float32) + beta * projected, 0.0).astype(jnp.bfloat16)
        result[span, half_of(half), :] = rows
        out_ref[span, half_of(half), :] = rows

        @pl.when(section < sections - 1)
        def _():
            row_copy(span, half).start()

    def finish_all(span):
        for half in range(halves):
            finish(span, half)

    load_kept.wait()
    load_features.wait()

    @pl.when(section == 0)
    def _():
        for span in range(spans):
            local(span, True)
            scatter(span)
            if span:
                pass_on(span - 1)
        gather()
        load_weight.wait()
        for span in range(spans - 1):
            finish_all(span)
            if span == 0:
                pass_on(spans - 1)

    @pl.when(section > 0)
    def _():
        for span in range(spans):
            local(span, False)
        gather()
        load_weight.wait()
        for span in range(spans):
            scatter(span)
            pass_on(span)
            if span:
                finish_all(span - 1)
            if span + 1 < spans:
                earlier(span + 1)

    def merge(i, _):
        here = pl.ds(pl.multiple_of(i * chunk, chunk), chunk)
        moved = jnp.dot(select_ref[here, :], fresh_ref[...], preferred_element_type=jnp.float32)
        kept_ref[here, :] = (kept_ref[here, :].astype(jnp.float32) + moved).astype(jnp.bfloat16)
        return 0

    @pl.when(section > 0)
    def _():
        lax.fori_loop(0, owned // chunk, merge, 0)

    store = pltpu.make_async_copy(kept_ref, table_hbm, table_sem)
    store.start()
    finish_all(spans - 1)

    for span in range(spans):
        for half in range(halves):
            support_copy(span, half).wait_send()
            for step in range(1, vertices):
                @pl.when(is_sent(step))
                def _(span=span, step=step, half=half):
                    part_copy(span, step, half).wait_send()

            if relayed:
                @pl.when(at_end)
                def _(span=span, half=half):
                    pass_copy(span, half).wait_send()

            @pl.when(section < sections - 1)
            def _(span=span, half=half):
                row_copy(span, half).wait_send()

    store.wait()

LINE = 4


def write(rows_ref, table_ref, rows_out, table_out, sem):
    chunks = sem.shape[0] - 1
    size = table_ref.shape[0] // chunks
    moves = [pltpu.make_async_copy(rows_ref, rows_out, sem.at[chunks])]
    for i in range(chunks):
        here = pl.ds(i * size, size)
        moves.append(pltpu.make_async_copy(table_ref.at[here], table_out.at[here], sem.at[i]))
    for move in moves:
        move.start()
    for move in moves:
        move.wait()


def stream(
    sections, vertices, feats,
    rows_ref, cols_ref, counts_ref, ids_ref, tiles_hbm, weight_hbm, kept_hbm, features_hbm, out_ref, kept_ref,
    tiles, left, right, right_select, base_ref, picks_ref, weight_ref, features_ref, select_ref, taken_ref, initial_ref,
    fresh_ref, partial, parts, passing, transit, support, other, result,
    load_sem, x_send, x_recv, p_send, p_recv, h_send, h_recv, s_send, s_recv, d_send, d_recv, t_send,
):
    section = lax.axis_index("section")
    vertex = lax.axis_index("vertex")
    feat = lax.axis_index("feat")
    spans, span_rows, width = result.shape
    pieces = x_send.shape[1]
    part = width // pieces
    wide = min(256, width)
    unit = min(256, width)
    slots, side = tiles.shape[1:3]
    row_blocks = left.shape[0] // side
    rows_all = spans * span_rows
    last = vertices - 1
    partner = lax.rem(feat + 1, feats)
    beside = lax.rem(section + sections // 2, sections)
    opposite = lax.rem(vertex + last - 1, vertices)
    beta = jnp.log(BETA_SCALE / (section + 1).astype(jnp.float32) + 1.0)
    col_blocks = kept_ref.shape[0]

    def load_tiles(span):
        return pltpu.make_async_copy(tiles_hbm.at[span], tiles.at[span], load_sem.at[span])

    quarters = min(4, col_blocks)
    quarter = col_blocks // quarters

    def load_table(q):
        here = pl.ds(q * quarter, quarter)
        return (
            pltpu.make_async_copy(kept_hbm.at[here], kept_ref.at[here], load_sem.at[spans + 1 + q]),
            pltpu.make_async_copy(features_hbm.at[here], features_ref.at[here], load_sem.at[spans + 1 + quarters + q]),
        )

    load_weight = pltpu.make_async_copy(weight_hbm, weight_ref, load_sem.at[spans])
    load_tiles(0).start()
    for q in range(quarters):
        for copy in load_table(q):
            copy.start()
    for span in range(1, spans):
        load_tiles(span).start()
    load_weight.start()

    barrier = pltpu.get_barrier_semaphore()
    for step in range(1, vertices):
        peer = lax.rem(vertex + step, vertices)
        pl.semaphore_signal(barrier, inc=1, device_id=(section, peer, feat), device_id_type=MESH)
    pl.semaphore_signal(barrier, inc=1, device_id=(section, vertex, partner), device_id_type=MESH)
    for step in (1, sections - 1):
        peer = lax.rem(section + step, sections)
        pl.semaphore_signal(barrier, inc=1, device_id=(peer, vertex, feat), device_id_type=MESH)
    for peer in (vertex, opposite):
        pl.semaphore_signal(barrier, inc=1, device_id=(beside, peer, feat), device_id_type=MESH)

    def meet():
        pl.semaphore_wait(barrier, vertices - 1 + 1 + 2 + 2)

    at_end = (vertex == 0) | (vertex == last)

    @pl.when(vertex == 0)
    def _():
        parts[:, 0] = jnp.zeros((spans, span_rows, width), jnp.bfloat16)

    @pl.when(vertex == last)
    def _():
        parts[:, last - 1] = jnp.zeros((spans, span_rows, width), jnp.bfloat16)

    def columns(j):
        return slice(j * part, (j + 1) * part)

    def lanes(j):
        return pl.ds(j * part, part)

    def span_of(span):
        return slice(span * span_rows, (span + 1) * span_rows)

    def row_copy(span, j):
        return pltpu.make_async_remote_copy(
            src_ref=result.at[span, :, lanes(j)],
            dst_ref=fresh_ref.at[pl.ds(span * span_rows, span_rows), lanes(j)],
            send_sem=x_send.at[span, j], recv_sem=x_recv.at[span, j],
            device_id=(lax.rem(section + 1, sections), vertex, feat), device_id_type=MESH,
        )

    def rows_of(peer):
        return pl.ds(pl.multiple_of(peer * span_rows, span_rows), span_rows)

    def part_copy(span, step, j):
        peer = lax.rem(vertex + step, vertices)
        return pltpu.make_async_remote_copy(
            src_ref=partial.at[span, rows_of(peer), lanes(j)], dst_ref=parts.at[span, step - 1, :, lanes(j)],
            send_sem=p_send.at[span, step - 1, j], recv_sem=p_recv.at[span, step - 1, j],
            device_id=(section, peer, feat), device_id_type=MESH,
        )

    def direct_copy(span, step, first):
        peer = lax.rem(vertex + step, vertices)
        k = first // part
        here = pl.ds(first, unit)
        return pltpu.make_async_remote_copy(
            src_ref=partial.at[span, rows_of(peer), here], dst_ref=parts.at[span, step - 1, :, here],
            send_sem=p_send.at[span, step - 1, k], recv_sem=p_recv.at[span, step - 1, k],
            device_id=(section, peer, feat), device_id_type=MESH,
        )

    def pass_copy(span, j):
        far = jnp.where(vertex == 0, last, 0)
        near = jnp.where(vertex == 0, 1, last - 1)
        return pltpu.make_async_remote_copy(
            src_ref=partial.at[span, rows_of(far), lanes(j)], dst_ref=passing.at[span, :, lanes(j)],
            send_sem=h_send.at[span, j], recv_sem=h_recv.at[span, j],
            device_id=(section, near, feat), device_id_type=MESH,
        )

    def detour_copy(span, j):
        return pltpu.make_async_remote_copy(
            src_ref=partial.at[span, rows_of(opposite), lanes(j)], dst_ref=transit.at[span, :, lanes(j)],
            send_sem=d_send.at[span, j], recv_sem=d_recv.at[span, j],
            device_id=(beside, vertex, feat), device_id_type=MESH,
        )

    def return_copy(span, j):
        return pltpu.make_async_remote_copy(
            src_ref=transit.at[span, :, lanes(j)], dst_ref=parts.at[span, last - 2, :, lanes(j)],
            send_sem=t_send.at[span, j], recv_sem=p_recv.at[span, last - 2, j],
            device_id=(beside, opposite, feat), device_id_type=MESH,
        )

    def support_copy(span, j):
        return pltpu.make_async_remote_copy(
            src_ref=support.at[span, :, lanes(j)], dst_ref=other.at[span, :, lanes(j)],
            send_sem=s_send.at[span, j], recv_sem=s_recv.at[span, j],
            device_id=(section, vertex, partner), device_id_type=MESH,
        )

    def ends_meet(here, there):
        return ((here == 0) & (there == last)) | ((here == last) & (there == 0))

    def is_sent(step):
        far = ends_meet(vertex, lax.rem(vertex + step, vertices))
        return jnp.logical_not(far | at_end) if step == last - 1 else jnp.logical_not(far)

    def is_received(step):
        return jnp.logical_not(ends_meet(lax.rem(vertex + vertices - step, vertices), vertex))

    def choose():
        def one_hot(i, _):
            for span in range(spans):
                hot = chosen(ids_ref[span : span + 1, :], side, i * side)
                select_ref[i, :, span_of(span)] = hot.astype(jnp.bfloat16)
            return 0

        lax.fori_loop(0, col_blocks, one_hot, 0)

    def count(span):
        taken_ref[span] = jnp.dot(
            select_ref[...].reshape(col_blocks * side, rows_all)[:, span_of(span)],
            jnp.ones((span_rows, side), jnp.bfloat16),
            preferred_element_type=jnp.float32,
        ).astype(jnp.bfloat16).reshape(col_blocks, side, side)

    def mark(span, leading):
        def clear(i, _):
            taken = taken_ref[span, i]
            rest = 1.0 - taken
            for first in range(0, width, side):
                group = slice(first, first + side)
                row = kept_ref[i, :, group] * rest
                kept_ref[i, :, group] = row + features_ref[i, :, group] * taken if leading else row
            return 0

        if span:
            lax.fori_loop(0, col_blocks, clear, 0)
        else:
            for q in range(quarters):
                for copy in load_table(q):
                    copy.wait()
                lax.fori_loop(q * quarter, (q + 1) * quarter, clear, 0)

    def lay_left(span):
        load_tiles(span).wait()
        lives = jnp.full((side, side), counts_ref[0, span], jnp.int32)

        def place(t, _):
            here = pl.ds(pl.multiple_of(t * side, side), side)
            tile = tiles[span, t].astype(jnp.float32)
            rows = jnp.where(lives > t, jnp.full(tile.shape, rows_ref[span, t], jnp.int32), row_blocks)
            for block in range(row_blocks):
                left[block * side : (block + 1) * side, here] = jnp.where(rows == block, tile, 0.0).astype(left.dtype)
            return 0

        lax.fori_loop(0, slots, place, 0)

    def lay_right(span, leading):
        def place(t, _):
            col = cols_ref[span, t]
            here = pl.ds(pl.multiple_of(t * side, side), side)
            right[here, :] = kept_ref[col]
            if not leading:
                right_select[here, :] = select_ref[col]
            return 0

        lax.fori_loop(0, slots, place, 0)

    def prepare_span(span, leading):
        if span:
            lay_left(span)
        mark(span, leading)
        lay_right(span, leading)

    def gather():
        initial_ref[...] = lax.dot_general(
            select_ref[...].reshape(col_blocks * side, rows_all),
            features_ref[...].reshape(col_blocks * side, width),
            (((0,), (0,)), ((), ())),
            preferred_element_type=jnp.float32,
        ).astype(jnp.bfloat16)

    def groups():
        return [slice(first, first + wide) for first in range(0, width, wide)]

    def product(group):
        return jnp.dot(left[...], right[:, group], preferred_element_type=jnp.float32)

    def first_sums(span, j):
        if j * part % wide == 0:
            group = slice(j * part, j * part + wide)
            partial[span, :, group] = product(group).astype(jnp.bfloat16)

    def later_sums(span, j):
        row_copy(span, j).wait_recv()
        partial[span, :, columns(j)] = (
            base_ref[span, :, columns(j)]
            + jnp.dot(
                picks_ref[span, :, span_of(span)], fresh_ref[span_of(span), columns(j)],
                preferred_element_type=jnp.float32,
            )
        ).astype(jnp.bfloat16)

    def scatter(span, sums):
        for j in range(pieces):
            sums(span, j)

            @pl.when(at_end)
            def _(j=j):
                pass_copy(span, j).start()
                detour_copy(span, j).start()

            if (j + 1) * part % unit == 0:
                @pl.when(jnp.logical_not(at_end))
                def _(j=j):
                    for step in (1, last):
                        direct_copy(span, step, (j + 1) * part - unit).start()

        for first in range(0, width, unit):
            for step in (1, last):
                @pl.when(at_end & is_sent(step))
                def _(step=step, first=first):
                    direct_copy(span, step, first).start()

    def pass_on(span):
        for who, step in ((1, last - 1), (last - 1, 2)):
            @pl.when(vertex == who)
            def _(who=who, step=step):
                far = last if who == 1 else 0
                here = pl.ds(far * span_rows, span_rows)
                for j in range(pieces):
                    pass_copy(span, j).wait_recv()
                    partial[span, here, columns(j)] = (
                        partial[span, here, columns(j)].astype(jnp.float32)
                        + passing[span, :, columns(j)].astype(jnp.float32)
                    ).astype(jnp.bfloat16)
                    part_copy(span, step, j).start()

    def hand_on(span):
        @pl.when(at_end)
        def _():
            for j in range(pieces):
                detour_copy(span, j).wait_recv()
                return_copy(span, j).start()

    def keep(span):
        used = (span + 1) * span_rows
        for group in groups():
            base_ref[span, :, group] = product(group)
        picks_ref[span, :, :used] = jnp.dot(
            left[...], right_select[:, :used], preferred_element_type=jnp.float32
        ).astype(jnp.bfloat16)

    def earlier(span):
        used = span * span_rows
        for group in groups():
            base_ref[span, :, group] += jnp.dot(
                picks_ref[span, :, :used], fresh_ref[:used, group], preferred_element_type=jnp.float32
            )

    def weight_rows(which):
        return pl.ds(pl.multiple_of(which * width, width), width)

    def finish(span):
        halves = groups()
        whole = [0.0] * len(halves)
        for half in halves:
            here = range(half.start // part, half.stop // part)
            for j in here:
                for step in range(1, vertices):
                    if step in (1, last):
                        if j * part % unit == 0:
                            @pl.when(is_received(step))
                            def _(step=step, j=j):
                                direct_copy(span, step, j * part).wait_recv()
                    else:
                        @pl.when(is_received(step))
                        def _(step=step, j=j):
                            part_copy(span, step, j).wait_recv()

                total = partial[span, rows_of(vertex), columns(j)].astype(jnp.float32)
                for step in range(1, vertices):
                    total += parts[span, step - 1, :, columns(j)].astype(jnp.float32)
                support[span, :, columns(j)] = (
                    (1.0 - RESIDUAL_SHARE) * total
                    + RESIDUAL_SHARE * initial_ref[span_of(span), columns(j)].astype(jnp.float32)
                ).astype(jnp.bfloat16)
                support_copy(span, j).start()

        def project(source, which, half, group):
            rows = pl.ds(pl.multiple_of(which * width + half.start, wide), wide)
            return jnp.dot(source[span, :, half], weight_ref[rows, group], preferred_element_type=jnp.float32)

        for k, group in enumerate(halves):
            for half in halves:
                whole[k] += project(support, feat, half, group)
        for half in halves:
            for j in range(half.start // part, half.stop // part):
                support_copy(span, j).wait_recv()
            if half is not halves[-1]:
                for k, group in enumerate(halves):
                    whole[k] += project(other, partner, half, group)
        for k, group in enumerate(halves):
            rows = jnp.maximum(
                (1.0 - beta) * support[span, :, group].astype(jnp.float32)
                + beta * (whole[k] + project(other, partner, halves[-1], group)),
                0.0,
            ).astype(jnp.bfloat16)
            result[span, :, group] = rows

            @pl.when(section < sections - 1)
            def _(group=group):
                for j in range(group.start // part, group.stop // part):
                    row_copy(span, j).start()

            out_ref[span, :, group] = rows

    choose()
    count(0)
    lay_left(0)
    for span in range(1, spans):
        count(span)

    @pl.when(section == 0)
    def _():
        for span in range(spans):
            prepare_span(span, True)
            if span == 0:
                meet()
            if span == 2:
                pass_on(0)
            scatter(span, first_sums)
        gather()
        load_weight.wait()
        if spans < 3:
            pass_on(0)
        for span in range(spans - 1):
            finish(span)
            pass_on(span + 1)

    @pl.when(section > 0)
    def _():
        for span in range(spans):
            prepare_span(span, False)
            keep(span)
            if span == 0:
                meet()

                @pl.when(section == sections // 2)
                def _():
                    for ahead in range(spans):
                        hand_on(ahead)

        gather()
        load_weight.wait()

        @pl.when(section > sections // 2)
        def _():
            for span in range(spans):
                hand_on(span)

        for span in range(spans):
            scatter(span, later_sums)
            if span:
                finish(span - 1)
            pass_on(span)
            if span + 1 < spans:
                earlier(span + 1)

    def merge():
        blocks = max(1, 512 // side)
        for first in range(0, col_blocks, blocks):
            picked = select_ref[first : first + blocks].reshape(blocks * side, rows_all)
            for group in groups():
                moved = jnp.dot(picked, fresh_ref[:, group], preferred_element_type=jnp.float32).astype(jnp.bfloat16)
                kept_ref[first : first + blocks, :, group] += moved.reshape(blocks, side, wide)

    @pl.when(section > 0)
    def _():
        merge()

    finish(spans - 1)

    @pl.when(section < sections // 2)
    def _():
        for span in range(spans):
            hand_on(span)

    for span in range(spans):
        for j in range(pieces):
            support_copy(span, j).wait_send()
            for step in range(1, vertices):
                if step in (1, last):
                    if j * part % unit == 0:
                        @pl.when(is_sent(step))
                        def _(span=span, step=step, j=j):
                            direct_copy(span, step, j * part).wait_send()
                else:
                    @pl.when(is_sent(step))
                    def _(span=span, step=step, j=j):
                        part_copy(span, step, j).wait_send()

            @pl.when(at_end)
            def _(span=span, j=j):
                pass_copy(span, j).wait_send()
                detour_copy(span, j).wait_send()
                return_copy(span, j).wait_send()

            @pl.when(section < sections - 1)
            def _(span=span, j=j):
                row_copy(span, j).wait_send()


def deliver(rows_hbm, table_hbm, rows_out, table_out, rows_ref, table_ref, in_sem, out_sem):
    chunks = in_sem.shape[0] - 1
    size = table_ref.shape[0] // chunks
    moves = []
    for i in range(chunks):
        here = pl.ds(i * size, size)
        moves.append((
            pltpu.make_async_copy(table_hbm.at[here], table_ref.at[here], in_sem.at[i]),
            pltpu.make_async_copy(table_ref.at[here], table_out.at[here], out_sem.at[i]),
        ))
    moves.append((
        pltpu.make_async_copy(rows_hbm, rows_ref, in_sem.at[chunks]),
        pltpu.make_async_copy(rows_ref, rows_out, out_sem.at[chunks]),
    ))
    for get, _ in moves:
        get.start()
    for get, put in moves:
        get.wait()
        put.start()
    for _, put in moves:
        put.wait()


def long_line(sizes, features, history, weights, tile_values, tile_rows, tile_cols, tile_counts, span_ids):
    sections, vertices, feats = sizes
    spans, span_rows = span_ids.shape
    owned, width = features.shape
    rows_whole = span_rows * vertices
    rows_all = spans * span_rows
    vmem = pl.BlockSpec(memory_space=pltpu.VMEM)
    smem = pl.BlockSpec(memory_space=pltpu.SMEM)
    anywhere = pl.BlockSpec(memory_space=pl.ANY)

    dense = pl.pallas_call(
        prepare,
        name="prepare",
        out_shape=jax.ShapeDtypeStruct((spans, rows_whole, owned), jnp.bfloat16),
        in_specs=[smem, smem, smem, vmem],
        out_specs=anywhere,
        scratch_shapes=[
            pltpu.VMEM((spans, rows_whole, owned), jnp.bfloat16),
            pltpu.SemaphoreType.DMA((spans,)),
        ],
        compiler_params=pltpu.CompilerParams(vmem_limit_bytes=VMEM_BYTES),
    )(tile_rows, tile_cols, tile_counts.reshape(1, spans), tile_values)

    rows_type = jax.ShapeDtypeStruct((spans, span_rows, width), jnp.bfloat16)
    table_type = jax.ShapeDtypeStruct((owned, width), jnp.bfloat16)
    block = pltpu.VMEM(rows_type.shape, jnp.bfloat16)
    halves = 2
    pair = pltpu.SemaphoreType.DMA((spans, halves))
    layer_rows, table_new = pl.pallas_call(
        functools.partial(relay, sections, vertices, feats),
        name="relay",
        out_shape=(rows_type, table_type),
        in_specs=[anywhere, vmem, anywhere, anywhere, anywhere],
        out_specs=(vmem, anywhere),
        scratch_shapes=[
            pltpu.VMEM((min(2, spans), rows_whole, owned), jnp.bfloat16),
            pltpu.VMEM((spans, rows_whole, width), jnp.float32),
            pltpu.VMEM((spans, rows_whole, rows_all), jnp.bfloat16),
            pltpu.VMEM(weights.shape[1:], weights.dtype),
            pltpu.VMEM((owned, width), jnp.bfloat16),
            pltpu.VMEM((owned, width), jnp.bfloat16),
            pltpu.VMEM((owned, rows_all), jnp.bfloat16),
            pltpu.VMEM((rows_all, width), jnp.bfloat16),
            pltpu.VMEM((rows_all, width), jnp.bfloat16),
            block,
            pltpu.VMEM((spans, rows_whole, width), jnp.bfloat16),
            pltpu.VMEM((spans, vertices - 1, span_rows, width), jnp.bfloat16),
            block, block, block, block,
            pltpu.SemaphoreType.DMA((spans + 3,)),
            pltpu.SemaphoreType.DMA,
            pair, pair,
            pltpu.SemaphoreType.DMA((spans, vertices - 1, halves)),
            pltpu.SemaphoreType.DMA((spans, vertices - 1, halves)),
            pair, pair, pair, pair,
        ],
        compiler_params=pltpu.CompilerParams(
            vmem_limit_bytes=VMEM_BYTES, collective_id=0, has_side_effects=True
        ),
    )(dense, span_ids, weights[0], history[0], features)

    table_type = jax.ShapeDtypeStruct((owned, width), jnp.bfloat16)
    chunks = 8
    return pl.pallas_call(
        deliver,
        name="deliver",
        out_shape=(rows_type, table_type),
        in_specs=[anywhere, anywhere],
        out_specs=(anywhere, anywhere),
        scratch_shapes=[
            pltpu.VMEM(rows_type.shape, jnp.bfloat16),
            pltpu.VMEM(table_type.shape, jnp.bfloat16),
            pltpu.SemaphoreType.DMA((chunks + 1,)),
            pltpu.SemaphoreType.DMA((chunks + 1,)),
        ],
        compiler_params=pltpu.CompilerParams(vmem_limit_bytes=VMEM_BYTES),
    )(layer_rows, table_new)


def short_line(sizes, features, history, weights, tile_values, tile_rows, tile_cols, tile_counts, span_ids):
    sections, vertices, feats = sizes
    spans, span_rows = span_ids.shape
    slots, side = tile_values.shape[1:3]
    owned, width = features.shape
    rows_whole = span_rows * vertices
    rows_all = spans * span_rows
    pieces = 4
    vmem = pl.BlockSpec(memory_space=pltpu.VMEM)
    smem = pl.BlockSpec(memory_space=pltpu.SMEM)
    anywhere = pl.BlockSpec(memory_space=pl.ANY)
    block = pltpu.VMEM((spans, span_rows, width), jnp.bfloat16)
    pair = pltpu.SemaphoreType.DMA((spans, pieces))
    triple = pltpu.SemaphoreType.DMA((spans, vertices - 1, pieces))
    table = history[0].reshape(owned // side, side, width)
    layer_rows, table_new = pl.pallas_call(
        functools.partial(stream, sections, vertices, feats),
        name="stream",
        out_shape=(
            pltpu.VMEM((spans, span_rows, width), jnp.bfloat16),
            pltpu.VMEM(table.shape, jnp.bfloat16),
        ),
        in_specs=[smem, smem, smem, vmem, anywhere, anywhere, anywhere, anywhere],
        out_specs=(vmem, vmem),
        scratch_shapes=[
            pltpu.VMEM(tile_values.shape, jnp.bfloat16),
            pltpu.VMEM((rows_whole, slots * side), jnp.bfloat16),
            pltpu.VMEM((slots * side, width), jnp.bfloat16),
            pltpu.VMEM((slots * side, rows_all), jnp.bfloat16),
            pltpu.VMEM((spans, rows_whole, width), jnp.float32),
            pltpu.VMEM((spans, rows_whole, rows_all), jnp.bfloat16),
            pltpu.VMEM(weights.shape[1:], weights.dtype),
            pltpu.VMEM(table.shape, jnp.bfloat16),
            pltpu.VMEM((owned // side, side, rows_all), jnp.bfloat16),
            pltpu.VMEM((spans, owned // side, side, side), jnp.bfloat16),
            pltpu.VMEM((rows_all, width), jnp.bfloat16),
            pltpu.VMEM((rows_all, width), jnp.bfloat16),
            pltpu.VMEM((spans, rows_whole, width), jnp.bfloat16),
            pltpu.VMEM((spans, vertices - 1, span_rows, width), jnp.bfloat16),
            block, block, block, block, block,
            pltpu.SemaphoreType.DMA((spans + 9,)),
            pair, pair, triple, triple, pair, pair, pair, pair, pair, pair, pair,
        ],
        compiler_params=pltpu.CompilerParams(
            vmem_limit_bytes=VMEM_BYTES, collective_id=0, has_side_effects=True
        ),
    )(tile_rows, tile_cols, tile_counts.reshape(1, spans), span_ids, tile_values, weights[0], table,
      features.reshape(table.shape))
    chunks = 4
    layer_rows, table_new = pl.pallas_call(
        write,
        name="write",
        out_shape=(
            jax.ShapeDtypeStruct((spans, span_rows, width), jnp.bfloat16),
            jax.ShapeDtypeStruct(table.shape, jnp.bfloat16),
        ),
        in_specs=[vmem, vmem],
        out_specs=(anywhere, anywhere),
        scratch_shapes=[pltpu.SemaphoreType.DMA((chunks + 1,))],
        compiler_params=pltpu.CompilerParams(vmem_limit_bytes=VMEM_BYTES),
    )(
        pltpu.with_memory_space_constraint(layer_rows, pltpu.VMEM),
        pltpu.with_memory_space_constraint(table_new, pltpu.VMEM),
    )
    return layer_rows, table_new.reshape(owned, width)


def shards(sizes, *arrays):
    layers = short_line if sizes[0] == sizes[1] == LINE else long_line
    layer_rows, table_new = layers(sizes, *arrays)
    return (layer_rows[None], table_new[None])


def solution(mesh):
    placed = (
        P("vertex", "feat"),
        P("section", "vertex", "feat"),
        P("section", None, "feat"),
        P(None, "vertex", None, None),
        P(None, "vertex"),
        P(None, "vertex"),
        P(None, "vertex"),
        P(None, "vertex"),
    )
    sizes = (mesh.shape["section"], mesh.shape["vertex"], mesh.shape["feat"])
    return jax.shard_map(
        functools.partial(shards, sizes),
        mesh=mesh,
        in_specs=placed,
        out_specs=(P("section", None, "vertex", "feat"), P("section", "vertex", "feat")),
        check_vma=False,
    )
```
